256 devices in a mesh: section: 4 (over y), tile: 64 (over x, z, core).
Axes of the slice: x: 4, y: 4, z: 8, core: 2. Of those that a mesh axis runs over, the one named last changes fastest.
Arguments:
- cams: bfloat16 [4, 32768, 768], P(None, 'tile'), may hold values from -6 to 6
- vit_up: bfloat16 [4, 768, 1536], P('section'), may hold values from -0.21875 to 0.21875
- vit_down: bfloat16 [4, 1536, 768], P('section'), may hold values from -0.15625 to 0.15625
- proj: bfloat16 [768, 256], replicated, may hold values from -0.21875 to 0.21875
- frustum_tiles: bfloat16 [64, 64, 128, 128], P('tile'), may hold values from -0.15625 to 0.15625
- src_block: int32 [64, 64], P('tile'), may hold values from 0 to 3
- dst_block: int32 [64, 64], P('tile'), may hold values from 0 to 4
- live: int32 [64, 64], P('tile'), may hold values 0 or 1
- render_up: bfloat16 [256, 512], replicated, may hold values from -0.375 to 0.375
- render_down: bfloat16 [512, 256], replicated, may hold values from -0.25 to 0.25
- decode_up: bfloat16 [256, 512], replicated, may hold values from -0.375 to 0.375
- decode_down: bfloat16 [512, 256], replicated, may hold values from -0.25 to 0.25
- pred_grad: bfloat16 [4, 40960, 256], P('section', 'tile'), may hold values from -6 to 6
Outputs:
- prediction: bfloat16 [4, 40960, 256], P('section', 'tile')
- grad_proj: float32 [768, 256], replicated
- grad_render_up: float32 [256, 512], replicated
- grad_render_down: float32 [512, 256], replicated
- grad_decode_up: float32 [256, 512], replicated
- grad_decode_down: float32 [512, 256], replicated
The draws below stay inside these ranges and needn't reach their ends.
All inputs are finite; a program needn't handle non-finite values. No bound on the sum of `live` on one device may be relied on, other than what follows from the above.
Results may differ from the reference program's by a relative error of at most 0.025.
Values may be sent and summed in bfloat16 or wider, within the bound.
A program may use at most 128 MiB of HBM per device.

```python
import math
import jax
import jax.numpy as jnp
from jax import lax

D = 768
FFV = 1536
C = 256
FFB = 512
BLK = 128
CAM_BLK = 4
BEV_BLK = 5
LAYERS = 4
MICRO = 4
TOKENS = 32768
CELLS = 40960
N_TILE = 64


def place_ends(entries, key, least, largest):
    spot = [jax.random.randint(jax.random.fold_in(key, axis), (), 0, length) for axis, length in enumerate(entries.shape)]
    widest = entries.shape.index(max(entries.shape))
    next_to = spot[:widest] + [(spot[widest] + 1) % entries.shape[widest]] + spot[widest + 1:]
    return entries.at[tuple(spot)].set(least).at[tuple(next_to)].set(largest)


def shard_levels(stream_key, extent, shards, least, high):
    level = 1.0
    for position, parts in shards:
        steps = jax.random.uniform(jax.random.fold_in(jax.random.fold_in(stream_key, 6), position), (parts,), jnp.float32, least / len(shards), high / len(shards))
        level = level * jnp.repeat(jnp.exp(steps), extent[position] // parts).reshape((-1,) + (1,) * (len(extent) - 1 - position))
    return level


def scatter_about(stream_key, dims, scale, most, shards=(), held_as=jnp.bfloat16):
    values = scale * jax.random.normal(stream_key, dims, jnp.float32)
    if shards:
        values = values * shard_levels(stream_key, dims, shards, -0.22, 0.18)
    return jnp.clip(values, -most, most).astype(held_as)


def setup_inputs(seed: int = 0) -> dict:
    key_of = jax.random.split(jax.random.key(seed), 14)
    cams = scatter_about(key_of[0], (MICRO, TOKENS, D), 1.0, 6.0, ((1, 64),))
    vit_up = scatter_about(key_of[1], (LAYERS, D, FFV), D ** -0.5, 0.21875, ((0, 4),))
    vit_down = scatter_about(key_of[2], (LAYERS, FFV, D), FFV ** -0.5, 0.15625, ((0, 4),))
    proj = scatter_about(key_of[3], (D, C), D ** -0.5, 0.21875)
    frustum_tiles = scatter_about(key_of[4], (N_TILE, N_TILE, BLK, BLK), (BLK * N_TILE // BEV_BLK) ** -0.5, 0.15625, ((0, 64),))
    src_block = place_ends(jax.random.randint(key_of[5], (N_TILE, N_TILE), 0, CAM_BLK), jax.random.fold_in(key_of[5], 1), 0, CAM_BLK - 1).astype(jnp.int32)
    dst_block = place_ends(jax.random.randint(key_of[6], (N_TILE, N_TILE), 0, BEV_BLK), jax.random.fold_in(key_of[6], 1), 0, BEV_BLK - 1).astype(jnp.int32)
    live = place_ends((jax.random.randint(key_of[7], (N_TILE, N_TILE), 0, 4) < 3).astype(jnp.int32), jax.random.fold_in(key_of[7], 1), 0, 1)
    render_up = scatter_about(key_of[8], (C, FFB), C ** -0.5, 0.375)
    render_down = scatter_about(key_of[9], (FFB, C), FFB ** -0.5, 0.25)
    decode_up = scatter_about(key_of[10], (C, FFB), C ** -0.5, 0.375)
    decode_down = scatter_about(key_of[11], (FFB, C), FFB ** -0.5, 0.25)
    pred_grad = scatter_about(key_of[12], (MICRO, CELLS, C), 1.0, 6.0, ((0, 4), (1, 64)))
    return {"cams": cams, "vit_up": vit_up, "vit_down": vit_down, "proj": proj, "frustum_tiles": frustum_tiles, "src_block": src_block, "dst_block": dst_block, "live": live, "render_up": render_up, "render_down": render_down, "decode_up": decode_up, "decode_down": decode_down, "pred_grad": pred_grad}


eps = 1e-05

def encoder_layer(state, w_up, w_down):
    widened = state.astype(jnp.float32)
    scaling = lax.rsqrt(lax.optimization_barrier(jnp.mean(widened * widened, axis=-1, keepdims=True)) + eps)
    normed = (widened * scaling).astype(jnp.bfloat16)
    hidden = jax.nn.gelu(jnp.dot(normed, w_up, preferred_element_type=jnp.float32)).astype(jnp.bfloat16)
    return (widened + jnp.dot(hidden, w_down, preferred_element_type=jnp.float32)).astype(jnp.bfloat16)

def contract_rows(left, right):
    return lax.dot_general(left, right, (((0,), (0,)), ((), ())), preferred_element_type=jnp.float32)

def against_rows(left, right):
    return lax.dot_general(left, right, (((1,), (1,)), ((), ())), preferred_element_type=jnp.float32)

def heads_forward(bev_grid, weights):
    state = bev_grid
    stored = []
    for w_up, w_down in weights:
        scaling = lax.rsqrt(lax.optimization_barrier(jnp.mean(state * state, axis=-1, keepdims=True)) + eps)
        normed = (state * scaling).astype(jnp.bfloat16)
        preact = jnp.dot(normed, w_up, preferred_element_type=jnp.float32)
        hidden = jax.nn.gelu(preact).astype(jnp.bfloat16)
        stored.append((state, scaling, normed, preact, hidden))
        state = state + jnp.dot(hidden, w_down, preferred_element_type=jnp.float32)
    return (state.astype(jnp.bfloat16), stored)

def heads_backward(cotangent, stored, weights):
    grad_state = cotangent
    gradients = []
    for saved_block, pair in zip(stored[::-1], weights[::-1]):
        state, scaling, normed, preact, hidden = saved_block
        w_up, w_down = pair
        rounded = grad_state.astype(jnp.bfloat16)
        grad_down = contract_rows(hidden, rounded)
        grad_hidden = against_rows(rounded, w_down)
        gelu_slope = jax.jvp(jax.nn.gelu, (preact,), (jnp.ones_like(preact),))[1]
        grad_pre = (grad_hidden * gelu_slope).astype(jnp.bfloat16)
        grad_up = contract_rows(normed, grad_pre)
        grad_normed = against_rows(grad_pre, w_up)
        unit_rows = state * scaling
        grad_state = grad_state + scaling * (grad_normed - unit_rows * lax.optimization_barrier(jnp.mean(grad_normed * unit_rows, axis=-1, keepdims=True)))
        gradients = [grad_up, grad_down] + gradients
    return (grad_state, gradients)

def reference(cams, vit_up, vit_down, proj, frustum_tiles, src_block, dst_block, live, render_up, render_down, decode_up, decode_down, pred_grad):
    weights = ((render_up, render_down), (decode_up, decode_down))
    scale_factor = 1.0 / math.sqrt(MICRO * CELLS)
    cam_range = jnp.arange(CAM_BLK, dtype=jnp.int32)
    bev_range = jnp.arange(BEV_BLK, dtype=jnp.int32)
    slot_range = jnp.arange(N_TILE, dtype=jnp.int32)
    alive_flags = live.astype(jnp.float32)

    def one_batch(inputs):
        tokens, grad_out = inputs
        encoded = tokens
        for layer_number in range(LAYERS):
            encoded = encoder_layer(encoded, vit_up[layer_number], vit_down[layer_number])
        projected = jnp.dot(encoded, proj, preferred_element_type=jnp.float32).astype(jnp.bfloat16)
        blocks = projected.reshape(N_TILE, CAM_BLK, BLK, C)

        def join_sender(running, sender):
            own_blocks, slot_tiles, sources, targets, alive_row = sender
            chosen = jnp.take(own_blocks, sources, axis=0).astype(jnp.float32)
            pieces = (jnp.einsum('pij,pjc->pic', slot_tiles.astype(jnp.float32), chosen) * alive_row[:, None, None]).astype(jnp.bfloat16)
            target_pick = (targets[:, None] == bev_range[None, :]).astype(jnp.float32)
            return (running + target_pick[:, :, None, None] * pieces.astype(jnp.float32)[:, None], None)
        initial = jnp.zeros((N_TILE, BEV_BLK, BLK, C), jnp.float32)
        bev_blocks, unused = lax.scan(join_sender, initial, (blocks, frustum_tiles, src_block, dst_block, alive_flags))
        prediction, stored = heads_forward(bev_blocks.reshape(CELLS, C), weights)
        cotangent = grad_out.astype(jnp.float32) * scale_factor
        grad_grid, gradients = heads_backward(cotangent, stored, weights)
        grad_blocks = grad_grid.reshape(N_TILE, BEV_BLK, BLK, C)

        def split_sender(carried, sender):
            slot_tiles, sources, targets, alive_row = sender
            grad_pieces = grad_blocks[slot_range, targets].astype(jnp.bfloat16)
            grad_pieces = lax.optimization_barrier(grad_pieces).astype(jnp.float32)
            grad_chosen = jnp.einsum('pij,pic->pjc', slot_tiles.astype(jnp.float32), grad_pieces) * alive_row[:, None, None]
            source_pick = (sources[:, None] == cam_range[None, :]).astype(jnp.float32)
            return (carried, jnp.einsum('pk,pjc->kjc', source_pick, grad_chosen, precision=lax.Precision.HIGHEST))
        unused_carry, grad_rows = lax.scan(split_sender, jnp.zeros((), jnp.float32), (frustum_tiles, src_block, dst_block, alive_flags))
        grad_rows = grad_rows.reshape(TOKENS, C).astype(jnp.bfloat16)
        grad_proj = contract_rows(encoded, grad_rows)
        return (prediction, grad_proj, gradients[0], gradients[1], gradients[2], gradients[3])
    results = lax.map(one_batch, (cams, pred_grad))
    return (results[0], lax.optimization_barrier(jnp.sum(results[1], axis=0)), lax.optimization_barrier(jnp.sum(results[2], axis=0)), lax.optimization_barrier(jnp.sum(results[3], axis=0)), lax.optimization_barrier(jnp.sum(results[4], axis=0)), lax.optimization_barrier(jnp.sum(results[5], axis=0)))
```

```python
import functools
import math

import jax
import jax.numpy as jnp
from jax import lax
from jax.experimental import pallas as pl
from jax.experimental.pallas import tpu as pltpu
from jax.sharding import PartitionSpec as P

eps = 1e-05
MESH = pl.DeviceIdType.MESH
BF = jnp.bfloat16
F32 = jnp.float32
NY, NX, NZ, NC = 4, 4, 8, 2
BLK = 128
VMEM_LIMIT = 60 * 2**20
ANY = pl.BlockSpec(memory_space=pl.ANY)
VM = pl.BlockSpec(memory_space=pltpu.VMEM)
SM = pl.BlockSpec(memory_space=pltpu.SMEM)
DMA = pltpu.SemaphoreType.DMA


def where_am_i():
    y = lax.axis_index("section")
    t = lax.axis_index("tile")
    return y, t // (NZ * NC), (t // NC) % NZ, t % NC


def at(y, x, z, c):
    return (y, (x * NZ + z) * NC + c)


def send(src, dst, ssem, rsem, device):
    copy = pltpu.make_async_remote_copy(
        src_ref=src, dst_ref=dst, send_sem=ssem, recv_sem=rsem, device_id=device, device_id_type=MESH
    )
    copy.start()


def sent(src, ssem, device):
    pltpu.make_async_remote_copy(
        src_ref=src, dst_ref=src, send_sem=ssem, recv_sem=ssem, device_id=device, device_id_type=MESH
    ).wait_send()


def arrived(dst, rsem, device):
    pltpu.make_async_remote_copy(
        src_ref=dst, dst_ref=dst, send_sem=rsem, recv_sem=rsem, device_id=device, device_id_type=MESH
    ).wait_recv()


def greet(devices):
    barrier = pltpu.get_barrier_semaphore()
    for device in devices:
        pl.semaphore_signal(barrier, inc=1, device_id=device, device_id_type=MESH)
    pl.semaphore_wait(barrier, len(devices))


def gelu(v):
    return 0.5 * v * (1.0 + jnp.tanh(math.sqrt(2.0 / math.pi) * (v + 0.044715 * v * v * v)))


def encoder_kernel(
    up, down, cams, proj, tiles, index,
    encoded, x_all, tiles_all, index_all,
    w_up, w_down, own, y_s, y_r, x_s, x_r, z_s, z_r, b_s, b_r, t_s, t_r, i_s, i_r, p_s, p_r, local,
):
    y, x, z, c = where_am_i()
    sibling = at(y, x, z, 1 - c)
    group = x * NC + c
    moved = NY - 1
    half = NZ // 2
    steps = half + 1
    n_group = NX * NC
    cols = w_up.shape[-1] // 2

    def layer_of(j):
        return j + jnp.where(j >= y, 1, 0)

    def up_slice(l, xx):
        return w_up.at[l, z, xx // 2, :, pl.ds(pl.multiple_of((xx % 2) * cols, 128), cols)]

    def zz(offset):
        return lax.rem(z + offset + 2 * NZ, NZ)

    def xx(offset):
        return lax.rem(x + offset + NX, NX)

    def gg(offset):
        g = lax.rem(group + offset + n_group, n_group)
        return g

    def g_dev(g):
        return at(y, g // NC, z, g % NC)

    loads = [
        pltpu.make_async_copy(up, w_up.at[y], local.at[0]),
        pltpu.make_async_copy(down, w_down.at[y], local.at[1]),
        pltpu.make_async_copy(cams.at[y], encoded, local.at[2]),
        pltpu.make_async_copy(tiles.at[x, :, c], tiles_all.at[group], local.at[3]),
        pltpu.make_async_copy(index, index_all.at[group], local.at[4]),
    ]
    for load in loads:
        load.start()
    greet(
        [at(lax.rem(y + o, NY), x, z, c) for o in range(1, NY)]
        + [g_dev(gg(o)) for o in range(1, n_group)]
        + [at(y, x, zz(1), c), at(y, x, zz(-1), c)]
    )
    for load in loads[:3]:
        load.wait()

    def share(l, core):
        return up_slice(l, x) if core == 0 else w_down.at[l, z, x]

    for core in range(NC):
        @pl.when(c == core)
        def _(core=core):
            for o in range(1, NY):
                send(share(y, core), share(y, core), y_s.at[o - 1], y_r.at[o - 1], at(lax.rem(y + o, NY), x, z, c))

    for o in range(1, n_group):
        send(index, index_all.at[group], i_s.at[o - 1], i_r.at[o - 1], g_dev(gg(o)))

    def sign(j, d):
        return (1 - 2 * (j % 2)) * (1 - 2 * d)

    @pl.when(c == 0)
    def _():
        @pl.loop(0, moved)
        def _(j):
            l = layer_of(j)
            o = lax.rem(y - l + NY, NY)
            arrived(share(l, 0), y_r.at[o - 1], sibling)
            for ox in range(1, NX):
                send(up_slice(l, x), up_slice(l, x), x_s.at[j, ox - 1], x_r.at[j, ox - 1], at(y, xx(ox), z, c))

    def z_hops(d):
        return half if d == 0 else half - 1

    @pl.when(c == 1)
    def _():
        @pl.loop(0, steps * moved)
        def _(n):
            k = n // moved + 1
            j = n % moved
            l = layer_of(j)
            o = lax.rem(y - l + NY, NY)

            @pl.when(k == 1)
            def _():
                arrived(share(l, 1), y_r.at[o - 1], sibling)

            for d in range(2):
                s = sign(j, d)
                block = w_down.at[l, zz(-s * (k - 1)), x]

                @pl.when(jnp.logical_and(k >= 2, k <= z_hops(d) + 1))
                def _():
                    arrived(block, z_r.at[j, d, k - 2], sibling)

                @pl.when(k <= z_hops(d))
                def _():
                    send(block, block, z_s.at[j, d, k - 1], z_r.at[j, d, k - 1], at(y, x, zz(s), c))

    def layer_rows(l, r, rows):
        wide = encoded[pl.ds(r, rows), :].astype(F32)
        scaling = lax.rsqrt(jnp.mean(wide * wide, axis=-1, keepdims=True) + eps)
        normed = (wide * scaling).astype(BF)
        total = wide
        parts = 2
        for q in range(parts):
            width = w_up.shape[-1] // parts
            w1 = w_up[l, :, :, :, q * width : (q + 1) * width].reshape(wide.shape[1], width)
            hidden = gelu(jnp.dot(normed, w1, preferred_element_type=F32)).astype(BF)
            nz = NZ // parts
            w2 = w_down[l, q * nz : (q + 1) * nz].reshape(width, wide.shape[1])
            total = total + jnp.dot(hidden, w2, preferred_element_type=F32)
        encoded[pl.ds(r, rows), :] = total.astype(BF)

    tokens = encoded.shape[0]
    rows = tokens // 2

    def wait_sibling(j):
        l = layer_of(j)

        @pl.when(c == 0)
        def _():
            for i, ox in enumerate((0, 1, NX - 1) + tuple(range(2, NX - 1)) if NX > 2 else (0, 1)):
                arrived(w_down.at[l, :, xx(-ox)], b_r.at[j, i], sibling)

        @pl.when(c == 1)
        def _():
            arrived(w_up.at[l, z], b_r.at[j, 0], sibling)
            for d in range(2):
                for k in range(2, z_hops(d) + 2):
                    arrived(w_up.at[l, zz(-sign(j, d) * (k - 1))], b_r.at[j, 1 + d * half + k - 2], sibling)

    x_order = (1, NX - 1) + tuple(range(2, NX - 1)) if NX > 2 else (1,)

    @pl.loop(0, steps * moved)
    def _(n):
        j = n // steps
        k = n % steps + 1
        l = layer_of(j)

        @pl.when(c == 0)
        def _():
            @pl.when(k == 1)
            def _():
                for ox in range(1, NX):
                    arrived(up_slice(l, xx(-ox)), x_r.at[j, ox - 1], sibling)

            for d in range(2):
                s = sign(j, d)
                block = w_up.at[l, zz(-s * (k - 1))]

                @pl.when(jnp.logical_and(k >= 2, k <= z_hops(d) + 1))
                def _():
                    arrived(block, z_r.at[j, d, k - 2], sibling)
                    send(block, block, b_s.at[j, 1 + d * half + k - 2], b_r.at[j, 1 + d * half + k - 2], sibling)

                @pl.when(k <= z_hops(d))
                def _():
                    send(block, block, z_s.at[j, d, k - 1], z_r.at[j, d, k - 1], at(y, x, zz(s), c))

            @pl.when(k == 1)
            def _():
                send(w_up.at[l, z], w_up.at[l, z], b_s.at[j, 0], b_r.at[j, 0], sibling)

        @pl.when(c == 1)
        def _():
            @pl.when(k == 1)
            def _():
                block = w_down.at[l, :, x]
                for ox in x_order:
                    send(block, block, x_s.at[j, ox - 1], x_r.at[j, ox - 1], at(y, xx(ox), z, c))
                send(block, block, b_s.at[j, 0], b_r.at[j, 0], sibling)

            for i, ox in enumerate(x_order):
                @pl.when(k == min(i + 2, steps))
                def _(i=i, ox=ox):
                    block = w_down.at[l, :, xx(-ox)]
                    arrived(block, x_r.at[j, ox - 1], sibling)
                    send(block, block, b_s.at[j, i + 1], b_r.at[j, i + 1], sibling)

        @pl.when(j >= 1)
        def _():
            @pl.when(k == 1)
            def _():
                wait_sibling(j - 1)

            @pl.when(jnp.logical_or(k == 2, k == steps))
            def _():
                layer_rows(j - 1, pl.multiple_of(jnp.where(k == 2, 0, rows), rows), rows)

    for o in range(1, n_group):
        g = gg(o)
        send(tiles.at[g // NC, :, g % NC], tiles_all.at[group], t_s.at[o - 1], t_r.at[o - 1], g_dev(g))
    wait_sibling(moved - 1)
    @pl.loop(0, 2 * 2)
    def _(n):
        layer_rows(NY - 2 + n // 2, pl.multiple_of((n % 2) * rows, rows), rows)

    own[...] = jnp.dot(encoded[...], proj[...], preferred_element_type=F32).astype(BF)
    keep = pltpu.make_async_copy(own, x_all.at[group], local.at[5])
    keep.start()
    for ox in range(1, NX):
        send(own, x_all.at[group], p_s.at[ox - 1], p_r.at[ox - 1], at(y, xx(ox), z, c))
    send(own, x_all.at[group], p_s.at[NX - 1], p_r.at[NX - 1], sibling)
    for ox in range(1, NX):
        block = x_all.at[xx(-ox) * NC + c]
        arrived(block, p_r.at[ox - 1], sibling)
        send(block, block, p_s.at[NX - 1 + ox], p_r.at[NX - 1 + ox], sibling)
    for ox in range(NX):
        arrived(x_all.at[xx(-ox) * NC + 1 - c], p_r.at[NX - 1 + ox], sibling)

    keep.wait()
    for load in loads[3:]:
        load.wait()
    for o in range(1, n_group):
        g = gg(-o)
        arrived(tiles_all.at[g], t_r.at[o - 1], sibling)
        arrived(index_all.at[g], i_r.at[o - 1], sibling)
        sent(tiles_all.at[group], t_s.at[o - 1], sibling)
        sent(index_all.at[group], i_s.at[o - 1], sibling)
    for i in range(2 * NX - 1):
        sent(own, p_s.at[i], sibling)
    for core in range(NC):
        @pl.when(c == core)
        def _(core=core):
            for o in range(1, NY):
                sent(share(y, core), y_s.at[o - 1], sibling)

    @pl.loop(0, moved)
    def _(j):
        @pl.when(c == 0)
        def _():
            for ox in range(1, NX):
                sent(up_slice(y, x), x_s.at[j, ox - 1], sibling)
            for d in range(2):
                for k in range(1, z_hops(d) + 1):
                    sent(w_up.at[y, z], z_s.at[j, d, k - 1], sibling)
            for i in range(NZ):
                sent(w_up.at[y, z], b_s.at[j, i], sibling)

        @pl.when(c == 1)
        def _():
            for ox in range(1, NX):
                sent(w_down.at[y, :, x], x_s.at[j, ox - 1], sibling)
            for d in range(2):
                for k in range(1, z_hops(d) + 1):
                    sent(w_down.at[y, z, x], z_s.at[j, d, k - 1], sibling)
            for i in range(NX):
                sent(w_down.at[y, :, x], b_s.at[j, i], sibling)


def encode(up, down, cams, proj, tiles, index):
    d, f = up.shape[1:]
    tokens = cams.shape[1]
    channels = proj.shape[1]
    up = up.reshape(NZ, NX // 2, 2 * d // (NZ * NX), f)
    down = down.reshape(NZ, NX, f // (NZ * NX), d)
    tiles = tiles.reshape(NX, NZ, NC, BLK, BLK)
    n = NX * NC
    half = NZ // 2
    moved = NY - 1
    return pl.pallas_call(
        encoder_kernel,
        out_shape=(
            jax.ShapeDtypeStruct((tokens, d), BF),
            jax.ShapeDtypeStruct((n, tokens, channels), BF),
            jax.ShapeDtypeStruct((n, NZ, BLK, BLK), BF),
            jax.ShapeDtypeStruct((n,) + index.shape, jnp.int32),
        ),
        in_specs=[ANY, ANY, ANY, VM, ANY, ANY],
        out_specs=(VM, ANY, ANY, ANY),
        scratch_shapes=[
            pltpu.VMEM((NY,) + up.shape, BF),
            pltpu.VMEM((NY,) + down.shape, BF),
            pltpu.VMEM((tokens, channels), BF),
            DMA((NY - 1,)), DMA((NY - 1,)),
            DMA((moved, NX - 1)), DMA((moved, NX - 1)),
            DMA((moved, 2, half)), DMA((moved, 2, half)),
            DMA((moved, NZ)), DMA((moved, NZ)),
            DMA((n - 1,)), DMA((n - 1,)),
            DMA((n - 1,)), DMA((n - 1,)),
            DMA((2 * NX - 1,)), DMA((2 * NX - 1,)),
            DMA((6,)),
        ],
        compiler_params=pltpu.CompilerParams(
            collective_id=0, has_side_effects=True, vmem_limit_bytes=VMEM_LIMIT
        ),
    )(up, down, cams, proj, tiles, index)


def join_kernel(index, x_all, tiles, grid_out, left, right, parts, s_buf, r_buf, s_sem, r_sem):
    y, x, z, c = where_am_i()
    half = NZ // 2
    n_group = NX * NC
    bev = grid_out.shape[0] // BLK
    chunk = grid_out.shape[0] // 2

    def zz(offset):
        return lax.rem(z + offset + 2 * NZ, NZ)

    beside = (at(y, x, zz(1), c), at(y, x, zz(-1), c))
    greet(beside)

    def hops(ch, d):
        return half if ch == d else half - 1

    def push(ch, d, k):
        send(s_buf.at[ch, d, k - 1], r_buf.at[ch, d, k - 1], s_sem.at[ch, d, k - 1], r_sem.at[ch, d, k - 1], beside[d])

    @pl.loop(0, NZ)
    def _(i):
        off = jnp.where(i == 0, half, jnp.where(i % 2 == 1, (NZ - 1 - i) // 2, -((NZ - i) // 2)))
        target = zz(off)
        p = (x * NZ + target) * NC + c
        for g in range(n_group):
            tile = tiles[g, target].astype(F32)
            dst = index[g, 1, p]
            alive = index[g, 2, p]
            for b in range(bev):
                weight = jnp.where(dst == b, alive, 0).astype(F32)
                left[b * BLK : (b + 1) * BLK, g * BLK : (g + 1) * BLK] = (tile * weight).astype(BF)
            right[g * BLK : (g + 1) * BLK, :] = x_all[g, index[g, 0, p]]
        parts[i] = jnp.dot(left[...], right[...], preferred_element_type=F32)

        @pl.when(i == 0)
        def _():
            for d in range(2):
                s_buf[d, d, 0] = parts[0, d * chunk : (d + 1) * chunk].astype(BF)
                push(d, d, 1)

        for d in range(2):
            @pl.when(i == 1 + d)
            def _(d=d):
                ch = 1 - d
                s_buf[ch, d, 0] = parts[1 + d, ch * chunk : (ch + 1) * chunk].astype(BF)
                push(ch, d, 1)

    for o in range(half - 1, 0, -1):
        for ch_is_d in (True, False):
            for d in range(2):
                ch = d if ch_is_d else 1 - d
                k = hops(ch, d) - o + 1
                if k == 1:
                    continue
                arrived(r_buf.at[ch, d, k - 2], r_sem.at[ch, d, k - 2], beside[d])
                i = NZ - 1 - 2 * o if d == 0 else NZ - 2 * o
                total = parts[i, ch * chunk : (ch + 1) * chunk] + r_buf[ch, d, k - 2].astype(F32)
                s_buf[ch, d, k - 1] = total.astype(BF)
                push(ch, d, k)
    for ch in range(2):
        total = parts[NZ - 1, ch * chunk : (ch + 1) * chunk]
        for d in range(2):
            k = hops(ch, d)
            arrived(r_buf.at[ch, d, k - 1], r_sem.at[ch, d, k - 1], beside[d])
            total = total + r_buf[ch, d, k - 1].astype(F32)
        grid_out[ch * chunk : (ch + 1) * chunk] = total
    for ch in range(2):
        for d in range(2):
            for k in range(hops(ch, d)):
                sent(s_buf.at[ch, d, k], s_sem.at[ch, d, k], beside[d])


def join(index_all, x_all, tiles_all, cells):
    channels = x_all.shape[-1]
    x_all = x_all.reshape(x_all.shape[0], -1, BLK, channels)
    n = NX * NC
    half = NZ // 2
    return pl.pallas_call(
        join_kernel,
        out_shape=jax.ShapeDtypeStruct((cells, channels), F32),
        in_specs=[SM, VM, VM],
        out_specs=VM,
        scratch_shapes=[
            pltpu.VMEM((cells, n * BLK), BF),
            pltpu.VMEM((n * BLK, channels), BF),
            pltpu.VMEM((NZ, cells, channels), F32),
            pltpu.VMEM((2, 2, half, cells // 2, channels), BF),
            pltpu.VMEM((2, 2, half, cells // 2, channels), BF),
            DMA((2, 2, half)), DMA((2, 2, half)),
        ],
        compiler_params=pltpu.CompilerParams(
            collective_id=1, has_side_effects=True, vmem_limit_bytes=VMEM_LIMIT
        ),
    )(index_all, x_all, tiles_all)


def split_kernel(
    index, grad, tiles, rows_out, all_grad, here, left, acc, core_s, core_r, x_send, x_recv, z_s, z_r, c_s, c_r, x_s, x_r, local
):
    y, x, z, c = where_am_i()
    half = NZ // 2
    n_group = NX * NC
    chunk = grad.shape[0] // 2
    cam = rows_out.shape[0] // BLK
    sibling = at(y, x, z, 1 - c)

    def zz(offset):
        return lax.rem(z + offset + 2 * NZ, NZ)

    def xx(offset):
        return lax.rem(x + offset + NX, NX)

    beside = (at(y, x, zz(1), c), at(y, x, zz(-1), c))
    greet(beside + (sibling,) + tuple(at(y, xx(o), z, c) for o in range(1, NX)))

    def hops(ch, d):
        return half if ch == d else half - 1

    def part(origin, ch):
        return all_grad.at[origin, pl.ds(ch * chunk, chunk)]

    keep = pltpu.make_async_copy(grad, all_grad.at[z], local)
    keep.start()
    keep.wait()
    for ch in range(2):
        for d in range(2):
            send(part(z, ch), part(z, ch), z_s.at[ch, d, 0], z_r.at[ch, d, 0], beside[d])

    def use(origin, first):
        p = (x * NZ + origin) * NC + c
        here[...] = all_grad[origin].reshape(here.shape)
        for g in range(n_group):
            tile = tiles[g, origin].astype(F32).T
            src = index[g, 0, p]
            alive = index[g, 2, p]
            for k in range(cam):
                weight = jnp.where(src == k, alive, 0).astype(F32)
                left[k * BLK : (k + 1) * BLK, :] = (tile * weight).astype(BF)
            product = jnp.dot(left[...], here[index[g, 1, p]], preferred_element_type=F32)
            if first:
                acc[g] = product
            else:
                acc[g] = acc[g] + product

    use(z, True)

    @pl.loop(1, half + 1)
    def _(k):
        for d in range(2):
            s = 1 - 2 * d
            origin = zz(-s * k)
            for ch in range(2):
                @pl.when(k <= hops(ch, d))
                def _(ch=ch, d=d):
                    arrived(part(origin, ch), z_r.at[ch, d, k - 1], beside[d])

                @pl.when(k + 1 <= hops(ch, d))
                def _(ch=ch, d=d):
                    send(part(origin, ch), part(origin, ch), z_s.at[ch, d, k], z_r.at[ch, d, k], beside[d])

        for d in range(2):
            s = 1 - 2 * d
            if d == 0:
                use(zz(-k), False)
            else:
                @pl.when(k < half)
                def _():
                    use(zz(k), False)

    for xi in range(NX):
        @pl.when(c == 0)
        def _(xi=xi):
            core_s[xi] = acc[xi * NC + 1].astype(BF)

        @pl.when(c == 1)
        def _(xi=xi):
            core_s[xi] = acc[xi * NC].astype(BF)
    send(core_s, core_r, c_s, c_r, sibling)
    arrived(core_r, c_r, sibling)
    for o in range(1, NX):
        g = xx(o) * NC + c
        x_send[o - 1] = (acc[g] + core_r[xx(o)].astype(F32)).astype(BF)
        send(x_send.at[o - 1], x_recv.at[o - 1], x_s.at[o - 1], x_r.at[o - 1], at(y, xx(o), z, c))
    total = acc[x * NC + c] + core_r[x].astype(F32)
    for o in range(1, NX):
        arrived(x_recv.at[o - 1], x_r.at[o - 1], sibling)
        total = total + x_recv[o - 1].astype(F32)
    rows_out[...] = total.astype(BF)
    sent(core_s, c_s, sibling)
    for o in range(1, NX):
        sent(x_send.at[o - 1], x_s.at[o - 1], sibling)
    for ch in range(2):
        for d in range(2):
            for k in range(hops(ch, d)):
                sent(part(z, ch), z_s.at[ch, d, k], beside[d])


def split(index_all, grad, tiles_all, tokens):
    cells, channels = grad.shape
    n = NX * NC
    half = NZ // 2
    return pl.pallas_call(
        split_kernel,
        out_shape=jax.ShapeDtypeStruct((tokens, channels), BF),
        in_specs=[SM, VM, VM],
        out_specs=VM,
        scratch_shapes=[
            pltpu.VMEM((NZ, cells, channels), BF),
            pltpu.VMEM((cells // BLK, BLK, channels), BF),
            pltpu.VMEM((tokens, BLK), BF),
            pltpu.VMEM((n, tokens, channels), F32),
            pltpu.VMEM((NX, tokens, channels), BF),
            pltpu.VMEM((NX, tokens, channels), BF),
            pltpu.VMEM((NX - 1, tokens, channels), BF),
            pltpu.VMEM((NX - 1, tokens, channels), BF),
            DMA((2, 2, half)), DMA((2, 2, half)),
            DMA(()), DMA(()),
            DMA((NX - 1,)), DMA((NX - 1,)),
            DMA(()),
        ],
        compiler_params=pltpu.CompilerParams(
            collective_id=2, has_side_effects=True, vmem_limit_bytes=VMEM_LIMIT
        ),
    )(index_all, grad, tiles_all)


def total_kernel(*refs):
    n = (len(refs) - 15) // 2
    ins, outs = refs[:n], refs[n : 2 * n]
    packed, from1, mid, from2, mine, gathered, result, s1, r1, s2, r2, s3, r3, s4, r4 = refs[2 * n :]
    y, x, z, c = where_am_i()
    n1, n2 = NX * NY, NZ * NC
    one, two = y * NX + x, z * NC + c
    real = packed.shape[1]
    share = mine.shape[0]
    width = packed.shape[2]

    def dev1(q):
        return at(q // NX, q % NX, z, c)

    def dev2(e):
        return at(y, x, e // NC, e % NC)

    def q1(o):
        return lax.rem(one + o + n1, n1)

    def q2(o):
        return lax.rem(two + o + n2, n2)

    greet([dev1(q1(o)) for o in range(1, n1)] + [dev2(q2(o)) for o in range(1, n2)])

    def pieces():
        row = 0
        for i, ref in enumerate(ins):
            height = ref.shape[0] // n1
            for col in range(ref.shape[1] // width):
                yield i, row, height, col
                row += height

    @pl.loop(0, n1)
    def _(o):
        q = lax.rem(one + 1 + o, n1)
        for i, row, height, col in pieces():
            packed[q, row : row + height, :] = ins[i][
                pl.ds(pl.multiple_of(q * height, height), height), col * width : (col + 1) * width
            ].astype(BF)

        @pl.when(o < n1 - 1)
        def _():
            send(packed.at[q], from1.at[o], s1.at[o], r1.at[o], dev1(q))

    mid[...] = jnp.zeros_like(mid)
    total = packed[one].astype(F32)
    for o in range(n1 - 1):
        arrived(from1.at[o], r1.at[o], dev1(one))
        total = total + from1[o].astype(F32)
    mid[0:real, :] = total.astype(BF)

    def part(ref, e):
        return ref.at[pl.ds(pl.multiple_of(e * share, share), share), :]

    for o in range(1, n2):
        e = q2(o)
        send(part(mid, e), from2.at[o - 1], s2.at[o - 1], r2.at[o - 1], dev2(e))
    total = mid[pl.ds(pl.multiple_of(two * share, share), share), :].astype(F32)
    for o in range(1, n2):
        arrived(from2.at[o - 1], r2.at[o - 1], dev2(two))
        total = total + from2[o - 1].astype(F32)
    mine[...] = total.astype(BF)
    for o in range(1, n2):
        send(mine, part(gathered, two), s3.at[o - 1], r3.at[o - 1], dev2(q2(o)))
    gathered[pl.ds(pl.multiple_of(two * share, share), share), :] = mine[...]
    for o in range(1, n2):
        arrived(part(gathered, q2(-o)), r3.at[o - 1], dev2(two))
    full = gathered.at[0:real, :]
    for o in range(1, n1):
        send(full, result.at[one], s4.at[o - 1], r4.at[o - 1], dev1(q1(o)))
    result[one] = gathered[0:real, :]

    @pl.loop(0, n1)
    def _(o):
        q = lax.rem(one - o + n1, n1)

        @pl.when(o >= 1)
        def _():
            arrived(result.at[q], r4.at[o - 1], dev1(one))

        for i, row, height, col in pieces():
            outs[i][pl.ds(pl.multiple_of(q * height, height), height), col * width : (col + 1) * width] = result[
                q, row : row + height, :
            ].astype(F32)

    for o in range(n1 - 1):
        sent(packed.at[0], s1.at[o], dev1(one))
        sent(full, s4.at[o], dev1(one))
    for o in range(n2 - 1):
        sent(part(mid, two), s2.at[o], dev2(two))
        sent(mine, s3.at[o], dev2(two))


def total_over_devices(arrays):
    n1, n2 = NX * NY, NZ * NC
    width = 256
    real = sum(a.shape[0] * a.shape[1] for a in arrays) // (n1 * width)
    share = -(-real // (n2 * 16)) * 16
    return pl.pallas_call(
        total_kernel,
        out_shape=tuple(jax.ShapeDtypeStruct(a.shape, F32) for a in arrays),
        in_specs=[VM] * len(arrays),
        out_specs=tuple([VM] * len(arrays)),
        scratch_shapes=[
            pltpu.VMEM((n1, real, width), BF),
            pltpu.VMEM((n1 - 1, real, width), BF),
            pltpu.VMEM((share * n2, width), BF),
            pltpu.VMEM((n2 - 1, share, width), BF),
            pltpu.VMEM((share, width), BF),
            pltpu.VMEM((share * n2, width), BF),
            pltpu.VMEM((n1, real, width), BF),
            DMA((n1 - 1,)), DMA((n1 - 1,)),
            DMA((n2 - 1,)), DMA((n2 - 1,)),
            DMA((n2 - 1,)), DMA((n2 - 1,)),
            DMA((n1 - 1,)), DMA((n1 - 1,)),
        ],
        compiler_params=pltpu.CompilerParams(
            collective_id=3, has_side_effects=True, vmem_limit_bytes=VMEM_LIMIT
        ),
    )(*arrays)


def contract_rows(left, right):
    return lax.dot_general(left, right, (((0,), (0,)), ((), ())), preferred_element_type=F32)


def against_rows(left, right):
    return lax.dot_general(left, right, (((1,), (1,)), ((), ())), preferred_element_type=F32)


def heads_forward(bev_grid, weights):
    state = bev_grid
    stored = []
    for w_up, w_down in weights:
        scaling = lax.rsqrt(jnp.mean(state * state, axis=-1, keepdims=True) + eps)
        normed = (state * scaling).astype(BF)
        preact = jnp.dot(normed, w_up, preferred_element_type=F32)
        hidden = jax.nn.gelu(preact).astype(BF)
        stored.append((state, scaling, normed, preact, hidden))
        state = state + jnp.dot(hidden, w_down, preferred_element_type=F32)
    return (state.astype(BF), stored)


def heads_backward(cotangent, stored, weights):
    grad_state = cotangent
    gradients = []
    for saved_block, pair in zip(stored[::-1], weights[::-1]):
        state, scaling, normed, preact, hidden = saved_block
        w_up, w_down = pair
        rounded = grad_state.astype(BF)
        grad_down = contract_rows(hidden, rounded)
        grad_hidden = against_rows(rounded, w_down)
        gelu_slope = jax.jvp(jax.nn.gelu, (preact,), (jnp.ones_like(preact),))[1]
        grad_pre = (grad_hidden * gelu_slope).astype(BF)
        grad_up = contract_rows(normed, grad_pre)
        grad_normed = against_rows(grad_pre, w_up)
        unit_rows = state * scaling
        grad_state = grad_state + scaling * (
            grad_normed - unit_rows * jnp.mean(grad_normed * unit_rows, axis=-1, keepdims=True)
        )
        gradients = [grad_up, grad_down] + gradients
    return (grad_state, gradients)


def on_device(
    cams, vit_up, vit_down, proj, frustum_tiles, src_block, dst_block, live,
    render_up, render_down, decode_up, decode_down, pred_grad,
):
    tile_count = NX * NZ * NC
    cells, channels = pred_grad.shape[1:]
    index = jnp.zeros((8, 128), jnp.int32)
    index = lax.dynamic_update_slice(index, jnp.concatenate([src_block, dst_block, live], axis=0), (0, 0))
    encoded, x_all, tiles_all, index_all = encode(vit_up, vit_down, cams, proj, frustum_tiles[0], index)
    bev_grid = join(index_all, x_all, tiles_all, cells)
    weights = ((render_up, render_down), (decode_up, decode_down))
    prediction, stored = heads_forward(bev_grid, weights)
    scale_factor = 1.0 / math.sqrt(cams.shape[0] * cells * tile_count)
    cotangent = pred_grad[0].astype(F32) * scale_factor
    grad_grid, gradients = heads_backward(cotangent, stored, weights)
    grad_rows = split(index_all, grad_grid.astype(BF), tiles_all, cams.shape[1])
    grad_proj = contract_rows(encoded, grad_rows)
    totals = total_over_devices((grad_proj, gradients[0], gradients[1], gradients[2], gradients[3]))
    return (prediction[None], *totals)


def solution(mesh):
    placed = (
        P(None, "tile", None),
        P("section", None, None),
        P("section", None, None),
        P(),
        P("tile", None, None, None),
        P("tile", None),
        P("tile", None),
        P("tile", None),
        P(),
        P(),
        P(),
        P(),
        P("section", "tile", None),
    )
    return jax.shard_map(
        on_device,
        mesh=mesh,
        in_specs=placed,
        out_specs=(P("section", "tile", None), P(), P(), P(), P(), P()),
        check_vma=False,
    )
```

```python
import functools
import math

import jax
import jax.numpy as jnp
from jax import lax
from jax.experimental import pallas as pl
from jax.experimental.pallas import tpu as pltpu
from jax.sharding import PartitionSpec as P

eps = 1e-05
MESH = pl.DeviceIdType.MESH
BF = jnp.bfloat16
F32 = jnp.float32
NY, NX, NZ, NC = 4, 4, 8, 2
BLK = 128
VMEM_LIMIT = 60 * 2**20
ANY = pl.BlockSpec(memory_space=pl.ANY)
VM = pl.BlockSpec(memory_space=pltpu.VMEM)
SM = pl.BlockSpec(memory_space=pltpu.SMEM)
DMA = pltpu.SemaphoreType.DMA


def where_am_i():
    y = lax.axis_index("section")
    t = lax.axis_index("tile")
    return y, t // (NZ * NC), (t // NC) % NZ, t % NC


def at(y, x, z, c):
    return (y, (x * NZ + z) * NC + c)


def send(src, dst, ssem, rsem, device):
    copy = pltpu.make_async_remote_copy(
        src_ref=src, dst_ref=dst, send_sem=ssem, recv_sem=rsem, device_id=device, device_id_type=MESH
    )
    copy.start()


def sent(src, ssem, device):
    pltpu.make_async_remote_copy(
        src_ref=src, dst_ref=src, send_sem=ssem, recv_sem=ssem, device_id=device, device_id_type=MESH
    ).wait_send()


def arrived(dst, rsem, device):
    pltpu.make_async_remote_copy(
        src_ref=dst, dst_ref=dst, send_sem=rsem, recv_sem=rsem, device_id=device, device_id_type=MESH
    ).wait_recv()


def greet(devices):
    barrier = pltpu.get_barrier_semaphore()
    for device in devices:
        pl.semaphore_signal(barrier, inc=1, device_id=device, device_id_type=MESH)
    pl.semaphore_wait(barrier, len(devices))


def gelu(v):
    return 0.5 * v * (1.0 + jnp.tanh(math.sqrt(2.0 / math.pi) * (v + 0.044715 * v * v * v)))


def encoder_kernel(
    up, down, cams, proj, tiles, index,
    encoded, x_all, tiles_all, index_all,
    w_up, w_down, own, y_s, y_r, x_s, x_r, u_s, u_r, z_s, z_r, b_s, b_r, t_s, t_r, i_s, i_r, p_s, p_r, local,
):
    y, x, z, c = where_am_i()
    sibling = at(y, x, z, 1 - c)
    group = x * NC + c
    moved = NY - 1
    half = NZ // 2
    steps = half + 1
    n_group = NX * NC
    cols = w_up.shape[-1] // 2
    quarter = BLK // NY

    def layer_of(j):
        return j + jnp.where(j >= y, 1, 0)

    def up_slice(l, xx):
        return w_up.at[l, z, xx // 2, :, pl.ds(pl.multiple_of((xx % 2) * cols, 128), cols)]

    def zz(offset):
        return lax.rem(z + offset + 2 * NZ, NZ)

    def xx(offset):
        return lax.rem(x + offset + NX, NX)

    def yy(offset):
        return lax.rem(y + offset + NY, NY)

    def gg(offset):
        return lax.rem(group + offset + n_group, n_group)

    def g_dev(g):
        return at(y, g // NC, z, g % NC)

    east, west = at(y, xx(1), z, c), at(y, xx(-1), z, c)
    north, south = at(yy(1), x, z, c), at(yy(-1), x, z, c)

    def tile_rows(ref, section):
        return ref.at[:, pl.ds(pl.multiple_of(section * quarter, quarter), quarter), :]

    loads = [
        pltpu.make_async_copy(up, w_up.at[y], local.at[0]),
        pltpu.make_async_copy(down, w_down.at[y], local.at[1]),
        pltpu.make_async_copy(cams.at[y], encoded, local.at[2]),
        pltpu.make_async_copy(tile_rows(tiles.at[x, :, c], y), tile_rows(tiles_all.at[group], y), local.at[3]),
        pltpu.make_async_copy(index, index_all.at[group], local.at[4]),
    ]
    for load in loads:
        load.start()
    greet(
        [at(yy(o), x, z, c) for o in range(1, NY)]
        + [g_dev(gg(o)) for o in range(1, n_group)]
        + [at(y, x, zz(1), c), at(y, x, zz(-1), c)]
    )
    for load in loads[:3]:
        load.wait()

    def share(l, core):
        return up_slice(l, x) if core == 0 else w_down.at[l, z, x]

    for core in range(NC):
        @pl.when(c == core)
        def _(core=core):
            for o in range(1, NY):
                send(share(y, core), share(y, core), y_s.at[o - 1], y_r.at[o - 1], at(yy(o), x, z, c))

    def sign(j, d):
        return (1 - 2 * (j % 2)) * (1 - 2 * d)

    @pl.when(c == 0)
    def _():
        @pl.loop(0, moved)
        def _(j):
            l = layer_of(j)
            o = yy(-l)
            arrived(share(l, 0), y_r.at[o - 1], sibling)
            for ox in range(1, NX):
                send(up_slice(l, x), up_slice(l, x), u_s.at[j, ox - 1], u_r.at[j, ox - 1], at(y, xx(ox), z, c))

    def z_hops(d):
        return half if d == 0 else half - 1

    @pl.when(c == 1)
    def _():
        @pl.loop(0, steps * moved)
        def _(n):
            k = n // moved + 1
            j = n % moved
            l = layer_of(j)
            o = yy(-l)

            @pl.when(k == 1)
            def _():
                arrived(share(l, 1), y_r.at[o - 1], sibling)

            for d in range(2):
                s = sign(j, d)
                block = w_down.at[l, zz(-s * (k - 1)), x]

                @pl.when(jnp.logical_and(k >= 2, k <= z_hops(d) + 1))
                def _():
                    arrived(block, z_r.at[j, d, k - 2], sibling)

                @pl.when(k <= z_hops(d))
                def _():
                    send(block, block, z_s.at[j, d, k - 1], z_r.at[j, d, k - 1], at(y, x, zz(s), c))

    def layer_rows(l, r, rows):
        wide = encoded[pl.ds(r, rows), :].astype(F32)
        scaling = lax.rsqrt(jnp.mean(wide * wide, axis=-1, keepdims=True) + eps)
        normed = (wide * scaling).astype(BF)
        total = wide
        parts = 2
        for q in range(parts):
            width = w_up.shape[-1] // parts
            w1 = w_up[l, :, :, :, q * width : (q + 1) * width].reshape(wide.shape[1], width)
            hidden = gelu(jnp.dot(normed, w1, preferred_element_type=F32)).astype(BF)
            nz = NZ // parts
            w2 = w_down[l, q * nz : (q + 1) * nz].reshape(width, wide.shape[1])
            total = total + jnp.dot(hidden, w2, preferred_element_type=F32)
        encoded[pl.ds(r, rows), :] = total.astype(BF)

    tokens = encoded.shape[0]
    rows = tokens // 2

    def wait_sibling(j):
        l = layer_of(j)

        @pl.when(c == 0)
        def _():
            for i, ox in enumerate((0, 1, NX - 1, 2)):
                arrived(w_down.at[l, :, xx(-ox)], b_r.at[j, i], sibling)

        @pl.when(c == 1)
        def _():
            arrived(w_up.at[l, z], b_r.at[j, 0], sibling)
            for d in range(2):
                for k in range(2, z_hops(d) + 2):
                    arrived(w_up.at[l, zz(-sign(j, d) * (k - 1))], b_r.at[j, 1 + d * half + k - 2], sibling)

    def second_half(l, xo, h):
        return w_down.at[l, pl.ds(h * half, half), xo]

    def begin(j):
        l = layer_of(j)

        @pl.when(c == 0)
        def _():
            for ox in range(1, NX):
                arrived(up_slice(l, xx(-ox)), u_r.at[j, ox - 1], sibling)
            block = w_up.at[l, z]
            for d in range(2):
                if z_hops(d) >= 1:
                    send(block, block, z_s.at[j, d, 0], z_r.at[j, d, 0], at(y, x, zz(sign(j, d)), c))
            send(block, block, b_s.at[j, 0], b_r.at[j, 0], sibling)

        @pl.when(c == 1)
        def _():
            block = w_down.at[l, :, x]
            send(block, block, x_s.at[j, 0], x_r.at[j, 0], east)
            send(block, block, x_s.at[j, 1], x_r.at[j, 1], west)
            send(block, block, b_s.at[j, 0], b_r.at[j, 0], sibling)

    begin(0)

    for o in range(1, n_group):
        g = gg(o)
        send(index, index_all.at[group], i_s.at[o - 1], i_r.at[o - 1], g_dev(g))
        send(
            tile_rows(tiles.at[g // NC, :, g % NC], y), tile_rows(tiles_all.at[group], y),
            t_s.at[o - 1], t_r.at[o - 1], g_dev(g),
        )

    def own_rows(section):
        return tiles_all.at[:, :, pl.ds(pl.multiple_of(section * quarter, quarter), quarter), :]

    def some_rows(section, h):
        return tiles_all.at[
            pl.ds(h * n_group // 2, n_group // 2), :, pl.ds(pl.multiple_of(section * quarter, quarter), quarter), :
        ]

    t0 = n_group - 1

    @pl.loop(0, steps * moved)
    def _(n):
        j = n // steps
        k = n % steps + 1
        l = layer_of(j)

        @pl.when(jnp.logical_and(c == 0, k >= 2))
        def _():
            for d in range(2):
                s = sign(j, d)
                block = w_up.at[l, zz(-s * (k - 1))]

                @pl.when(k <= z_hops(d) + 1)
                def _():
                    arrived(block, z_r.at[j, d, k - 2], sibling)

                    @pl.when(k <= z_hops(d))
                    def _():
                        send(block, block, z_s.at[j, d, k - 1], z_r.at[j, d, k - 1], at(y, x, zz(s), c))

                    send(block, block, b_s.at[j, 1 + d * half + k - 2], b_r.at[j, 1 + d * half + k - 2], sibling)

            @pl.when(jnp.logical_and(k == half, j + 1 < moved))
            def _():
                begin(j + 1)

        @pl.when(c == 1)
        def _():
            @pl.when(k == 2)
            def _():
                block = w_down.at[l, :, xx(-1)]
                arrived(block, x_r.at[j, 0], sibling)
                send(second_half(l, xx(-1), 0), second_half(l, xx(-1), 0), x_s.at[j, 2], x_r.at[j, 2], east)
                send(block, block, b_s.at[j, 1], b_r.at[j, 1], sibling)
                other = w_down.at[l, :, xx(1)]
                arrived(other, x_r.at[j, 1], sibling)
                send(second_half(l, xx(1), 1), second_half(l, xx(1), 1), x_s.at[j, 3], x_r.at[j, 3], west)
                send(other, other, b_s.at[j, 2], b_r.at[j, 2], sibling)

                @pl.when(j + 1 < moved)
                def _():
                    begin(j + 1)

            @pl.when(k == steps)
            def _():
                arrived(second_half(l, xx(2), 0), x_r.at[j, 2], sibling)
                arrived(second_half(l, xx(2), 1), x_r.at[j, 3], sibling)
                block = w_down.at[l, :, xx(2)]
                send(block, block, b_s.at[j, 3], b_r.at[j, 3], sibling)

        @pl.when(n == 3)
        def _():
            for load in loads[3:]:
                load.wait()
            for o in range(1, n_group):
                arrived(tile_rows(tiles_all.at[gg(-o)], y), t_r.at[o - 1], sibling)
            send(own_rows(y), own_rows(y), t_s.at[t0], t_r.at[t0], north)
            send(own_rows(y), own_rows(y), t_s.at[t0 + 1], t_r.at[t0 + 1], south)

        @pl.when(n == 3 + 2 * (moved * steps // 5))
        def _():
            arrived(own_rows(yy(-1)), t_r.at[t0], sibling)
            send(some_rows(yy(-1), 0), some_rows(yy(-1), 0), t_s.at[t0 + 2], t_r.at[t0 + 2], north)
            arrived(own_rows(yy(1)), t_r.at[t0 + 1], sibling)
            send(some_rows(yy(1), 1), some_rows(yy(1), 1), t_s.at[t0 + 3], t_r.at[t0 + 3], south)

        @pl.when(j >= 1)
        def _():
            @pl.when(k == 1)
            def _():
                wait_sibling(j - 1)

            @pl.when(jnp.logical_or(k == 2, k == steps))
            def _():
                layer_rows(j - 1, pl.multiple_of(jnp.where(k == 2, 0, rows), rows), rows)

            if steps == 2:
                @pl.when(k == 2)
                def _():
                    layer_rows(j - 1, rows, rows)

    wait_sibling(moved - 1)

    @pl.loop(0, 3)
    def _(n):
        layer_rows(NY - 2 + n // 2, pl.multiple_of((n % 2) * rows, rows), rows)

    def half_of(g, h):
        return x_all.at[g, pl.ds(h * rows, rows), :]

    def project(h):
        mine = own.at[h * rows : (h + 1) * rows]
        mine[...] = jnp.dot(encoded[h * rows : (h + 1) * rows], proj[...], preferred_element_type=F32).astype(BF)
        send(mine, half_of(group, h), p_s.at[h], p_r.at[h], east)
        send(mine, half_of(group, h), p_s.at[2 + h], p_r.at[2 + h], west)
        send(mine, half_of(group, h), p_s.at[4 + h], p_r.at[4 + h], sibling)

    project(0)
    layer_rows(NY - 1, rows, rows)
    project(1)
    keep = pltpu.make_async_copy(own, x_all.at[group], local.at[5])
    keep.start()
    near, far = (xx(-1) * NC + c, xx(1) * NC + c), xx(2) * NC + c
    arrived(half_of(near[0], 0), p_r.at[0], sibling)
    send(half_of(near[0], 0), half_of(near[0], 0), p_s.at[6], p_r.at[6], east)
    arrived(half_of(near[1], 0), p_r.at[2], sibling)
    arrived(half_of(near[1], 1), p_r.at[3], sibling)
    send(half_of(near[1], 1), half_of(near[1], 1), p_s.at[7], p_r.at[7], west)
    send(x_all.at[near[1]], x_all.at[near[1]], p_s.at[9], p_r.at[9], sibling)
    arrived(half_of(near[0], 1), p_r.at[1], sibling)
    send(x_all.at[near[0]], x_all.at[near[0]], p_s.at[8], p_r.at[8], sibling)
    arrived(half_of(far, 0), p_r.at[6], sibling)
    arrived(half_of(far, 1), p_r.at[7], sibling)
    send(x_all.at[far], x_all.at[far], p_s.at[10], p_r.at[10], sibling)
    for h in range(2):
        arrived(half_of(x * NC + 1 - c, h), p_r.at[4 + h], sibling)
    for i, ox in enumerate((-1, 1, 2)):
        arrived(x_all.at[xx(ox) * NC + 1 - c], p_r.at[8 + i], sibling)

    keep.wait()
    arrived(some_rows(yy(2), 0), t_r.at[t0 + 2], sibling)
    arrived(some_rows(yy(2), 1), t_r.at[t0 + 3], sibling)
    for o in range(1, n_group):
        arrived(index_all.at[gg(-o)], i_r.at[o - 1], sibling)
        sent(tile_rows(tiles_all.at[group], y), t_s.at[o - 1], sibling)
        sent(index_all.at[group], i_s.at[o - 1], sibling)
    for i in range(2):
        sent(own_rows(y), t_s.at[t0 + i], sibling)
        sent(some_rows(y, 0), t_s.at[t0 + 2 + i], sibling)
    for i in range(8):
        sent(own.at[0:rows], p_s.at[i], sibling)
    for i in range(8, 11):
        sent(own, p_s.at[i], sibling)
    for core in range(NC):
        @pl.when(c == core)
        def _(core=core):
            for o in range(1, NY):
                sent(share(y, core), y_s.at[o - 1], sibling)

    @pl.loop(0, moved)
    def _(j):
        @pl.when(c == 0)
        def _():
            for ox in range(1, NX):
                sent(up_slice(y, x), u_s.at[j, ox - 1], sibling)
            for d in range(2):
                for k in range(1, z_hops(d) + 1):
                    sent(w_up.at[y, z], z_s.at[j, d, k - 1], sibling)
            for i in range(NZ):
                sent(w_up.at[y, z], b_s.at[j, i], sibling)

        @pl.when(c == 1)
        def _():
            for i in range(2):
                sent(w_down.at[y, :, x], x_s.at[j, i], sibling)
                sent(second_half(y, x, 0), x_s.at[j, 2 + i], sibling)
            for d in range(2):
                for k in range(1, z_hops(d) + 1):
                    sent(w_down.at[y, z, x], z_s.at[j, d, k - 1], sibling)
            for i in range(NX):
                sent(w_down.at[y, :, x], b_s.at[j, i], sibling)


def encode(up, down, cams, proj, tiles, index):
    d, f = up.shape[1:]
    tokens = cams.shape[1]
    channels = proj.shape[1]
    up = up.reshape(NZ, NX // 2, 2 * d // (NZ * NX), f)
    down = down.reshape(NZ, NX, f // (NZ * NX), d)
    tiles = tiles.reshape(NX, NZ, NC, BLK, BLK)
    n = NX * NC
    half = NZ // 2
    moved = NY - 1
    return pl.pallas_call(
        encoder_kernel,
        out_shape=(
            jax.ShapeDtypeStruct((tokens, d), BF),
            jax.ShapeDtypeStruct((n, tokens, channels), BF),
            jax.ShapeDtypeStruct((n, NZ, BLK, BLK), BF),
            jax.ShapeDtypeStruct((n,) + index.shape, jnp.int32),
        ),
        in_specs=[ANY, ANY, ANY, VM, ANY, ANY],
        out_specs=(VM, ANY, ANY, ANY),
        scratch_shapes=[
            pltpu.VMEM((NY,) + up.shape, BF),
            pltpu.VMEM((NY,) + down.shape, BF),
            pltpu.VMEM((tokens, channels), BF),
            DMA((NY - 1,)), DMA((NY - 1,)),
            DMA((moved, 4)), DMA((moved, 4)),
            DMA((moved, NX - 1)), DMA((moved, NX - 1)),
            DMA((moved, 2, half)), DMA((moved, 2, half)),
            DMA((moved, max(NZ, NX))), DMA((moved, max(NZ, NX))),
            DMA((n + 3,)), DMA((n + 3,)),
            DMA((n - 1,)), DMA((n - 1,)),
            DMA((11,)), DMA((11,)),
            DMA((6,)),
        ],
        compiler_params=pltpu.CompilerParams(
            collective_id=0, has_side_effects=True, vmem_limit_bytes=VMEM_LIMIT
        ),
    )(up, down, cams, proj, tiles, index)


def join_kernel(index, x_all, tiles, grid_out, left, right, parts, s_buf, r_buf, s_sem, r_sem):
    y, x, z, c = where_am_i()
    half = NZ // 2
    n_group = NX * NC
    bev = grid_out.shape[0] // BLK
    chunk = grid_out.shape[0] // 2

    def zz(offset):
        return lax.rem(z + offset + 2 * NZ, NZ)

    beside = (at(y, x, zz(1), c), at(y, x, zz(-1), c))
    greet(beside)

    def hops(ch, d):
        return half if ch == d else half - 1

    def push(ch, d, k):
        send(s_buf.at[ch, d, k - 1], r_buf.at[ch, d, k - 1], s_sem.at[ch, d, k - 1], r_sem.at[ch, d, k - 1], beside[d])

    @pl.loop(0, NZ)
    def _(i):
        off = jnp.where(i == 0, half, jnp.where(i % 2 == 1, (NZ - 1 - i) // 2, -((NZ - i) // 2)))
        target = zz(off)
        p = (x * NZ + target) * NC + c
        for g in range(n_group):
            tile = tiles[g, target].astype(F32)
            dst = index[g, 1, p]
            alive = index[g, 2, p]
            for b in range(bev):
                weight = jnp.where(dst == b, alive, 0).astype(F32)
                left[b * BLK : (b + 1) * BLK, g * BLK : (g + 1) * BLK] = (tile * weight).astype(BF)
            right[g * BLK : (g + 1) * BLK, :] = x_all[g, index[g, 0, p]]
        parts[i] = jnp.dot(left[...], right[...], preferred_element_type=F32)

        @pl.when(i == 0)
        def _():
            for d in range(2):
                s_buf[d, d, 0] = parts[0, d * chunk : (d + 1) * chunk].astype(BF)
                push(d, d, 1)

        for d in range(2):
            if half == 1:
                continue

            @pl.when(i == 1 + d)
            def _(d=d):
                ch = 1 - d
                s_buf[ch, d, 0] = parts[1 + d, ch * chunk : (ch + 1) * chunk].astype(BF)
                push(ch, d, 1)

    for o in range(half - 1, 0, -1):
        for ch_is_d in (True, False):
            for d in range(2):
                ch = d if ch_is_d else 1 - d
                k = hops(ch, d) - o + 1
                if k == 1:
                    continue
                arrived(r_buf.at[ch, d, k - 2], r_sem.at[ch, d, k - 2], beside[d])
                i = NZ - 1 - 2 * o if d == 0 else NZ - 2 * o
                total = parts[i, ch * chunk : (ch + 1) * chunk] + r_buf[ch, d, k - 2].astype(F32)
                s_buf[ch, d, k - 1] = total.astype(BF)
                push(ch, d, k)
    for ch in range(2):
        total = parts[NZ - 1, ch * chunk : (ch + 1) * chunk]
        for d in range(2):
            k = hops(ch, d)
            if k == 0:
                continue
            arrived(r_buf.at[ch, d, k - 1], r_sem.at[ch, d, k - 1], beside[d])
            total = total + r_buf[ch, d, k - 1].astype(F32)
        grid_out[ch * chunk : (ch + 1) * chunk] = total
    for ch in range(2):
        for d in range(2):
            for k in range(hops(ch, d)):
                sent(s_buf.at[ch, d, k], s_sem.at[ch, d, k], beside[d])


def join(index_all, x_all, tiles_all, cells):
    channels = x_all.shape[-1]
    x_all = x_all.reshape(x_all.shape[0], -1, BLK, channels)
    n = NX * NC
    half = NZ // 2
    return pl.pallas_call(
        join_kernel,
        out_shape=jax.ShapeDtypeStruct((cells, channels), F32),
        in_specs=[SM, VM, VM],
        out_specs=VM,
        scratch_shapes=[
            pltpu.VMEM((cells, n * BLK), BF),
            pltpu.VMEM((n * BLK, channels), BF),
            pltpu.VMEM((NZ, cells, channels), F32),
            pltpu.VMEM((2, 2, half, cells // 2, channels), BF),
            pltpu.VMEM((2, 2, half, cells // 2, channels), BF),
            DMA((2, 2, half)), DMA((2, 2, half)),
        ],
        compiler_params=pltpu.CompilerParams(
            collective_id=1, has_side_effects=True, vmem_limit_bytes=VMEM_LIMIT
        ),
    )(index_all, x_all, tiles_all)


class Total:
    n1, n2, width = NX * NY, NZ, 128

    def __init__(self, ins, outs, scratch):
        self.ins, self.outs = ins, outs
        (
            self.packed, self.from0, self.half, self.from1, self.mid, self.from2, self.mine, self.gathered, self.result,
            self.s0, self.r0, self.s1, self.r1, self.s2, self.r2, self.s3, self.r3, self.s4, self.r4, self.s5, self.r5,
        ) = scratch
        y, x, z, c = where_am_i()
        self.y, self.x, self.z, self.c = y, x, z, c
        self.one, self.two = y * NX + x, z
        self.sibling = at(y, x, z, 1 - c)
        self.real = self.half.shape[1]
        self.share = self.mine.shape[0]

    @classmethod
    def scratch_for(cls, shapes):
        n1, n2, width = NX * NY, NZ, cls.width
        real = sum(a * b for a, b in shapes) // (n1 * NC * width)
        share = -(-real // (n2 * 16)) * 16
        buffers = [
            (NC, n1, real, width), (n1, real, width), (n1, real, width), (n1 - 1, real, width), (share * n2, width),
            (n2 - 1, share, width), (share, width), (share * n2, width), (NC, n1, real, width),
        ]
        counts = [1, n1 - 1, n2 - 1, n2 - 1, n1 - 1, 1]
        return [pltpu.VMEM(b, BF) for b in buffers] + [DMA((n,)) for n in counts for _ in range(2)]

    def dev1(self, q):
        return at(q // NX, q % NX, self.z, self.c)

    def dev2(self, e):
        return at(self.y, self.x, e, self.c)

    def q1(self, o):
        n1 = NX * NY
        return lax.rem(self.one + o + n1, n1)

    def q2(self, o):
        return lax.rem(self.two + o + NZ, NZ)

    def peers(self):
        n1 = NX * NY
        return [self.sibling] + [self.dev1(self.q1(o)) for o in range(1, n1)] + [self.dev2(self.q2(o)) for o in range(1, NZ)]

    def pieces(self):
        row = 0
        for i, ref in enumerate(self.ins):
            height = ref.shape[0] // (NX * NY)
            for col in range(ref.shape[1] // (NC * self.width)):
                yield i, row, height, col * NC * self.width
                row += height

    def start(self):
        n1 = NX * NY

        @pl.loop(0, n1)
        def _(q):
            for i, row, height, col in self.pieces():
                for core in range(NC):
                    left = col + core * self.width
                    self.packed[core, q, row : row + height, :] = self.ins[i][
                        pl.ds(pl.multiple_of(q * height, height), height), left : left + self.width
                    ].astype(BF)
        send(self.packed.at[1 - self.c], self.from0, self.s0.at[0], self.r0.at[0], self.sibling)
        self.mid[...] = jnp.zeros_like(self.mid)

    def over_xy(self):
        n1 = NX * NY
        arrived(self.from0, self.r0.at[0], self.sibling)

        @pl.loop(0, n1)
        def _(o):
            q = lax.rem(self.one + 1 + o, n1)
            self.half[q] = (self.packed[self.c, q].astype(F32) + self.from0[q].astype(F32)).astype(BF)

            @pl.when(o < n1 - 1)
            def _():
                send(self.half.at[q], self.from1.at[o], self.s1.at[o], self.r1.at[o], self.dev1(q))

    def part(self, ref, e):
        return ref.at[pl.ds(pl.multiple_of(e * self.share, self.share), self.share), :]

    def over_z(self):
        total = self.half[self.one].astype(F32)
        for o in range(NX * NY - 1):
            arrived(self.from1.at[o], self.r1.at[o], self.sibling)
            total = total + self.from1[o].astype(F32)
        self.mid[0 : self.real, :] = total.astype(BF)
        for o in range(1, NZ):
            e = self.q2(o)
            send(self.part(self.mid, e), self.from2.at[o - 1], self.s2.at[o - 1], self.r2.at[o - 1], self.dev2(e))

    def back_over_z(self):
        total = self.mid[pl.ds(pl.multiple_of(self.two * self.share, self.share), self.share), :].astype(F32)
        for o in range(1, NZ):
            arrived(self.from2.at[o - 1], self.r2.at[o - 1], self.sibling)
            total = total + self.from2[o - 1].astype(F32)
        self.mine[...] = total.astype(BF)
        for o in range(1, NZ):
            send(self.mine, self.part(self.gathered, self.two), self.s3.at[o - 1], self.r3.at[o - 1], self.dev2(self.q2(o)))
        self.gathered[pl.ds(pl.multiple_of(self.two * self.share, self.share), self.share), :] = self.mine[...]

    def back_over_xy(self):
        for o in range(1, NZ):
            arrived(self.part(self.gathered, self.q2(-o)), self.r3.at[o - 1], self.sibling)
        for o in range(1, NX * NY):
            send(
                self.gathered.at[0 : self.real, :], self.result.at[self.c, self.one],
                self.s4.at[o - 1], self.r4.at[o - 1], self.dev1(self.q1(o)),
            )
        self.result[self.c, self.one] = self.gathered[0 : self.real, :]

    def back_over_core(self):
        for o in range(1, NX * NY):
            arrived(self.result.at[self.c, self.q1(-o)], self.r4.at[o - 1], self.sibling)
        send(self.result.at[self.c], self.result.at[self.c], self.s5.at[0], self.r5.at[0], self.sibling)

    def finish(self):
        n1 = NX * NY
        arrived(self.result.at[1 - self.c], self.r5.at[0], self.sibling)

        @pl.loop(0, n1)
        def _(q):
            for i, row, height, col in self.pieces():
                for core in range(NC):
                    left = col + core * self.width
                    self.outs[i][pl.ds(pl.multiple_of(q * height, height), height), left : left + self.width] = self.result[
                        core, q, row : row + height, :
                    ].astype(F32)

        sent(self.from0, self.s0.at[0], self.sibling)
        sent(self.result.at[self.c], self.s5.at[0], self.sibling)
        for o in range(n1 - 1):
            sent(self.half.at[0], self.s1.at[o], self.sibling)
            sent(self.half.at[0], self.s4.at[o], self.sibling)
        for o in range(NZ - 1):
            sent(self.mine, self.s2.at[o], self.sibling)
            sent(self.mine, self.s3.at[o], self.sibling)


def total_kernel(value, out, *scratch):
    total = Total([value], [out], scratch)
    greet(total.peers())
    total.start()
    total.over_xy()
    total.over_z()
    total.back_over_z()
    total.back_over_xy()
    total.back_over_core()
    total.finish()


def total_over_devices(value):
    return pl.pallas_call(
        total_kernel,
        out_shape=jax.ShapeDtypeStruct(value.shape, F32),
        in_specs=[VM],
        out_specs=VM,
        scratch_shapes=Total.scratch_for([value.shape]),
        compiler_params=pltpu.CompilerParams(
            collective_id=3, has_side_effects=True, vmem_limit_bytes=VMEM_LIMIT
        ),
    )(value)


N_GRADS = 4


def split_kernel(index, grad, tiles, *refs):
    ins, refs = refs[:N_GRADS], refs[N_GRADS:]
    rows_out, outs, refs = refs[0], refs[1 : 1 + N_GRADS], refs[1 + N_GRADS :]
    all_grad, here, left, acc, core_s, core_r, x_send, x_recv, z_s, z_r, c_s, c_r, x_s, x_r, local = refs[:15]
    total = Total(ins, outs, refs[15:])
    y, x, z, c = where_am_i()
    half = NZ // 2
    n_group = NX * NC
    chunk = grad.shape[0] // 2
    cam = rows_out.shape[0] // BLK
    sibling = at(y, x, z, 1 - c)

    def zz(offset):
        return lax.rem(z + offset + 2 * NZ, NZ)

    def xx(offset):
        return lax.rem(x + offset + NX, NX)

    beside = (at(y, x, zz(1), c), at(y, x, zz(-1), c))
    east, west = at(y, xx(1), z, c), at(y, xx(-1), z, c)
    keep = pltpu.make_async_copy(grad, all_grad.at[z], local)
    keep.start()
    greet(total.peers())
    keep.wait()

    def hops(ch, d):
        return half if ch == d else half - 1

    def part(origin, ch):
        return all_grad.at[origin, pl.ds(ch * chunk, chunk)]

    for ch in range(2):
        for d in range(2):
            if hops(ch, d) >= 1:
                send(part(z, ch), part(z, ch), z_s.at[ch, d, 0], z_r.at[ch, d, 0], beside[d])
    total.start()

    def use(origin, first):
        p = (x * NZ + origin) * NC + c
        here[...] = all_grad[origin].reshape(here.shape)
        for g in range(n_group):
            tile = tiles[g, origin].astype(F32).T
            src = index[g, 0, p]
            alive = index[g, 2, p]
            for k in range(cam):
                weight = jnp.where(src == k, alive, 0).astype(F32)
                left[k * BLK : (k + 1) * BLK, :] = (tile * weight).astype(BF)
            product = jnp.dot(left[...], here[index[g, 1, p]], preferred_element_type=F32)
            if first:
                acc[g] = product
            else:
                acc[g] = acc[g] + product

    use(z, True)
    total.over_xy()

    @pl.loop(1, half + 1)
    def _(k):
        for d in range(2):
            s = 1 - 2 * d
            origin = zz(-s * k)
            for ch in range(2):
                @pl.when(k <= hops(ch, d))
                def _(ch=ch, d=d):
                    arrived(part(origin, ch), z_r.at[ch, d, k - 1], beside[d])

                @pl.when(k + 1 <= hops(ch, d))
                def _(ch=ch, d=d):
                    send(part(origin, ch), part(origin, ch), z_s.at[ch, d, k], z_r.at[ch, d, k], beside[d])

        @pl.when(k == max(half - 2, 1))
        def _():
            total.over_z()

        @pl.when(k == max(half - 1, 1))
        def _():
            total.back_over_z()

        @pl.when(k == half)
        def _():
            total.back_over_xy()

        use(zz(-k), False)

        @pl.when(k < half)
        def _():
            use(zz(k), False)

    rows = rows_out.shape[0] // 2
    order = (2, 1, NX - 1, 0)
    for i, o in enumerate(order):
        core_s[i] = acc[xx(o) * NC + 1 - c].astype(BF)
        send(core_s.at[i], core_r.at[i], c_s.at[i], c_r.at[i], sibling)

    def pair_sum(i, h):
        return acc[xx(order[i]) * NC + c, h * rows : (h + 1) * rows, :] + core_r[
            i, h * rows : (h + 1) * rows, :
        ].astype(F32)

    def push(n, value, device):
        x_send[n] = value.astype(BF)
        send(x_send.at[n], x_recv.at[n], x_s.at[n], x_r.at[n], device)

    for i in range(3):
        arrived(core_r.at[i], c_r.at[i], sibling)
        if i == 0:
            push(0, pair_sum(0, 0), east)
            push(1, pair_sum(0, 1), west)
        if i == 1:
            push(2, pair_sum(1, 1), east)
        if i == 2:
            push(3, pair_sum(2, 0), west)
    arrived(x_recv.at[0], x_r.at[0], sibling)
    push(4, pair_sum(1, 0) + x_recv[0].astype(F32), east)
    arrived(x_recv.at[1], x_r.at[1], sibling)
    push(5, pair_sum(2, 1) + x_recv[1].astype(F32), west)
    arrived(core_r.at[3], c_r.at[3], sibling)
    total.back_over_core()
    for n in range(2, 6):
        arrived(x_recv.at[n], x_r.at[n], sibling)
    rows_out[0:rows] = (pair_sum(3, 0) + x_recv[4].astype(F32) + x_recv[3].astype(F32)).astype(BF)
    rows_out[rows : 2 * rows] = (pair_sum(3, 1) + x_recv[2].astype(F32) + x_recv[5].astype(F32)).astype(BF)
    total.finish()
    for i in range(4):
        sent(core_s.at[i], c_s.at[i], sibling)
    for n in range(6):
        sent(x_send.at[n], x_s.at[n], sibling)
    for ch in range(2):
        for d in range(2):
            for k in range(hops(ch, d)):
                sent(part(z, ch), z_s.at[ch, d, k], beside[d])


def split(index_all, grad, tiles_all, tokens, gradients):
    cells, channels = grad.shape
    n = NX * NC
    half = NZ // 2
    shapes = [g.shape for g in gradients]
    return pl.pallas_call(
        split_kernel,
        out_shape=(jax.ShapeDtypeStruct((tokens, channels), BF),) + tuple(jax.ShapeDtypeStruct(a, F32) for a in shapes),
        in_specs=[SM, VM, VM] + [VM] * N_GRADS,
        out_specs=tuple([VM] * (1 + N_GRADS)),
        scratch_shapes=[
            pltpu.VMEM((NZ, cells, channels), BF),
            pltpu.VMEM((cells // BLK, BLK, channels), BF),
            pltpu.VMEM((tokens, BLK), BF),
            pltpu.VMEM((n, tokens, channels), F32),
            pltpu.VMEM((NX, tokens, channels), BF),
            pltpu.VMEM((NX, tokens, channels), BF),
            pltpu.VMEM((6, tokens // 2, channels), BF),
            pltpu.VMEM((6, tokens // 2, channels), BF),
            DMA((2, 2, half)), DMA((2, 2, half)),
            DMA((NX,)), DMA((NX,)),
            DMA((6,)), DMA((6,)),
            DMA(()),
        ] + Total.scratch_for(shapes),
        compiler_params=pltpu.CompilerParams(
            collective_id=2, has_side_effects=True, vmem_limit_bytes=VMEM_LIMIT
        ),
    )(index_all, grad, tiles_all, *gradients)


def contract_rows(left, right):
    return lax.dot_general(left, right, (((0,), (0,)), ((), ())), preferred_element_type=F32)


def against_rows(left, right):
    return lax.dot_general(left, right, (((1,), (1,)), ((), ())), preferred_element_type=F32)


def heads_forward(bev_grid, weights):
    state = bev_grid
    stored = []
    for w_up, w_down in weights:
        scaling = lax.rsqrt(jnp.mean(state * state, axis=-1, keepdims=True) + eps)
        normed = (state * scaling).astype(BF)
        preact = jnp.dot(normed, w_up, preferred_element_type=F32)
        hidden = jax.nn.gelu(preact).astype(BF)
        stored.append((state, scaling, normed, preact, hidden))
        state = state + jnp.dot(hidden, w_down, preferred_element_type=F32)
    return (state.astype(BF), stored)


def heads_backward(cotangent, stored, weights):
    grad_state = cotangent
    gradients = []
    for saved_block, pair in zip(stored[::-1], weights[::-1]):
        state, scaling, normed, preact, hidden = saved_block
        w_up, w_down = pair
        rounded = grad_state.astype(BF)
        grad_down = contract_rows(hidden, rounded)
        grad_hidden = against_rows(rounded, w_down)
        gelu_slope = jax.jvp(jax.nn.gelu, (preact,), (jnp.ones_like(preact),))[1]
        grad_pre = (grad_hidden * gelu_slope).astype(BF)
        grad_up = contract_rows(normed, grad_pre)
        grad_normed = against_rows(grad_pre, w_up)
        unit_rows = state * scaling
        grad_state = grad_state + scaling * (
            grad_normed - unit_rows * jnp.mean(grad_normed * unit_rows, axis=-1, keepdims=True)
        )
        gradients = [grad_up, grad_down] + gradients
    return (grad_state, gradients)


def on_device(
    cams, vit_up, vit_down, proj, frustum_tiles, src_block, dst_block, live,
    render_up, render_down, decode_up, decode_down, pred_grad,
):
    tile_count = NX * NZ * NC
    cells, channels = pred_grad.shape[1:]
    index = jnp.zeros((8, 128), jnp.int32)
    index = lax.dynamic_update_slice(index, jnp.concatenate([src_block, dst_block, live], axis=0), (0, 0))
    encoded, x_all, tiles_all, index_all = encode(vit_up, vit_down, cams, proj, frustum_tiles[0], index)
    bev_grid = join(index_all, x_all, tiles_all, cells)
    weights = ((render_up, render_down), (decode_up, decode_down))
    prediction, stored = heads_forward(bev_grid, weights)
    scale_factor = 1.0 / math.sqrt(cams.shape[0] * cells * tile_count)
    cotangent = pred_grad[0].astype(F32) * scale_factor
    grad_grid, gradients = heads_backward(cotangent, stored, weights)
    grad_rows, *totals = split(index_all, grad_grid.astype(BF), tiles_all, cams.shape[1], gradients)
    grad_proj = total_over_devices(contract_rows(encoded, grad_rows))
    return (prediction[None], grad_proj, *totals)


def solution(mesh):
    placed = (
        P(None, "tile", None),
        P("section", None, None),
        P("section", None, None),
        P(),
        P("tile", None, None, None),
        P("tile", None),
        P("tile", None),
        P("tile", None),
        P(),
        P(),
        P(),
        P(),
        P("section", "tile", None),
    )
    return jax.shard_map(
        on_device,
        mesh=mesh,
        in_specs=placed,
        out_specs=(P("section", "tile", None), P(), P(), P(), P(), P()),
        check_vma=False,
    )
```

```python
import functools
import math

import jax
import jax.numpy as jnp
from jax import lax
from jax.experimental import pallas as pl
from jax.experimental.pallas import tpu as pltpu
from jax.sharding import PartitionSpec as P

eps = 1e-05
MESH = pl.DeviceIdType.MESH
BF = jnp.bfloat16
F32 = jnp.float32
NY, NX, NZ, NC = 4, 4, 8, 2
BLK = 128
VMEM_LIMIT = 60 * 2**20
ANY = pl.BlockSpec(memory_space=pl.ANY)
VM = pl.BlockSpec(memory_space=pltpu.VMEM)
SM = pl.BlockSpec(memory_space=pltpu.SMEM)
DMA = pltpu.SemaphoreType.DMA


def where_am_i():
    y = lax.axis_index("section")
    t = lax.axis_index("tile")
    return y, t // (NZ * NC), (t // NC) % NZ, t % NC


def at(y, x, z, c):
    return (y, (x * NZ + z) * NC + c)


def send(src, dst, ssem, rsem, device):
    copy = pltpu.make_async_remote_copy(
        src_ref=src, dst_ref=dst, send_sem=ssem, recv_sem=rsem, device_id=device, device_id_type=MESH
    )
    copy.start()


def sent(src, ssem, device):
    pltpu.make_async_remote_copy(
        src_ref=src, dst_ref=src, send_sem=ssem, recv_sem=ssem, device_id=device, device_id_type=MESH
    ).wait_send()


def arrived(dst, rsem, device):
    pltpu.make_async_remote_copy(
        src_ref=dst, dst_ref=dst, send_sem=rsem, recv_sem=rsem, device_id=device, device_id_type=MESH
    ).wait_recv()


def greet(devices):
    barrier = pltpu.get_barrier_semaphore()
    for device in devices:
        pl.semaphore_signal(barrier, inc=1, device_id=device, device_id_type=MESH)
    pl.semaphore_wait(barrier, len(devices))


def gelu(v):
    return 0.5 * v * (1.0 + jnp.tanh(math.sqrt(2.0 / math.pi) * (v + 0.044715 * v * v * v)))


def contract_rows(left, right):
    return lax.dot_general(left, right, (((0,), (0,)), ((), ())), preferred_element_type=F32)


def against_rows(left, right):
    return lax.dot_general(left, right, (((1,), (1,)), ((), ())), preferred_element_type=F32)


def encoder_kernel(
    up, down, cams, proj, tiles, index,
    encoded, x_all, tiles_all, index_all,
    w_up, w_down, own, y_s, y_r, x_s, x_r, u_s, u_r, z_s, z_r, b_s, b_r, t_s, t_r, i_s, i_r, p_s, p_r, v_s, v_r, w_s, w_r,
    local,
):
    y, x, z, c = where_am_i()
    sibling = at(y, x, z, 1 - c)
    group = x * NC + c
    moved = NY - 1
    half = NZ // 2
    steps = half + 1
    n_group = NX * NC
    plane_up, plane_down = 2 * w_up.shape[-1] // 3, 2 * w_down.shape[-1] // 3
    cols = plane_up // 2
    quarter = BLK // NY

    def layer_of(j):
        return j + jnp.where(j >= y, 1, 0)

    def up_slice(l, xx):
        return w_up.at[l, z, xx // 2, :, pl.ds(pl.multiple_of((xx % 2) * cols, 128), cols)]

    def up_block(l, zo):
        return w_up.at[l, zo, :, :, pl.ds(0, plane_up)]

    def down_slice(l, zo):
        return w_down.at[l, zo, x, :, pl.ds(0, plane_down)]

    def down_block(l, xo):
        return w_down.at[l, :, xo, :, pl.ds(0, plane_down)]

    def y_part(l, core, h):
        if core == 0:
            width = (w_up.shape[-1] - plane_up) // 2
            return w_up.at[l, :, :, :, pl.ds(plane_up + h * width, width)]
        return w_down.at[l, pl.ds(h * half, half), :, :, pl.ds(plane_down, w_down.shape[-1] - plane_down)]

    def zz(offset):
        return lax.rem(z + offset + 2 * NZ, NZ)

    def xx(offset):
        return lax.rem(x + offset + NX, NX)

    def yy(offset):
        return lax.rem(y + offset + NY, NY)

    def gg(offset):
        return lax.rem(group + offset + n_group, n_group)

    def g_dev(g):
        return at(y, g // NC, z, g % NC)

    east, west = at(y, xx(1), z, c), at(y, xx(-1), z, c)
    north, south = at(yy(1), x, z, c), at(yy(-1), x, z, c)

    def tile_rows(ref, section):
        return ref.at[:, pl.ds(pl.multiple_of(section * quarter, quarter), quarter), :]

    loads = [
        pltpu.make_async_copy(up, w_up.at[y], local.at[0]),
        pltpu.make_async_copy(down, w_down.at[y], local.at[1]),
        pltpu.make_async_copy(cams.at[y], encoded, local.at[2]),
        pltpu.make_async_copy(tile_rows(tiles.at[x, :, c], y), tile_rows(tiles_all.at[group], y), local.at[3]),
        pltpu.make_async_copy(index, index_all.at[group], local.at[4]),
    ]
    for load in loads:
        load.start()
    greet(
        [at(yy(o), x, z, c) for o in range(1, NY)]
        + [g_dev(gg(o)) for o in range(1, n_group)]
        + [at(y, x, zz(1), c), at(y, x, zz(-1), c)]
    )
    for load in loads[:3]:
        load.wait()

    def share(l, core):
        return up_slice(l, x) if core == 0 else down_slice(l, z)

    for core in range(NC):
        @pl.when(c == core)
        def _(core=core):
            for o in range(1, NY):
                send(share(y, core), share(y, core), y_s.at[o - 1], y_r.at[o - 1], at(yy(o), x, z, c))
            for h, i, device in ((0, 0, north), (1, 3, south), (1, 1, north), (0, 2, south)):
                send(y_part(y, core, h), y_part(y, core, h), v_s.at[i], v_r.at[i], device)

    def sign(j, d):
        return (1 - 2 * (j % 2)) * (1 - 2 * d)

    def send_tiles():
        for o in range(1, n_group):
            g = gg(o)
            send(index, index_all.at[group], i_s.at[o - 1], i_r.at[o - 1], g_dev(g))
            send(
                tile_rows(tiles.at[g // NC, :, g % NC], y), tile_rows(tiles_all.at[group], y),
                t_s.at[o - 1], t_r.at[o - 1], g_dev(g),
            )

    @pl.when(c == 0)
    def _():
        @pl.loop(0, moved)
        def _(j):
            l = layer_of(j)
            o = yy(-l)
            arrived(share(l, 0), y_r.at[o - 1], sibling)
            for ox in range(1, NX):
                send(up_slice(l, x), up_slice(l, x), u_s.at[j, ox - 1], u_r.at[j, ox - 1], at(y, xx(ox), z, c))
        send_tiles()

    def z_hops(d):
        return half if d == 0 else half - 1

    @pl.when(c == 1)
    def _():
        send_tiles()

        @pl.loop(0, steps * moved)
        def _(n):
            k = n // moved + 1
            j = n % moved
            l = layer_of(j)
            o = yy(-l)

            @pl.when(k == 1)
            def _():
                arrived(share(l, 1), y_r.at[o - 1], sibling)

            for d in range(2):
                s = sign(j, d)
                block = down_slice(l, zz(-s * (k - 1)))

                @pl.when(jnp.logical_and(k >= 2, k <= z_hops(d) + 1))
                def _():
                    arrived(block, z_r.at[j, d, k - 2], sibling)

                @pl.when(k <= z_hops(d))
                def _():
                    send(block, block, z_s.at[j, d, k - 1], z_r.at[j, d, k - 1], at(y, x, zz(s), c))

    def layer_rows(l, r, rows):
        wide = encoded[pl.ds(r, rows), :].astype(F32)
        scaling = lax.rsqrt(jnp.mean(wide * wide, axis=-1, keepdims=True) + eps)
        normed = (wide * scaling).astype(BF)
        total = wide
        parts = 2
        for q in range(parts):
            width = w_up.shape[-1] // parts
            w1 = w_up[l, :, :, :, q * width : (q + 1) * width].reshape(wide.shape[1], width)
            hidden = gelu(jnp.dot(normed, w1, preferred_element_type=F32)).astype(BF)
            nz = NZ // parts
            w2 = w_down[l, q * nz : (q + 1) * nz].reshape(width, wide.shape[1])
            total = total + jnp.dot(hidden, w2, preferred_element_type=F32)
        encoded[pl.ds(r, rows), :] = total.astype(BF)

    tokens = encoded.shape[0]
    rows = tokens // 2

    def wait_sibling(j):
        l = layer_of(j)

        @pl.when(c == 0)
        def _():
            for i, ox in enumerate((0, 1, NX - 1, 2)):
                arrived(down_block(l, xx(-ox)), b_r.at[j, i], sibling)

        @pl.when(c == 1)
        def _():
            arrived(up_block(l, z), b_r.at[j, 0], sibling)
            for d in range(2):
                for k in range(2, z_hops(d) + 2):
                    arrived(up_block(l, zz(-sign(j, d) * (k - 1))), b_r.at[j, 1 + d * half + k - 2], sibling)

    def second_half(l, xo, h):
        return w_down.at[l, pl.ds(h * half, half), xo, :, pl.ds(0, plane_down)]

    def begin(j):
        l = layer_of(j)

        @pl.when(c == 0)
        def _():
            for ox in range(1, NX):
                arrived(up_slice(l, xx(-ox)), u_r.at[j, ox - 1], sibling)
            block = up_block(l, z)
            for d in range(2):
                if z_hops(d) >= 1:
                    send(block, block, z_s.at[j, d, 0], z_r.at[j, d, 0], at(y, x, zz(sign(j, d)), c))
            send(block, block, b_s.at[j, 0], b_r.at[j, 0], sibling)

        @pl.when(c == 1)
        def _():
            block = down_block(l, x)
            send(block, block, x_s.at[j, 0], x_r.at[j, 0], east)
            send(block, block, x_s.at[j, 1], x_r.at[j, 1], west)
            send(block, block, b_s.at[j, 0], b_r.at[j, 0], sibling)

    def own_rows(section):
        return tiles_all.at[:, :, pl.ds(pl.multiple_of(section * quarter, quarter), quarter), :]

    def some_rows(section, h):
        return tiles_all.at[
            pl.ds(h * n_group // 2, n_group // 2), :, pl.ds(pl.multiple_of(section * quarter, quarter), quarter), :
        ]

    t0 = n_group - 1

    def y_piece(i):
        return (yy(-1), yy(-1), yy(1), yy(1), yy(2), yy(2))[i], (0, 1, 0, 1, 0, 1)[i]

    def take_y(i):
        l, h = y_piece(i)
        for core in range(NC):
            @pl.when(c == core)
            def _(core=core):
                piece = y_part(l, core, h)
                arrived(piece, v_r.at[i], sibling)
                if i == 0:
                    send(piece, piece, v_s.at[4], v_r.at[4], north)
                if i == 3:
                    send(piece, piece, v_s.at[5], v_r.at[5], south)
                send(piece, piece, w_s.at[i], w_r.at[i], sibling)

    last = max(steps, 5)

    @pl.loop(1, 2 * (moved - 1) + last + 1)
    def _(slot):
        @pl.loop(0, moved)
        def _(j):
            k = slot - 2 * j
            l = layer_of(j)

            @pl.when(jnp.logical_and(c == 0, k >= 2))
            def _():
                for d in range(2):
                    s = sign(j, d)
                    block = up_block(l, zz(-s * (k - 1)))

                    @pl.when(k <= z_hops(d) + 1)
                    def _():
                        arrived(block, z_r.at[j, d, k - 2], sibling)

                        @pl.when(k <= z_hops(d))
                        def _():
                            send(block, block, z_s.at[j, d, k - 1], z_r.at[j, d, k - 1], at(y, x, zz(s), c))

                        send(block, block, b_s.at[j, 1 + d * half + k - 2], b_r.at[j, 1 + d * half + k - 2], sibling)

            @pl.when(jnp.logical_and(c == 1, k == 3))
            def _():
                block = down_block(l, xx(-1))
                arrived(block, x_r.at[j, 0], sibling)
                send(second_half(l, xx(-1), 0), second_half(l, xx(-1), 0), x_s.at[j, 2], x_r.at[j, 2], east)
                send(block, block, b_s.at[j, 1], b_r.at[j, 1], sibling)
                other = down_block(l, xx(1))
                arrived(other, x_r.at[j, 1], sibling)
                send(second_half(l, xx(1), 1), second_half(l, xx(1), 1), x_s.at[j, 3], x_r.at[j, 3], west)
                send(other, other, b_s.at[j, 2], b_r.at[j, 2], sibling)

            @pl.when(jnp.logical_and(c == 1, k == last))
            def _():
                arrived(second_half(l, xx(2), 0), x_r.at[j, 2], sibling)
                arrived(second_half(l, xx(2), 1), x_r.at[j, 3], sibling)
                block = down_block(l, xx(2))
                send(block, block, b_s.at[j, 3], b_r.at[j, 3], sibling)

            @pl.when(k == 1)
            def _():
                begin(j)

        for when, pieces in ((1, (0, 3)), (3, (1, 2)), (5, (4, 5))):
            @pl.when(slot == when)
            def _(pieces=pieces):
                for i in pieces:
                    take_y(i)

        @pl.when(slot == last + 1)
        def _():
            for load in loads[3:]:
                load.wait()
            for o in range(1, n_group):
                arrived(tile_rows(tiles_all.at[gg(-o)], y), t_r.at[o - 1], sibling)
            send(own_rows(y), own_rows(y), t_s.at[t0], t_r.at[t0], north)
            send(own_rows(y), own_rows(y), t_s.at[t0 + 1], t_r.at[t0 + 1], south)
            for i in range(6):
                l, h = y_piece(i)
                for core in range(NC):
                    @pl.when(c != core)
                    def _(core=core):
                        arrived(y_part(l, core, h), w_r.at[i], sibling)

        @pl.when(slot == last + 4)
        def _():
            arrived(own_rows(yy(-1)), t_r.at[t0], sibling)
            send(some_rows(yy(-1), 0), some_rows(yy(-1), 0), t_s.at[t0 + 2], t_r.at[t0 + 2], north)
            arrived(own_rows(yy(1)), t_r.at[t0 + 1], sibling)
            send(some_rows(yy(1), 1), some_rows(yy(1), 1), t_s.at[t0 + 3], t_r.at[t0 + 3], south)

        @pl.when(slot > last)
        def _():
            done = slot - last - 1

            @pl.when(done % 2 == 0)
            def _():
                wait_sibling(done // 2)

            layer_rows(done // 2, pl.multiple_of((done % 2) * rows, rows), rows)

    wait_sibling(moved - 1)

    @pl.loop(0, 3)
    def _(n):
        layer_rows(NY - 2 + n // 2, pl.multiple_of((n % 2) * rows, rows), rows)

    def half_of(g, h):
        return x_all.at[g, pl.ds(h * rows, rows), :]

    def project(h):
        mine = own.at[h * rows : (h + 1) * rows]
        mine[...] = jnp.dot(encoded[h * rows : (h + 1) * rows], proj[...], preferred_element_type=F32).astype(BF)
        send(mine, half_of(group, h), p_s.at[h], p_r.at[h], east)
        send(mine, half_of(group, h), p_s.at[2 + h], p_r.at[2 + h], west)
        send(mine, half_of(group, h), p_s.at[4 + h], p_r.at[4 + h], sibling)

    project(0)
    layer_rows(NY - 1, rows, rows)
    project(1)
    keep = pltpu.make_async_copy(own, x_all.at[group], local.at[5])
    keep.start()
    near, far = (xx(-1) * NC + c, xx(1) * NC + c), xx(2) * NC + c
    arrived(half_of(near[0], 0), p_r.at[0], sibling)
    send(half_of(near[0], 0), half_of(near[0], 0), p_s.at[6], p_r.at[6], east)
    arrived(half_of(near[1], 0), p_r.at[2], sibling)
    arrived(half_of(near[1], 1), p_r.at[3], sibling)
    send(half_of(near[1], 1), half_of(near[1], 1), p_s.at[7], p_r.at[7], west)
    send(x_all.at[near[1]], x_all.at[near[1]], p_s.at[9], p_r.at[9], sibling)
    arrived(half_of(near[0], 1), p_r.at[1], sibling)
    send(x_all.at[near[0]], x_all.at[near[0]], p_s.at[8], p_r.at[8], sibling)
    arrived(half_of(far, 0), p_r.at[6], sibling)
    arrived(half_of(far, 1), p_r.at[7], sibling)
    send(x_all.at[far], x_all.at[far], p_s.at[10], p_r.at[10], sibling)
    for h in range(2):
        arrived(half_of(x * NC + 1 - c, h), p_r.at[4 + h], sibling)
    for i, ox in enumerate((-1, 1, 2)):
        arrived(x_all.at[xx(ox) * NC + 1 - c], p_r.at[8 + i], sibling)

    keep.wait()
    arrived(some_rows(yy(2), 0), t_r.at[t0 + 2], sibling)
    arrived(some_rows(yy(2), 1), t_r.at[t0 + 3], sibling)
    for o in range(1, n_group):
        arrived(index_all.at[gg(-o)], i_r.at[o - 1], sibling)
        sent(tile_rows(tiles_all.at[group], y), t_s.at[o - 1], sibling)
        sent(index_all.at[group], i_s.at[o - 1], sibling)
    for i in range(2):
        sent(own_rows(y), t_s.at[t0 + i], sibling)
        sent(some_rows(y, 0), t_s.at[t0 + 2 + i], sibling)
    for i in range(8):
        sent(own.at[0:rows], p_s.at[i], sibling)
    for i in range(8, 11):
        sent(own, p_s.at[i], sibling)
    for core in range(NC):
        @pl.when(c == core)
        def _(core=core):
            for o in range(1, NY):
                sent(share(y, core), y_s.at[o - 1], sibling)
            for i in range(6):
                sent(y_part(y, core, 0), v_s.at[i], sibling)
                sent(y_part(y, core, 0), w_s.at[i], sibling)

    @pl.loop(0, moved)
    def _(j):
        @pl.when(c == 0)
        def _():
            for ox in range(1, NX):
                sent(up_slice(y, x), u_s.at[j, ox - 1], sibling)
            for d in range(2):
                for k in range(1, z_hops(d) + 1):
                    sent(up_block(y, z), z_s.at[j, d, k - 1], sibling)
            for i in range(NZ):
                sent(up_block(y, z), b_s.at[j, i], sibling)

        @pl.when(c == 1)
        def _():
            for i in range(2):
                sent(down_block(y, x), x_s.at[j, i], sibling)
                sent(second_half(y, x, 0), x_s.at[j, 2 + i], sibling)
            for d in range(2):
                for k in range(1, z_hops(d) + 1):
                    sent(down_slice(y, z), z_s.at[j, d, k - 1], sibling)
            for i in range(NX):
                sent(down_block(y, x), b_s.at[j, i], sibling)


def encode(up, down, cams, proj, tiles, index):
    d, f = up.shape[1:]
    tokens = cams.shape[1]
    channels = proj.shape[1]
    up = up.reshape(NZ, NX // 2, 2 * d // (NZ * NX), f)
    down = down.reshape(NZ, NX, f // (NZ * NX), d)
    tiles = tiles.reshape(NX, NZ, NC, BLK, BLK)
    n = NX * NC
    half = NZ // 2
    moved = NY - 1
    return pl.pallas_call(
        encoder_kernel,
        out_shape=(
            jax.ShapeDtypeStruct((tokens, d), BF),
            jax.ShapeDtypeStruct((n, tokens, channels), BF),
            jax.ShapeDtypeStruct((n, NZ, BLK, BLK), BF),
            jax.ShapeDtypeStruct((n,) + index.shape, jnp.int32),
        ),
        in_specs=[ANY, ANY, ANY, VM, ANY, ANY],
        out_specs=(VM, ANY, ANY, ANY),
        scratch_shapes=[
            pltpu.VMEM((NY,) + up.shape, BF),
            pltpu.VMEM((NY,) + down.shape, BF),
            pltpu.VMEM((tokens, channels), BF),
            DMA((NY - 1,)), DMA((NY - 1,)),
            DMA((moved, 4)), DMA((moved, 4)),
            DMA((moved, NX - 1)), DMA((moved, NX - 1)),
            DMA((moved, 2, half)), DMA((moved, 2, half)),
            DMA((moved, max(NZ, NX))), DMA((moved, max(NZ, NX))),
            DMA((n + 3,)), DMA((n + 3,)),
            DMA((n - 1,)), DMA((n - 1,)),
            DMA((11,)), DMA((11,)),
            DMA((6,)), DMA((6,)),
            DMA((6,)), DMA((6,)),
            DMA((6,)),
        ],
        compiler_params=pltpu.CompilerParams(
            collective_id=0, has_side_effects=True, vmem_limit_bytes=VMEM_LIMIT
        ),
    )(up, down, cams, proj, tiles, index)


def join_kernel(index, x_all, tiles, grid_out, left, right, parts, s_buf, r_buf, s_sem, r_sem):
    y, x, z, c = where_am_i()
    half = NZ // 2
    n_group = NX * NC
    bev = grid_out.shape[0] // BLK
    chunk = grid_out.shape[0] // 2

    def zz(offset):
        return lax.rem(z + offset + 2 * NZ, NZ)

    beside = (at(y, x, zz(1), c), at(y, x, zz(-1), c))
    greet(beside)

    def hops(ch, d):
        return half if ch == d else half - 1

    def push(ch, d, k):
        send(s_buf.at[ch, d, k - 1], r_buf.at[ch, d, k - 1], s_sem.at[ch, d, k - 1], r_sem.at[ch, d, k - 1], beside[d])

    @pl.loop(0, NZ)
    def _(i):
        off = jnp.where(i == 0, half, jnp.where(i % 2 == 1, (NZ - 1 - i) // 2, -((NZ - i) // 2)))
        target = zz(off)
        p = (x * NZ + target) * NC + c
        for g in range(n_group):
            tile = tiles[g, target].astype(F32)
            dst = index[g, 1, p]
            alive = index[g, 2, p]
            for b in range(bev):
                weight = jnp.where(dst == b, alive, 0).astype(F32)
                left[b * BLK : (b + 1) * BLK, g * BLK : (g + 1) * BLK] = (tile * weight).astype(BF)
            right[g * BLK : (g + 1) * BLK, :] = x_all[g, index[g, 0, p]]
        parts[i] = jnp.dot(left[...], right[...], preferred_element_type=F32)

        @pl.when(i == 0)
        def _():
            for d in range(2):
                s_buf[d, d, 0] = parts[0, d * chunk : (d + 1) * chunk].astype(BF)
                push(d, d, 1)

        for d in range(2):
            if half == 1:
                continue

            @pl.when(i == 1 + d)
            def _(d=d):
                ch = 1 - d
                s_buf[ch, d, 0] = parts[1 + d, ch * chunk : (ch + 1) * chunk].astype(BF)
                push(ch, d, 1)

    for o in range(half - 1, 0, -1):
        for ch_is_d in (True, False):
            for d in range(2):
                ch = d if ch_is_d else 1 - d
                k = hops(ch, d) - o + 1
                if k == 1:
                    continue
                arrived(r_buf.at[ch, d, k - 2], r_sem.at[ch, d, k - 2], beside[d])
                i = NZ - 1 - 2 * o if d == 0 else NZ - 2 * o
                total = parts[i, ch * chunk : (ch + 1) * chunk] + r_buf[ch, d, k - 2].astype(F32)
                s_buf[ch, d, k - 1] = total.astype(BF)
                push(ch, d, k)
    for ch in range(2):
        total = parts[NZ - 1, ch * chunk : (ch + 1) * chunk]
        for d in range(2):
            k = hops(ch, d)
            if k == 0:
                continue
            arrived(r_buf.at[ch, d, k - 1], r_sem.at[ch, d, k - 1], beside[d])
            total = total + r_buf[ch, d, k - 1].astype(F32)
        grid_out[ch * chunk : (ch + 1) * chunk] = total
    for ch in range(2):
        for d in range(2):
            for k in range(hops(ch, d)):
                sent(s_buf.at[ch, d, k], s_sem.at[ch, d, k], beside[d])


def join(index_all, x_all, tiles_all, cells):
    channels = x_all.shape[-1]
    x_all = x_all.reshape(x_all.shape[0], -1, BLK, channels)
    n = NX * NC
    half = NZ // 2
    return pl.pallas_call(
        join_kernel,
        out_shape=jax.ShapeDtypeStruct((cells, channels), F32),
        in_specs=[SM, VM, VM],
        out_specs=VM,
        scratch_shapes=[
            pltpu.VMEM((cells, n * BLK), BF),
            pltpu.VMEM((n * BLK, channels), BF),
            pltpu.VMEM((NZ, cells, channels), F32),
            pltpu.VMEM((2, 2, half, cells // 2, channels), BF),
            pltpu.VMEM((2, 2, half, cells // 2, channels), BF),
            DMA((2, 2, half)), DMA((2, 2, half)),
        ],
        compiler_params=pltpu.CompilerParams(
            collective_id=1, has_side_effects=True, vmem_limit_bytes=VMEM_LIMIT
        ),
    )(index_all, x_all, tiles_all)


class Total:
    n1, n2, width = NX * NY, NZ, 128

    def __init__(self, ins, outs, scratch):
        self.ins, self.outs = ins, outs
        (
            self.packed, self.from0, self.half, self.from1, self.mid, self.from2, self.mine, self.gathered, self.result,
            self.s0, self.r0, self.s1, self.r1, self.s2, self.r2, self.s3, self.r3, self.s4, self.r4, self.s5, self.r5,
        ) = scratch
        y, x, z, c = where_am_i()
        self.y, self.x, self.z, self.c = y, x, z, c
        self.one, self.two = y * NX + x, z
        self.sibling = at(y, x, z, 1 - c)
        self.real = self.half.shape[1]
        self.share = self.mine.shape[0]

    @classmethod
    def scratch_for(cls, shapes):
        n1, n2, width = NX * NY, NZ, cls.width
        real = sum(a * b for a, b in shapes) // (n1 * NC * width)
        share = -(-real // (n2 * 16)) * 16
        buffers = [
            (NC, n1, real, width), (n1, real, width), (n1, real, width), (n1 - 1, real, width), (share * n2, width),
            (n2 - 1, share, width), (share, width), (share * n2, width), (NC, n1, real, width),
        ]
        counts = [1, n1 - 1, n2 - 1, n2 - 1, n1 - 1, 1]
        return [pltpu.VMEM(b, BF) for b in buffers] + [DMA((n,)) for n in counts for _ in range(2)]

    def dev1(self, q):
        return at(q // NX, q % NX, self.z, self.c)

    def dev2(self, e):
        return at(self.y, self.x, e, self.c)

    def q1(self, o):
        n1 = NX * NY
        return lax.rem(self.one + o + n1, n1)

    def q2(self, o):
        return lax.rem(self.two + o + NZ, NZ)

    def peers(self):
        n1 = NX * NY
        return [self.sibling] + [self.dev1(self.q1(o)) for o in range(1, n1)] + [self.dev2(self.q2(o)) for o in range(1, NZ)]

    def pieces(self):
        row = 0
        for i, ref in enumerate(self.ins):
            height = ref.shape[0] // (NX * NY)
            for col in range(ref.shape[1] // (NC * self.width)):
                yield i, row, height, col * NC * self.width
                row += height

    def start(self):
        n1 = NX * NY

        @pl.loop(0, n1)
        def _(q):
            for i, row, height, col in self.pieces():
                for core in range(NC):
                    left = col + core * self.width
                    self.packed[core, q, row : row + height, :] = self.ins[i][
                        pl.ds(pl.multiple_of(q * height, height), height), left : left + self.width
                    ].astype(BF)
        send(self.packed.at[1 - self.c], self.from0, self.s0.at[0], self.r0.at[0], self.sibling)
        self.mid[...] = jnp.zeros_like(self.mid)

    def over_xy(self):
        n1 = NX * NY
        arrived(self.from0, self.r0.at[0], self.sibling)

        @pl.loop(0, n1)
        def _(o):
            q = lax.rem(self.one + 1 + o, n1)
            self.half[q] = (self.packed[self.c, q].astype(F32) + self.from0[q].astype(F32)).astype(BF)

            @pl.when(o < n1 - 1)
            def _():
                send(self.half.at[q], self.from1.at[o], self.s1.at[o], self.r1.at[o], self.dev1(q))

    def part(self, ref, e):
        return ref.at[pl.ds(pl.multiple_of(e * self.share, self.share), self.share), :]

    def over_z(self):
        total = self.half[self.one].astype(F32)
        for o in range(NX * NY - 1):
            arrived(self.from1.at[o], self.r1.at[o], self.sibling)
            total = total + self.from1[o].astype(F32)
        self.mid[0 : self.real, :] = total.astype(BF)
        for o in range(1, NZ):
            e = self.q2(o)
            send(self.part(self.mid, e), self.from2.at[o - 1], self.s2.at[o - 1], self.r2.at[o - 1], self.dev2(e))

    def back_over_z(self):
        total = self.mid[pl.ds(pl.multiple_of(self.two * self.share, self.share), self.share), :].astype(F32)
        for o in range(1, NZ):
            arrived(self.from2.at[o - 1], self.r2.at[o - 1], self.sibling)
            total = total + self.from2[o - 1].astype(F32)
        self.mine[...] = total.astype(BF)
        for o in range(1, NZ):
            send(self.mine, self.part(self.gathered, self.two), self.s3.at[o - 1], self.r3.at[o - 1], self.dev2(self.q2(o)))
        self.gathered[pl.ds(pl.multiple_of(self.two * self.share, self.share), self.share), :] = self.mine[...]

    def back_over_xy(self):
        for o in range(1, NZ):
            arrived(self.part(self.gathered, self.q2(-o)), self.r3.at[o - 1], self.sibling)
        for o in range(1, NX * NY):
            send(
                self.gathered.at[0 : self.real, :], self.result.at[self.c, self.one],
                self.s4.at[o - 1], self.r4.at[o - 1], self.dev1(self.q1(o)),
            )
        self.result[self.c, self.one] = self.gathered[0 : self.real, :]

    def back_over_core(self):
        for o in range(1, NX * NY):
            arrived(self.result.at[self.c, self.q1(-o)], self.r4.at[o - 1], self.sibling)
        send(self.result.at[self.c], self.result.at[self.c], self.s5.at[0], self.r5.at[0], self.sibling)

    def finish(self):
        n1 = NX * NY
        arrived(self.result.at[1 - self.c], self.r5.at[0], self.sibling)

        @pl.loop(0, n1)
        def _(q):
            for i, row, height, col in self.pieces():
                for core in range(NC):
                    left = col + core * self.width
                    self.outs[i][pl.ds(pl.multiple_of(q * height, height), height), left : left + self.width] = self.result[
                        core, q, row : row + height, :
                    ].astype(F32)

        sent(self.from0, self.s0.at[0], self.sibling)
        sent(self.result.at[self.c], self.s5.at[0], self.sibling)
        for o in range(n1 - 1):
            sent(self.half.at[0], self.s1.at[o], self.sibling)
            sent(self.half.at[0], self.s4.at[o], self.sibling)
        for o in range(NZ - 1):
            sent(self.mine, self.s2.at[o], self.sibling)
            sent(self.mine, self.s3.at[o], self.sibling)


def total_kernel(value, out, *scratch):
    total = Total([value], [out], scratch)
    greet(total.peers())
    total.start()
    total.over_xy()
    total.over_z()
    total.back_over_z()
    total.back_over_xy()
    total.back_over_core()
    total.finish()


def total_over_devices(value):
    return pl.pallas_call(
        total_kernel,
        out_shape=jax.ShapeDtypeStruct(value.shape, F32),
        in_specs=[VM],
        out_specs=VM,
        scratch_shapes=Total.scratch_for([value.shape]),
        compiler_params=pltpu.CompilerParams(
            collective_id=3, has_side_effects=True, vmem_limit_bytes=VMEM_LIMIT
        ),
    )(value)


N_GRADS = 4


def gelu_parts(v):
    inner = math.sqrt(2.0 / math.pi) * (v + 0.044715 * v * v * v)
    slope = math.sqrt(2.0 / math.pi) * (1.0 + 3.0 * 0.044715 * v * v)
    t = jnp.tanh(inner)
    return 0.5 * v * (1.0 + t), 0.5 * (1.0 + t) + 0.5 * v * (1.0 - t * t) * slope


def split_kernel(index, grid, pred_grad, tiles, ru, rd, du, dd, *refs, scale):
    rows_out, prediction, outs, refs = refs[0], refs[1], refs[2 : 2 + N_GRADS], refs[2 + N_GRADS :]
    all_grad, here, left, acc, core_s, core_r, x_send, x_recv, z_s, z_r, c_s, c_r, x_s, x_r = refs[:14]
    kept = refs[14:22]
    ins = refs[22 : 22 + N_GRADS]
    total = Total(ins, outs, refs[22 + N_GRADS :])
    grad = pred_grad
    y, x, z, c = where_am_i()
    half = NZ // 2
    n_group = NX * NC
    chunk = grad.shape[0] // 2
    cam = rows_out.shape[0] // BLK
    sibling = at(y, x, z, 1 - c)

    def zz(offset):
        return lax.rem(z + offset + 2 * NZ, NZ)

    def xx(offset):
        return lax.rem(x + offset + NX, NX)

    beside = (at(y, x, zz(1), c), at(y, x, zz(-1), c))
    east, west = at(y, xx(1), z, c), at(y, xx(-1), z, c)
    barrier = pltpu.get_barrier_semaphore()
    for device in total.peers():
        pl.semaphore_signal(barrier, inc=1, device_id=device, device_id_type=MESH)

    def hops(ch, d):
        return half if ch == d else half - 1

    def part(origin, ch):
        return all_grad.at[origin, pl.ds(ch * chunk, chunk)]

    n1_ref, h1_ref, n2_ref, h2_ref, p1_ref, p2_ref, r1_ref, r2_ref = kept

    def heads(ch):
        r = slice(ch * chunk, (ch + 1) * chunk)

        def forward(state, w_up, w_down, n_ref, h_ref):
            scaling = lax.rsqrt(jnp.mean(state * state, axis=-1, keepdims=True) + eps)
            normed = (state * scaling).astype(BF)
            n_ref[r] = normed
            preact = jnp.dot(normed, w_up[...], preferred_element_type=F32)
            value, slope = gelu_parts(preact)
            hidden = value.astype(BF)
            h_ref[r] = hidden
            return state + jnp.dot(hidden, w_down[...], preferred_element_type=F32), scaling, slope

        def backward(g, state, scaling, slope, w_up, w_down, p_ref, r_ref):
            rounded = g.astype(BF)
            r_ref[r] = rounded
            grad_pre = (against_rows(rounded, w_down[...]) * slope).astype(BF)
            p_ref[r] = grad_pre
            grad_normed = against_rows(grad_pre, w_up[...])
            unit = state * scaling
            return g + scaling * (grad_normed - unit * jnp.mean(grad_normed * unit, axis=-1, keepdims=True))

        s0 = grid[r]
        s1, scale1, slope1 = forward(s0, ru, rd, n1_ref, h1_ref)
        s2, scale2, slope2 = forward(s1, du, dd, n2_ref, h2_ref)
        prediction[r] = s2.astype(BF)
        g1 = backward(pred_grad[r].astype(F32) * scale, s1, scale2, slope2, du, dd, p2_ref, r2_ref)
        g0 = backward(g1, s0, scale1, slope1, ru, rd, p1_ref, r1_ref)
        all_grad[z, r] = g0.astype(BF)

    for ch in range(2):
        heads(ch)
        if ch == 0:
            pl.semaphore_wait(barrier, len(total.peers()))
        for d in range(2):
            if hops(ch, d) >= 1:
                send(part(z, ch), part(z, ch), z_s.at[ch, d, 0], z_r.at[ch, d, 0], beside[d])
    ins[0][...] = contract_rows(n1_ref[...], p1_ref[...])
    ins[1][...] = contract_rows(h1_ref[...], r1_ref[...])
    ins[2][...] = contract_rows(n2_ref[...], p2_ref[...])
    ins[3][...] = contract_rows(h2_ref[...], r2_ref[...])
    total.start()

    def use(origin, first):
        p = (x * NZ + origin) * NC + c
        here[...] = all_grad[origin].reshape(here.shape)
        for g in range(n_group):
            tile = tiles[g, origin].astype(F32).T
            src = index[g, 0, p]
            alive = index[g, 2, p]
            for k in range(cam):
                weight = jnp.where(src == k, alive, 0).astype(F32)
                left[k * BLK : (k + 1) * BLK, :] = (tile * weight).astype(BF)
            product = jnp.dot(left[...], here[index[g, 1, p]], preferred_element_type=F32)
            if first:
                acc[g] = product
            else:
                acc[g] = acc[g] + product

    use(z, True)
    total.over_xy()

    @pl.loop(1, half + 1)
    def _(k):
        for d in range(2):
            s = 1 - 2 * d
            origin = zz(-s * k)
            for ch in range(2):
                @pl.when(k <= hops(ch, d))
                def _(ch=ch, d=d):
                    arrived(part(origin, ch), z_r.at[ch, d, k - 1], beside[d])

                @pl.when(k + 1 <= hops(ch, d))
                def _(ch=ch, d=d):
                    send(part(origin, ch), part(origin, ch), z_s.at[ch, d, k], z_r.at[ch, d, k], beside[d])

        @pl.when(k == max(half - 2, 1))
        def _():
            total.over_z()

        @pl.when(k == max(half - 1, 1))
        def _():
            total.back_over_z()

        @pl.when(k == half)
        def _():
            total.back_over_xy()

        use(zz(-k), False)

        @pl.when(k < half)
        def _():
            use(zz(k), False)

    rows = rows_out.shape[0] // 2
    order = (2, 1, NX - 1, 0)
    for i, o in enumerate(order):
        core_s[i] = acc[xx(o) * NC + 1 - c].astype(BF)
        send(core_s.at[i], core_r.at[i], c_s.at[i], c_r.at[i], sibling)

    def pair_sum(i, h):
        return acc[xx(order[i]) * NC + c, h * rows : (h + 1) * rows, :] + core_r[
            i, h * rows : (h + 1) * rows, :
        ].astype(F32)

    def push(n, value, device):
        x_send[n] = value.astype(BF)
        send(x_send.at[n], x_recv.at[n], x_s.at[n], x_r.at[n], device)

    for i in range(3):
        arrived(core_r.at[i], c_r.at[i], sibling)
        if i == 0:
            push(0, pair_sum(0, 0), east)
            push(1, pair_sum(0, 1), west)
        if i == 1:
            push(2, pair_sum(1, 1), east)
        if i == 2:
            push(3, pair_sum(2, 0), west)
    arrived(x_recv.at[0], x_r.at[0], sibling)
    push(4, pair_sum(1, 0) + x_recv[0].astype(F32), east)
    arrived(x_recv.at[1], x_r.at[1], sibling)
    push(5, pair_sum(2, 1) + x_recv[1].astype(F32), west)
    arrived(core_r.at[3], c_r.at[3], sibling)
    total.back_over_core()
    for n in range(2, 6):
        arrived(x_recv.at[n], x_r.at[n], sibling)
    rows_out[0:rows] = (pair_sum(3, 0) + x_recv[4].astype(F32) + x_recv[3].astype(F32)).astype(BF)
    rows_out[rows : 2 * rows] = (pair_sum(3, 1) + x_recv[2].astype(F32) + x_recv[5].astype(F32)).astype(BF)
    total.finish()
    for i in range(4):
        sent(core_s.at[i], c_s.at[i], sibling)
    for n in range(6):
        sent(x_send.at[n], x_s.at[n], sibling)
    for ch in range(2):
        for d in range(2):
            for k in range(hops(ch, d)):
                sent(part(z, ch), z_s.at[ch, d, k], beside[d])


def split(index_all, grid, pred_grad, tiles_all, tokens, weights, scale):
    cells, channels = grid.shape
    hidden = weights[0].shape[1]
    n = NX * NC
    half = NZ // 2
    shapes = [w.shape for w in weights]
    return pl.pallas_call(
        functools.partial(split_kernel, scale=scale),
        out_shape=(
            jax.ShapeDtypeStruct((tokens, channels), BF),
            jax.ShapeDtypeStruct((cells, channels), BF),
        ) + tuple(jax.ShapeDtypeStruct(a, F32) for a in shapes),
        in_specs=[SM, VM, VM, VM] + [VM] * N_GRADS,
        out_specs=tuple([VM] * (2 + N_GRADS)),
        scratch_shapes=[
            pltpu.VMEM((NZ, cells, channels), BF),
            pltpu.VMEM((cells // BLK, BLK, channels), BF),
            pltpu.VMEM((tokens, BLK), BF),
            pltpu.VMEM((n, tokens, channels), F32),
            pltpu.VMEM((NX, tokens, channels), BF),
            pltpu.VMEM((NX, tokens, channels), BF),
            pltpu.VMEM((6, tokens // 2, channels), BF),
            pltpu.VMEM((6, tokens // 2, channels), BF),
            DMA((2, 2, half)), DMA((2, 2, half)),
            DMA((NX,)), DMA((NX,)),
            DMA((6,)), DMA((6,)),
        ]
        + [pltpu.VMEM((cells, w), BF) for w in (channels, hidden) * 2 + (hidden, hidden, channels, channels)]
        + [pltpu.VMEM(a, F32) for a in shapes]
        + Total.scratch_for(shapes),
        compiler_params=pltpu.CompilerParams(
            collective_id=2, has_side_effects=True, vmem_limit_bytes=VMEM_LIMIT
        ),
    )(index_all, grid, pred_grad, tiles_all, *weights)


def on_device(
    cams, vit_up, vit_down, proj, frustum_tiles, src_block, dst_block, live,
    render_up, render_down, decode_up, decode_down, pred_grad,
):
    tile_count = NX * NZ * NC
    cells, channels = pred_grad.shape[1:]
    index = jnp.zeros((8, 128), jnp.int32)
    index = lax.dynamic_update_slice(index, jnp.concatenate([src_block, dst_block, live], axis=0), (0, 0))
    encoded, x_all, tiles_all, index_all = encode(vit_up, vit_down, cams, proj, frustum_tiles[0], index)
    bev_grid = join(index_all, x_all, tiles_all, cells)
    scale = 1.0 / math.sqrt(cams.shape[0] * cells * tile_count)
    weights = (render_up, render_down, decode_up, decode_down)
    grad_rows, prediction, *totals = split(
        index_all, bev_grid, pred_grad[0], tiles_all, cams.shape[1], weights, scale
    )
    grad_proj = total_over_devices(contract_rows(encoded, grad_rows))
    return (prediction[None], grad_proj, *totals)


def solution(mesh):
    placed = (
        P(None, "tile", None),
        P("section", None, None),
        P("section", None, None),
        P(),
        P("tile", None, None, None),
        P("tile", None),
        P("tile", None),
        P("tile", None),
        P(),
        P(),
        P(),
        P(),
        P("section", "tile", None),
    )
    return jax.shard_map(
        on_device,
        mesh=mesh,
        in_specs=placed,
        out_specs=(P("section", "tile", None), P(), P(), P(), P(), P()),
        check_vma=False,
    )
```

```python
import functools
import math

import jax
import jax.numpy as jnp
from jax import lax
from jax.experimental import pallas as pl
from jax.experimental.pallas import tpu as pltpu
from jax.sharding import PartitionSpec as P

eps = 1e-05
MESH = pl.DeviceIdType.MESH
BF = jnp.bfloat16
F32 = jnp.float32
NY, NX, NZ, NC = 4, 4, 8, 2
BLK = 128
VMEM_LIMIT = 60 * 2**20
ANY = pl.BlockSpec(memory_space=pl.ANY)
VM = pl.BlockSpec(memory_space=pltpu.VMEM)
SM = pl.BlockSpec(memory_space=pltpu.SMEM)
DMA = pltpu.SemaphoreType.DMA


def where_am_i():
    y = lax.axis_index("section")
    t = lax.axis_index("tile")
    return y, t // (NZ * NC), (t // NC) % NZ, t % NC


def at(y, x, z, c):
    return (y, (x * NZ + z) * NC + c)


def send(src, dst, ssem, rsem, device):
    copy = pltpu.make_async_remote_copy(
        src_ref=src, dst_ref=dst, send_sem=ssem, recv_sem=rsem, device_id=device, device_id_type=MESH
    )
    copy.start()


def sent(src, ssem, device):
    pltpu.make_async_remote_copy(
        src_ref=src, dst_ref=src, send_sem=ssem, recv_sem=ssem, device_id=device, device_id_type=MESH
    ).wait_send()


def arrived(dst, rsem, device):
    pltpu.make_async_remote_copy(
        src_ref=dst, dst_ref=dst, send_sem=rsem, recv_sem=rsem, device_id=device, device_id_type=MESH
    ).wait_recv()


def greet(devices):
    barrier = pltpu.get_barrier_semaphore()
    for device in devices:
        pl.semaphore_signal(barrier, inc=1, device_id=device, device_id_type=MESH)
    pl.semaphore_wait(barrier, len(devices))


def gelu(v):
    return 0.5 * v * (1.0 + jnp.tanh(math.sqrt(2.0 / math.pi) * (v + 0.044715 * v * v * v)))


def contract_rows(left, right):
    return lax.dot_general(left, right, (((0,), (0,)), ((), ())), preferred_element_type=F32)


def against_rows(left, right):
    return lax.dot_general(left, right, (((1,), (1,)), ((), ())), preferred_element_type=F32)


def encoder_kernel(
    up, down, cams, proj, tiles, index,
    encoded, x_all, tiles_all, index_all,
    w_up, w_down, own, y_s, y_r, x_s, x_r, u_s, u_r, z_s, z_r, b_s, b_r, t_s, t_r, i_s, i_r, p_s, p_r, v_s, v_r, w_s, w_r,
    local,
):
    y, x, z, c = where_am_i()
    sibling = at(y, x, z, 1 - c)
    group = x * NC + c
    moved = NY - 1
    half = NZ // 2
    steps = half + 1
    n_group = NX * NC
    plane_up, plane_down = 2 * w_up.shape[-1] // 3, 2 * w_down.shape[-1] // 3
    cols = plane_up // 2
    quarter = BLK // NY

    def layer_of(j):
        return j + jnp.where(j >= y, 1, 0)

    def up_slice(l, xx):
        return w_up.at[l, z, xx // 2, :, pl.ds(pl.multiple_of((xx % 2) * cols, 128), cols)]

    def up_block(l, zo):
        return w_up.at[l, zo, :, :, pl.ds(0, plane_up)]

    def down_slice(l, zo):
        return w_down.at[l, zo, x, :, pl.ds(0, plane_down)]

    def down_block(l, xo):
        return w_down.at[l, :, xo, :, pl.ds(0, plane_down)]

    def y_part(l, core, h):
        if core == 0:
            width = (w_up.shape[-1] - plane_up) // 2
            return w_up.at[l, :, :, :, pl.ds(plane_up + h * width, width)]
        return w_down.at[l, pl.ds(h * half, half), :, :, pl.ds(plane_down, w_down.shape[-1] - plane_down)]

    def zz(offset):
        return lax.rem(z + offset + 2 * NZ, NZ)

    def xx(offset):
        return lax.rem(x + offset + NX, NX)

    def yy(offset):
        return lax.rem(y + offset + NY, NY)

    def gg(offset):
        return lax.rem(group + offset + n_group, n_group)

    def g_dev(g):
        return at(y, g // NC, z, g % NC)

    east, west = at(y, xx(1), z, c), at(y, xx(-1), z, c)
    north, south = at(yy(1), x, z, c), at(yy(-1), x, z, c)

    def tile_rows(ref, section):
        return ref.at[:, pl.ds(pl.multiple_of(section * quarter, quarter), quarter), :]

    loads = [
        pltpu.make_async_copy(up, w_up.at[y], local.at[0]),
        pltpu.make_async_copy(down, w_down.at[y], local.at[1]),
        pltpu.make_async_copy(cams.at[y], encoded, local.at[2]),
        pltpu.make_async_copy(tile_rows(tiles.at[x, :, c], y), tile_rows(tiles_all.at[group], y), local.at[3]),
        pltpu.make_async_copy(index, index_all.at[group], local.at[4]),
    ]
    for load in loads:
        load.start()
    greet(
        [at(yy(o), x, z, c) for o in range(1, NY)]
        + [g_dev(gg(o)) for o in range(1, n_group)]
        + [at(y, x, zz(o), c) for o in ((1, -1, 2, -2) if NZ == 8 else (1, -1))]
    )
    for load in loads[:3]:
        load.wait()

    def share(l, core):
        return up_slice(l, x) if core == 0 else down_slice(l, z)

    for core in range(NC):
        @pl.when(c == core)
        def _(core=core):
            for o in range(1, NY):
                send(share(y, core), share(y, core), y_s.at[o - 1], y_r.at[o - 1], at(yy(o), x, z, c))
            for h, i, device in ((0, 0, north), (1, 3, south), (1, 1, north), (0, 2, south)):
                send(y_part(y, core, h), y_part(y, core, h), v_s.at[i], v_r.at[i], device)

    def sign(j, d):
        return (1 - 2 * (j % 2)) * (1 - 2 * d)

    def send_tiles():
        for o in range(1, n_group):
            g = gg(o)
            send(index, index_all.at[group], i_s.at[o - 1], i_r.at[o - 1], g_dev(g))
            send(
                tile_rows(tiles.at[g // NC, :, g % NC], y), tile_rows(tiles_all.at[group], y),
                t_s.at[o - 1], t_r.at[o - 1], g_dev(g),
            )

    first_hops = (1, -1, 2, -2) if NZ == 8 else tuple(range(1, NZ))
    later_hops = ((4, 1, 2), (5, 2, 2), (6, -1, -2)) if NZ == 8 else ()

    def sem_of(sems, j, i):
        return sems.at[j, i // half, i % half]

    def slice_to(j, l, i, off, origin):
        s = sign(j, 0)
        block = down_slice(l, zz(-s * origin))
        send(block, block, sem_of(z_s, j, i), sem_of(z_r, j, i), at(y, x, zz(s * off), c))

    def slices_arrived(j, l):
        s = sign(j, 0)
        for i, off in enumerate(first_hops):
            if off not in [origin for _, _, origin in later_hops]:
                arrived(down_slice(l, zz(-s * off)), sem_of(z_r, j, i), sibling)
        for i, off, origin in later_hops:
            arrived(down_slice(l, zz(-s * (off + origin))), sem_of(z_r, j, i), sibling)

    @pl.when(c == 0)
    def _():
        @pl.loop(0, moved)
        def _(j):
            l = layer_of(j)
            o = yy(-l)
            arrived(share(l, 0), y_r.at[o - 1], sibling)
            for ox in range(1, NX):
                send(up_slice(l, x), up_slice(l, x), u_s.at[j, ox - 1], u_r.at[j, ox - 1], at(y, xx(ox), z, c))
        send_tiles()

    def z_hops(d):
        return half if d == 0 else half - 1

    @pl.when(c == 1)
    def _():
        @pl.loop(0, moved)
        def _(j):
            l = layer_of(j)
            arrived(share(l, 1), y_r.at[yy(-l) - 1], sibling)
            for i, off in enumerate(first_hops):
                slice_to(j, l, i, off, 0)
        send_tiles()

        @pl.loop(0, moved)
        def _(j):
            l = layer_of(j)
            for i, off, origin in later_hops:
                if i != 5:
                    first = first_hops.index(origin)
                    arrived(down_slice(l, zz(-sign(j, 0) * origin)), sem_of(z_r, j, first), sibling)
                slice_to(j, l, i, off, origin)

    def layer_rows(l, r, rows):
        wide = encoded[pl.ds(r, rows), :].astype(F32)
        scaling = lax.rsqrt(jnp.mean(wide * wide, axis=-1, keepdims=True) + eps)
        normed = (wide * scaling).astype(BF)
        total = wide
        parts = 2
        for q in range(parts):
            width = w_up.shape[-1] // parts
            w1 = w_up[l, :, :, :, q * width : (q + 1) * width].reshape(wide.shape[1], width)
            hidden = gelu(jnp.dot(normed, w1, preferred_element_type=F32)).astype(BF)
            nz = NZ // parts
            w2 = w_down[l, q * nz : (q + 1) * nz].reshape(width, wide.shape[1])
            total = total + jnp.dot(hidden, w2, preferred_element_type=F32)
        encoded[pl.ds(r, rows), :] = total.astype(BF)

    tokens = encoded.shape[0]
    rows = tokens // 2

    def wait_sibling(j):
        l = layer_of(j)

        @pl.when(c == 0)
        def _():
            for i, ox in enumerate((0, 1, NX - 1, 2)):
                arrived(down_block(l, xx(-ox)), b_r.at[j, i], sibling)

        @pl.when(c == 1)
        def _():
            arrived(up_block(l, z), b_r.at[j, 0], sibling)
            for d in range(2):
                for k in range(2, z_hops(d) + 2):
                    arrived(up_block(l, zz(-sign(j, d) * (k - 1))), b_r.at[j, 1 + d * half + k - 2], sibling)

    def second_half(l, xo, h):
        return w_down.at[l, pl.ds(h * half, half), xo, :, pl.ds(0, plane_down)]

    def begin(j):
        l = layer_of(j)

        @pl.when(c == 0)
        def _():
            for ox in range(1, NX):
                arrived(up_slice(l, xx(-ox)), u_r.at[j, ox - 1], sibling)
            block = up_block(l, z)
            for d in range(2):
                if z_hops(d) >= 1:
                    send(block, block, z_s.at[j, d, 0], z_r.at[j, d, 0], at(y, x, zz(sign(j, d)), c))
            send(block, block, b_s.at[j, 0], b_r.at[j, 0], sibling)

        @pl.when(c == 1)
        def _():
            slices_arrived(j, l)
            block = down_block(l, x)
            send(block, block, x_s.at[j, 0], x_r.at[j, 0], east)
            send(block, block, x_s.at[j, 1], x_r.at[j, 1], west)
            send(block, block, b_s.at[j, 0], b_r.at[j, 0], sibling)

    def own_rows(section):
        return tiles_all.at[:, :, pl.ds(pl.multiple_of(section * quarter, quarter), quarter), :]

    def some_rows(section, h):
        return tiles_all.at[
            pl.ds(h * n_group // 2, n_group // 2), :, pl.ds(pl.multiple_of(section * quarter, quarter), quarter), :
        ]

    t0 = n_group - 1

    def y_piece(i):
        return (yy(-1), yy(-1), yy(1), yy(1), yy(2), yy(2))[i], (0, 1, 0, 1, 0, 1)[i]

    def take_y(i):
        l, h = y_piece(i)
        for core in range(NC):
            @pl.when(c == core)
            def _(core=core):
                piece = y_part(l, core, h)
                arrived(piece, v_r.at[i], sibling)
                if i == 0:
                    send(piece, piece, v_s.at[4], v_r.at[4], north)
                if i == 3:
                    send(piece, piece, v_s.at[5], v_r.at[5], south)
                send(piece, piece, w_s.at[i], w_r.at[i], sibling)

    last = max(steps, 5)

    @pl.loop(1, moved - 1 + last + 1)
    def _(slot):
        @pl.loop(0, moved)
        def _(j):
            k = slot - j
            l = layer_of(j)

            @pl.when(jnp.logical_and(c == 0, k >= 2))
            def _():
                for d in range(2):
                    s = sign(j, d)
                    block = up_block(l, zz(-s * (k - 1)))

                    @pl.when(k <= z_hops(d) + 1)
                    def _():
                        arrived(block, z_r.at[j, d, k - 2], sibling)

                        @pl.when(k <= z_hops(d))
                        def _():
                            send(block, block, z_s.at[j, d, k - 1], z_r.at[j, d, k - 1], at(y, x, zz(s), c))

                        send(block, block, b_s.at[j, 1 + d * half + k - 2], b_r.at[j, 1 + d * half + k - 2], sibling)

            @pl.when(jnp.logical_and(c == 1, k == 3))
            def _():
                block = down_block(l, xx(-1))
                arrived(block, x_r.at[j, 0], sibling)
                send(second_half(l, xx(-1), 0), second_half(l, xx(-1), 0), x_s.at[j, 2], x_r.at[j, 2], east)
                send(block, block, b_s.at[j, 1], b_r.at[j, 1], sibling)
                other = down_block(l, xx(1))
                arrived(other, x_r.at[j, 1], sibling)
                send(second_half(l, xx(1), 1), second_half(l, xx(1), 1), x_s.at[j, 3], x_r.at[j, 3], west)
                send(other, other, b_s.at[j, 2], b_r.at[j, 2], sibling)

            @pl.when(jnp.logical_and(c == 1, k == last))
            def _():
                arrived(second_half(l, xx(2), 0), x_r.at[j, 2], sibling)
                arrived(second_half(l, xx(2), 1), x_r.at[j, 3], sibling)
                block = down_block(l, xx(2))
                send(block, block, b_s.at[j, 3], b_r.at[j, 3], sibling)

            @pl.when(k == 1)
            def _():
                begin(j)

        for when, pieces in ((1, (0, 3)), (3, (1, 2)), (5, (4, 5))):
            @pl.when(slot == when)
            def _(pieces=pieces):
                for i in pieces:
                    take_y(i)

        @pl.when(slot == last)
        def _():
            for load in loads[3:]:
                load.wait()
            for o in range(1, n_group):
                arrived(tile_rows(tiles_all.at[gg(-o)], y), t_r.at[o - 1], sibling)
            send(own_rows(y), own_rows(y), t_s.at[t0], t_r.at[t0], north)
            send(own_rows(y), own_rows(y), t_s.at[t0 + 1], t_r.at[t0 + 1], south)

        @pl.when(slot == last + 1)
        def _():
            for i in range(6):
                l, h = y_piece(i)
                for core in range(NC):
                    @pl.when(c != core)
                    def _(core=core):
                        arrived(y_part(l, core, h), w_r.at[i], sibling)

        @pl.when(slot > last)
        def _():
            wait_sibling(slot - last - 1)
            for h in range(2):
                layer_rows(slot - last - 1, h * rows, rows)

    wait_sibling(moved - 1)

    @pl.loop(0, 2)
    def _(n):
        layer_rows(NY - 2, pl.multiple_of(n * rows, rows), rows)

    arrived(own_rows(yy(-1)), t_r.at[t0], sibling)
    send(some_rows(yy(-1), 0), some_rows(yy(-1), 0), t_s.at[t0 + 2], t_r.at[t0 + 2], north)
    arrived(own_rows(yy(1)), t_r.at[t0 + 1], sibling)
    send(some_rows(yy(1), 1), some_rows(yy(1), 1), t_s.at[t0 + 3], t_r.at[t0 + 3], south)
    layer_rows(NY - 1, 0, rows)

    def half_of(g, h):
        return x_all.at[g, pl.ds(h * rows, rows), :]

    def project(h):
        mine = own.at[h * rows : (h + 1) * rows]
        mine[...] = jnp.dot(encoded[h * rows : (h + 1) * rows], proj[...], preferred_element_type=F32).astype(BF)
        send(mine, half_of(group, h), p_s.at[h], p_r.at[h], east)
        send(mine, half_of(group, h), p_s.at[2 + h], p_r.at[2 + h], west)
        send(mine, half_of(group, h), p_s.at[4 + h], p_r.at[4 + h], sibling)

    project(0)
    layer_rows(NY - 1, rows, rows)
    project(1)
    keep = pltpu.make_async_copy(own, x_all.at[group], local.at[5])
    keep.start()
    near, far = (xx(-1) * NC + c, xx(1) * NC + c), xx(2) * NC + c
    arrived(half_of(near[0], 0), p_r.at[0], sibling)
    send(half_of(near[0], 0), half_of(near[0], 0), p_s.at[6], p_r.at[6], east)
    arrived(half_of(near[1], 0), p_r.at[2], sibling)
    arrived(half_of(near[1], 1), p_r.at[3], sibling)
    send(half_of(near[1], 1), half_of(near[1], 1), p_s.at[7], p_r.at[7], west)
    send(x_all.at[near[1]], x_all.at[near[1]], p_s.at[9], p_r.at[9], sibling)
    arrived(half_of(near[0], 1), p_r.at[1], sibling)
    send(x_all.at[near[0]], x_all.at[near[0]], p_s.at[8], p_r.at[8], sibling)
    arrived(half_of(far, 0), p_r.at[6], sibling)
    arrived(half_of(far, 1), p_r.at[7], sibling)
    send(x_all.at[far], x_all.at[far], p_s.at[10], p_r.at[10], sibling)
    for h in range(2):
        arrived(half_of(x * NC + 1 - c, h), p_r.at[4 + h], sibling)
    for i, ox in enumerate((-1, 1, 2)):
        arrived(x_all.at[xx(ox) * NC + 1 - c], p_r.at[8 + i], sibling)

    keep.wait()
    arrived(some_rows(yy(2), 0), t_r.at[t0 + 2], sibling)
    arrived(some_rows(yy(2), 1), t_r.at[t0 + 3], sibling)
    for o in range(1, n_group):
        arrived(index_all.at[gg(-o)], i_r.at[o - 1], sibling)
        sent(tile_rows(tiles_all.at[group], y), t_s.at[o - 1], sibling)
        sent(index_all.at[group], i_s.at[o - 1], sibling)
    for i in range(2):
        sent(own_rows(y), t_s.at[t0 + i], sibling)
        sent(some_rows(y, 0), t_s.at[t0 + 2 + i], sibling)
    for i in range(8):
        sent(own.at[0:rows], p_s.at[i], sibling)
    for i in range(8, 11):
        sent(own, p_s.at[i], sibling)
    for core in range(NC):
        @pl.when(c == core)
        def _(core=core):
            for o in range(1, NY):
                sent(share(y, core), y_s.at[o - 1], sibling)
            for i in range(6):
                sent(y_part(y, core, 0), v_s.at[i], sibling)
                sent(y_part(y, core, 0), w_s.at[i], sibling)

    @pl.loop(0, moved)
    def _(j):
        @pl.when(c == 0)
        def _():
            for ox in range(1, NX):
                sent(up_slice(y, x), u_s.at[j, ox - 1], sibling)
            for d in range(2):
                for k in range(1, z_hops(d) + 1):
                    sent(up_block(y, z), z_s.at[j, d, k - 1], sibling)
            for i in range(NZ):
                sent(up_block(y, z), b_s.at[j, i], sibling)

        @pl.when(c == 1)
        def _():
            for i in range(2):
                sent(down_block(y, x), x_s.at[j, i], sibling)
                sent(second_half(y, x, 0), x_s.at[j, 2 + i], sibling)
            for i in range(NZ - 1):
                sent(down_slice(y, z), sem_of(z_s, j, i), sibling)
            for i in range(NX):
                sent(down_block(y, x), b_s.at[j, i], sibling)


def encode(up, down, cams, proj, tiles, index):
    d, f = up.shape[1:]
    tokens = cams.shape[1]
    channels = proj.shape[1]
    up = up.reshape(NZ, NX // 2, 2 * d // (NZ * NX), f)
    down = down.reshape(NZ, NX, f // (NZ * NX), d)
    tiles = tiles.reshape(NX, NZ, NC, BLK, BLK)
    n = NX * NC
    half = NZ // 2
    moved = NY - 1
    return pl.pallas_call(
        encoder_kernel,
        out_shape=(
            jax.ShapeDtypeStruct((tokens, d), BF),
            jax.ShapeDtypeStruct((n, tokens, channels), BF),
            jax.ShapeDtypeStruct((n, NZ, BLK, BLK), BF),
            jax.ShapeDtypeStruct((n,) + index.shape, jnp.int32),
        ),
        in_specs=[ANY, ANY, ANY, VM, ANY, ANY],
        out_specs=(VM, ANY, ANY, ANY),
        scratch_shapes=[
            pltpu.VMEM((NY,) + up.shape, BF),
            pltpu.VMEM((NY,) + down.shape, BF),
            pltpu.VMEM((tokens, channels), BF),
            DMA((NY - 1,)), DMA((NY - 1,)),
            DMA((moved, 4)), DMA((moved, 4)),
            DMA((moved, NX - 1)), DMA((moved, NX - 1)),
            DMA((moved, 2, half)), DMA((moved, 2, half)),
            DMA((moved, max(NZ, NX))), DMA((moved, max(NZ, NX))),
            DMA((n + 3,)), DMA((n + 3,)),
            DMA((n - 1,)), DMA((n - 1,)),
            DMA((11,)), DMA((11,)),
            DMA((6,)), DMA((6,)),
            DMA((6,)), DMA((6,)),
            DMA((6,)),
        ],
        compiler_params=pltpu.CompilerParams(
            collective_id=0, has_side_effects=True, vmem_limit_bytes=VMEM_LIMIT
        ),
    )(up, down, cams, proj, tiles, index)


def join_kernel(index, x_all, tiles, grid_out, left, right, parts, s_buf, r_buf, s_sem, r_sem):
    y, x, z, c = where_am_i()
    half = NZ // 2
    n_group = NX * NC
    bev = grid_out.shape[0] // BLK
    chunk = grid_out.shape[0] // 2

    def zz(offset):
        return lax.rem(z + offset + 2 * NZ, NZ)

    beside = (at(y, x, zz(1), c), at(y, x, zz(-1), c))
    greet(beside)

    def hops(ch, d):
        return half if ch == d else half - 1

    def push(ch, d, k):
        send(s_buf.at[ch, d, k - 1], r_buf.at[ch, d, k - 1], s_sem.at[ch, d, k - 1], r_sem.at[ch, d, k - 1], beside[d])

    @pl.loop(0, NZ)
    def _(i):
        off = jnp.where(i == 0, half, jnp.where(i % 2 == 1, (NZ - 1 - i) // 2, -((NZ - i) // 2)))
        target = zz(off)
        p = (x * NZ + target) * NC + c
        for g in range(n_group):
            tile = tiles[g, target].astype(F32)
            dst = index[g, 1, p]
            alive = index[g, 2, p]
            for b in range(bev):
                weight = jnp.where(dst == b, alive, 0).astype(F32)
                left[b * BLK : (b + 1) * BLK, g * BLK : (g + 1) * BLK] = (tile * weight).astype(BF)
            right[g * BLK : (g + 1) * BLK, :] = x_all[g, index[g, 0, p]]
        parts[i] = jnp.dot(left[...], right[...], preferred_element_type=F32)

        @pl.when(i == 0)
        def _():
            for d in range(2):
                s_buf[d, d, 0] = parts[0, d * chunk : (d + 1) * chunk].astype(BF)
                push(d, d, 1)

        for d in range(2):
            if half == 1:
                continue

            @pl.when(i == 1 + d)
            def _(d=d):
                ch = 1 - d
                s_buf[ch, d, 0] = parts[1 + d, ch * chunk : (ch + 1) * chunk].astype(BF)
                push(ch, d, 1)

    for o in range(half - 1, 0, -1):
        for ch_is_d in (True, False):
            for d in range(2):
                ch = d if ch_is_d else 1 - d
                k = hops(ch, d) - o + 1
                if k == 1:
                    continue
                arrived(r_buf.at[ch, d, k - 2], r_sem.at[ch, d, k - 2], beside[d])
                i = NZ - 1 - 2 * o if d == 0 else NZ - 2 * o
                total = parts[i, ch * chunk : (ch + 1) * chunk] + r_buf[ch, d, k - 2].astype(F32)
                s_buf[ch, d, k - 1] = total.astype(BF)
                push(ch, d, k)
    for ch in range(2):
        total = parts[NZ - 1, ch * chunk : (ch + 1) * chunk]
        for d in range(2):
            k = hops(ch, d)
            if k == 0:
                continue
            arrived(r_buf.at[ch, d, k - 1], r_sem.at[ch, d, k - 1], beside[d])
            total = total + r_buf[ch, d, k - 1].astype(F32)
        grid_out[ch * chunk : (ch + 1) * chunk] = total
    for ch in range(2):
        for d in range(2):
            for k in range(hops(ch, d)):
                sent(s_buf.at[ch, d, k], s_sem.at[ch, d, k], beside[d])


def join(index_all, x_all, tiles_all, cells):
    channels = x_all.shape[-1]
    x_all = x_all.reshape(x_all.shape[0], -1, BLK, channels)
    n = NX * NC
    half = NZ // 2
    return pl.pallas_call(
        join_kernel,
        out_shape=jax.ShapeDtypeStruct((cells, channels), F32),
        in_specs=[SM, VM, VM],
        out_specs=VM,
        scratch_shapes=[
            pltpu.VMEM((cells, n * BLK), BF),
            pltpu.VMEM((n * BLK, channels), BF),
            pltpu.VMEM((NZ, cells, channels), F32),
            pltpu.VMEM((2, 2, half, cells // 2, channels), BF),
            pltpu.VMEM((2, 2, half, cells // 2, channels), BF),
            DMA((2, 2, half)), DMA((2, 2, half)),
        ],
        compiler_params=pltpu.CompilerParams(
            collective_id=1, has_side_effects=True, vmem_limit_bytes=VMEM_LIMIT
        ),
    )(index_all, x_all, tiles_all)


class Total:
    n1, n2, width = NX * NY, NZ, 128

    def __init__(self, ins, outs, scratch):
        self.ins, self.outs = ins, outs
        (
            self.packed, self.from0, self.half, self.from1, self.mid, self.from2, self.mine, self.gathered, self.result,
            self.s0, self.r0, self.s1, self.r1, self.s2, self.r2, self.s3, self.r3, self.s4, self.r4, self.s5, self.r5,
        ) = scratch
        y, x, z, c = where_am_i()
        self.y, self.x, self.z, self.c = y, x, z, c
        self.one, self.two = y * NX + x, z
        self.sibling = at(y, x, z, 1 - c)
        self.real = self.half.shape[1]
        self.share = self.mine.shape[0]

    @classmethod
    def scratch_for(cls, shapes):
        n1, n2, width = NX * NY, NZ, cls.width
        real = sum(a * b for a, b in shapes) // (n1 * NC * width)
        share = -(-real // (n2 * 16)) * 16
        buffers = [
            (NC, n1, real, width), (n1, real, width), (n1, real, width), (n1 - 1, real, width), (share * n2, width),
            (n2 - 1, share, width), (share, width), (share * n2, width), (NC, n1, real, width),
        ]
        counts = [1, n1 - 1, n2 - 1, n2 - 1, n1 - 1, 1]
        return [pltpu.VMEM(b, BF) for b in buffers] + [DMA((n,)) for n in counts for _ in range(2)]

    def dev1(self, q):
        return at(q // NX, q % NX, self.z, self.c)

    def dev2(self, e):
        return at(self.y, self.x, e, self.c)

    def q1(self, o):
        n1 = NX * NY
        return lax.rem(self.one + o + n1, n1)

    def q2(self, o):
        return lax.rem(self.two + o + NZ, NZ)

    def peers(self):
        n1 = NX * NY
        return [self.sibling] + [self.dev1(self.q1(o)) for o in range(1, n1)] + [self.dev2(self.q2(o)) for o in range(1, NZ)]

    def pieces(self):
        row = 0
        for i, ref in enumerate(self.ins):
            height = ref.shape[0] // (NX * NY)
            for col in range(ref.shape[1] // (NC * self.width)):
                yield i, row, height, col * NC * self.width
                row += height

    def start(self):
        n1 = NX * NY

        @pl.loop(0, n1)
        def _(q):
            for i, row, height, col in self.pieces():
                for core in range(NC):
                    left = col + core * self.width
                    self.packed[core, q, row : row + height, :] = self.ins[i][
                        pl.ds(pl.multiple_of(q * height, height), height), left : left + self.width
                    ].astype(BF)
        send(self.packed.at[1 - self.c], self.from0, self.s0.at[0], self.r0.at[0], self.sibling)
        self.mid[...] = jnp.zeros_like(self.mid)

    def over_xy(self):
        n1 = NX * NY
        arrived(self.from0, self.r0.at[0], self.sibling)

        @pl.loop(0, n1)
        def _(o):
            q = lax.rem(self.one + 1 + o, n1)
            self.half[q] = (self.packed[self.c, q].astype(F32) + self.from0[q].astype(F32)).astype(BF)

            @pl.when(o < n1 - 1)
            def _():
                send(self.half.at[q], self.from1.at[o], self.s1.at[o], self.r1.at[o], self.dev1(q))

    def part(self, ref, e):
        return ref.at[pl.ds(pl.multiple_of(e * self.share, self.share), self.share), :]

    def over_z(self):
        total = self.half[self.one].astype(F32)
        for o in range(NX * NY - 1):
            arrived(self.from1.at[o], self.r1.at[o], self.sibling)
            total = total + self.from1[o].astype(F32)
        self.mid[0 : self.real, :] = total.astype(BF)
        for o in range(1, NZ):
            e = self.q2(o)
            send(self.part(self.mid, e), self.from2.at[o - 1], self.s2.at[o - 1], self.r2.at[o - 1], self.dev2(e))

    def back_over_z(self):
        total = self.mid[pl.ds(pl.multiple_of(self.two * self.share, self.share), self.share), :].astype(F32)
        for o in range(1, NZ):
            arrived(self.from2.at[o - 1], self.r2.at[o - 1], self.sibling)
            total = total + self.from2[o - 1].astype(F32)
        self.mine[...] = total.astype(BF)
        for o in range(1, NZ):
            send(self.mine, self.part(self.gathered, self.two), self.s3.at[o - 1], self.r3.at[o - 1], self.dev2(self.q2(o)))
        self.gathered[pl.ds(pl.multiple_of(self.two * self.share, self.share), self.share), :] = self.mine[...]

    def back_over_xy(self):
        for o in range(1, NZ):
            arrived(self.part(self.gathered, self.q2(-o)), self.r3.at[o - 1], self.sibling)
        for o in range(1, NX * NY):
            send(
                self.gathered.at[0 : self.real, :], self.result.at[self.c, self.one],
                self.s4.at[o - 1], self.r4.at[o - 1], self.dev1(self.q1(o)),
            )
        self.result[self.c, self.one] = self.gathered[0 : self.real, :]

    def back_over_core(self):
        for o in range(1, NX * NY):
            arrived(self.result.at[self.c, self.q1(-o)], self.r4.at[o - 1], self.sibling)
        send(self.result.at[self.c], self.result.at[self.c], self.s5.at[0], self.r5.at[0], self.sibling)

    def finish(self):
        n1 = NX * NY
        arrived(self.result.at[1 - self.c], self.r5.at[0], self.sibling)

        @pl.loop(0, n1)
        def _(q):
            for i, row, height, col in self.pieces():
                for core in range(NC):
                    left = col + core * self.width
                    self.outs[i][pl.ds(pl.multiple_of(q * height, height), height), left : left + self.width] = self.result[
                        core, q, row : row + height, :
                    ].astype(F32)

        sent(self.from0, self.s0.at[0], self.sibling)
        sent(self.result.at[self.c], self.s5.at[0], self.sibling)
        for o in range(n1 - 1):
            sent(self.half.at[0], self.s1.at[o], self.sibling)
            sent(self.half.at[0], self.s4.at[o], self.sibling)
        for o in range(NZ - 1):
            sent(self.mine, self.s2.at[o], self.sibling)
            sent(self.mine, self.s3.at[o], self.sibling)


N_GRADS = 4


def gelu_parts(v):
    inner = math.sqrt(2.0 / math.pi) * (v + 0.044715 * v * v * v)
    slope = math.sqrt(2.0 / math.pi) * (1.0 + 3.0 * 0.044715 * v * v)
    t = jnp.tanh(inner)
    return 0.5 * v * (1.0 + t), 0.5 * (1.0 + t) + 0.5 * v * (1.0 - t * t) * slope


def split_kernel(index, grid, pred_grad, tiles, encoded, ru, rd, du, dd, *refs, scale):
    prediction, proj_out, outs, refs = refs[0], refs[1], refs[2 : 2 + N_GRADS], refs[2 + N_GRADS :]
    all_grad, here, left, acc, core_s, core_r, x_send, x_recv, z_s, z_r, c_s, c_r, x_s, x_r = refs[:14]
    kept = refs[14:22]
    ins = refs[22 : 22 + N_GRADS]
    rows_out, grad_proj = refs[22 + N_GRADS : 24 + N_GRADS]
    refs = refs[24 + N_GRADS :]
    total = Total(ins, outs, refs[: len(refs) // 2])
    last = Total([grad_proj], [proj_out], refs[len(refs) // 2 :])
    grad = pred_grad
    y, x, z, c = where_am_i()
    half = NZ // 2
    n_group = NX * NC
    chunk = grad.shape[0] // 2
    cam = rows_out.shape[0] // BLK
    sibling = at(y, x, z, 1 - c)

    def zz(offset):
        return lax.rem(z + offset + 2 * NZ, NZ)

    def xx(offset):
        return lax.rem(x + offset + NX, NX)

    beside = (at(y, x, zz(1), c), at(y, x, zz(-1), c))
    east, west = at(y, xx(1), z, c), at(y, xx(-1), z, c)
    barrier = pltpu.get_barrier_semaphore()
    for device in total.peers():
        pl.semaphore_signal(barrier, inc=1, device_id=device, device_id_type=MESH)

    def hops(ch, d):
        return half if ch == d else half - 1

    def part(origin, ch):
        return all_grad.at[origin, pl.ds(ch * chunk, chunk)]

    n1_ref, h1_ref, n2_ref, h2_ref, p1_ref, p2_ref, r1_ref, r2_ref = kept

    def heads(ch):
        r = slice(ch * chunk, (ch + 1) * chunk)

        def forward(state, w_up, w_down, n_ref, h_ref):
            scaling = lax.rsqrt(jnp.mean(state * state, axis=-1, keepdims=True) + eps)
            normed = (state * scaling).astype(BF)
            n_ref[r] = normed
            preact = jnp.dot(normed, w_up[...], preferred_element_type=F32)
            value, slope = gelu_parts(preact)
            hidden = value.astype(BF)
            h_ref[r] = hidden
            return state + jnp.dot(hidden, w_down[...], preferred_element_type=F32), scaling, slope

        def backward(g, state, scaling, slope, w_up, w_down, p_ref, r_ref):
            rounded = g.astype(BF)
            r_ref[r] = rounded
            grad_pre = (against_rows(rounded, w_down[...]) * slope).astype(BF)
            p_ref[r] = grad_pre
            grad_normed = against_rows(grad_pre, w_up[...])
            unit = state * scaling
            return g + scaling * (grad_normed - unit * jnp.mean(grad_normed * unit, axis=-1, keepdims=True))

        s0 = grid[r]
        s1, scale1, slope1 = forward(s0, ru, rd, n1_ref, h1_ref)
        s2, scale2, slope2 = forward(s1, du, dd, n2_ref, h2_ref)
        prediction[r] = s2.astype(BF)
        g1 = backward(pred_grad[r].astype(F32) * scale, s1, scale2, slope2, du, dd, p2_ref, r2_ref)
        g0 = backward(g1, s0, scale1, slope1, ru, rd, p1_ref, r1_ref)
        all_grad[z, r] = g0.astype(BF)

    for ch in range(2):
        heads(ch)
        if ch == 0:
            pl.semaphore_wait(barrier, len(total.peers()))
        for d in range(2):
            if hops(ch, d) >= 1:
                send(part(z, ch), part(z, ch), z_s.at[ch, d, 0], z_r.at[ch, d, 0], beside[d])
    ins[0][...] = contract_rows(n1_ref[...], p1_ref[...])
    ins[1][...] = contract_rows(h1_ref[...], r1_ref[...])
    ins[2][...] = contract_rows(n2_ref[...], p2_ref[...])
    ins[3][...] = contract_rows(h2_ref[...], r2_ref[...])
    total.start()

    def use(origin, first):
        p = (x * NZ + origin) * NC + c
        here[...] = all_grad[origin].reshape(here.shape)
        for g in range(n_group):
            tile = tiles[g, origin].astype(F32).T
            src = index[g, 0, p]
            alive = index[g, 2, p]
            for k in range(cam):
                weight = jnp.where(src == k, alive, 0).astype(F32)
                left[k * BLK : (k + 1) * BLK, :] = (tile * weight).astype(BF)
            product = jnp.dot(left[...], here[index[g, 1, p]], preferred_element_type=F32)
            if first:
                acc[g] = product
            else:
                acc[g] = acc[g] + product

    use(z, True)
    total.over_xy()

    @pl.loop(1, half + 1)
    def _(k):
        for d in range(2):
            s = 1 - 2 * d
            origin = zz(-s * k)
            for ch in range(2):
                @pl.when(k <= hops(ch, d))
                def _(ch=ch, d=d):
                    arrived(part(origin, ch), z_r.at[ch, d, k - 1], beside[d])

                @pl.when(k + 1 <= hops(ch, d))
                def _(ch=ch, d=d):
                    send(part(origin, ch), part(origin, ch), z_s.at[ch, d, k], z_r.at[ch, d, k], beside[d])

        @pl.when(k == max(half - 2, 1))
        def _():
            total.over_z()

        @pl.when(k == max(half - 1, 1))
        def _():
            total.back_over_z()

        @pl.when(k == half)
        def _():
            total.back_over_xy()

        use(zz(-k), False)

        @pl.when(k < half)
        def _():
            use(zz(k), False)

    rows = rows_out.shape[0] // 2
    order = (2, 1, NX - 1, 0)
    for i, o in enumerate(order):
        core_s[i] = acc[xx(o) * NC + 1 - c].astype(BF)
        send(core_s.at[i], core_r.at[i], c_s.at[i], c_r.at[i], sibling)

    def pair_sum(i, h):
        return acc[xx(order[i]) * NC + c, h * rows : (h + 1) * rows, :] + core_r[
            i, h * rows : (h + 1) * rows, :
        ].astype(F32)

    def push(n, value, device):
        x_send[n] = value.astype(BF)
        send(x_send.at[n], x_recv.at[n], x_s.at[n], x_r.at[n], device)

    for i in range(3):
        arrived(core_r.at[i], c_r.at[i], sibling)
        if i == 0:
            push(0, pair_sum(0, 0), east)
            push(1, pair_sum(0, 1), west)
        if i == 1:
            push(2, pair_sum(1, 1), east)
        if i == 2:
            push(3, pair_sum(2, 0), west)
    arrived(x_recv.at[0], x_r.at[0], sibling)
    push(4, pair_sum(1, 0) + x_recv[0].astype(F32), east)
    arrived(x_recv.at[1], x_r.at[1], sibling)
    push(5, pair_sum(2, 1) + x_recv[1].astype(F32), west)
    arrived(core_r.at[3], c_r.at[3], sibling)
    for n in range(2, 6):
        arrived(x_recv.at[n], x_r.at[n], sibling)
    rows_out[0:rows] = (pair_sum(3, 0) + x_recv[4].astype(F32) + x_recv[3].astype(F32)).astype(BF)
    rows_out[rows : 2 * rows] = (pair_sum(3, 1) + x_recv[2].astype(F32) + x_recv[5].astype(F32)).astype(BF)
    grad_proj[...] = contract_rows(encoded[...], rows_out[...])
    last.start()
    total.back_over_core()
    last.over_xy()
    total.finish()
    last.over_z()
    last.back_over_z()
    last.back_over_xy()
    last.back_over_core()
    last.finish()
    for i in range(4):
        sent(core_s.at[i], c_s.at[i], sibling)
    for n in range(6):
        sent(x_send.at[n], x_s.at[n], sibling)
    for ch in range(2):
        for d in range(2):
            for k in range(hops(ch, d)):
                sent(part(z, ch), z_s.at[ch, d, k], beside[d])


def split(index_all, grid, pred_grad, tiles_all, encoded, weights, scale):
    cells, channels = grid.shape
    tokens, features = encoded.shape
    hidden = weights[0].shape[1]
    n = NX * NC
    half = NZ // 2
    shapes = [w.shape for w in weights]
    return pl.pallas_call(
        functools.partial(split_kernel, scale=scale),
        out_shape=(
            jax.ShapeDtypeStruct((cells, channels), BF),
            jax.ShapeDtypeStruct((features, channels), F32),
        ) + tuple(jax.ShapeDtypeStruct(a, F32) for a in shapes),
        in_specs=[SM, VM, VM, VM, VM] + [VM] * N_GRADS,
        out_specs=tuple([VM] * (2 + N_GRADS)),
        scratch_shapes=[
            pltpu.VMEM((NZ, cells, channels), BF),
            pltpu.VMEM((cells // BLK, BLK, channels), BF),
            pltpu.VMEM((tokens, BLK), BF),
            pltpu.VMEM((n, tokens, channels), F32),
            pltpu.VMEM((NX, tokens, channels), BF),
            pltpu.VMEM((NX, tokens, channels), BF),
            pltpu.VMEM((6, tokens // 2, channels), BF),
            pltpu.VMEM((6, tokens // 2, channels), BF),
            DMA((2, 2, half)), DMA((2, 2, half)),
            DMA((NX,)), DMA((NX,)),
            DMA((6,)), DMA((6,)),
        ]
        + [pltpu.VMEM((cells, w), BF) for w in (channels, hidden) * 2 + (hidden, hidden, channels, channels)]
        + [pltpu.VMEM(a, F32) for a in shapes]
        + [pltpu.VMEM((tokens, channels), BF), pltpu.VMEM((features, channels), F32)]
        + Total.scratch_for(shapes)
        + Total.scratch_for([(features, channels)]),
        compiler_params=pltpu.CompilerParams(
            collective_id=2, has_side_effects=True, vmem_limit_bytes=VMEM_LIMIT
        ),
    )(index_all, grid, pred_grad, tiles_all, encoded, *weights)


def on_device(
    cams, vit_up, vit_down, proj, frustum_tiles, src_block, dst_block, live,
    render_up, render_down, decode_up, decode_down, pred_grad,
):
    tile_count = NX * NZ * NC
    cells, channels = pred_grad.shape[1:]
    index = jnp.zeros((8, 128), jnp.int32)
    index = lax.dynamic_update_slice(index, jnp.concatenate([src_block, dst_block, live], axis=0), (0, 0))
    encoded, x_all, tiles_all, index_all = encode(vit_up, vit_down, cams, proj, frustum_tiles[0], index)
    bev_grid = join(index_all, x_all, tiles_all, cells)
    scale = 1.0 / math.sqrt(cams.shape[0] * cells * tile_count)
    weights = (render_up, render_down, decode_up, decode_down)
    prediction, grad_proj, *totals = split(
        index_all, bev_grid, pred_grad[0], tiles_all, encoded, weights, scale
    )
    return (prediction[None], grad_proj, *totals)


def solution(mesh):
    placed = (
        P(None, "tile", None),
        P("section", None, None),
        P("section", None, None),
        P(),
        P("tile", None, None, None),
        P("tile", None),
        P("tile", None),
        P("tile", None),
        P(),
        P(),
        P(),
        P(),
        P("section", "tile", None),
    )
    return jax.shard_map(
        on_device,
        mesh=mesh,
        in_specs=placed,
        out_specs=(P("section", "tile", None), P(), P(), P(), P(), P()),
        check_vma=False,
    )
```

```python
import functools
import math

import jax
import jax.numpy as jnp
from jax import lax
from jax.experimental import pallas as pl
from jax.experimental.pallas import tpu as pltpu
from jax.sharding import PartitionSpec as P

eps = 1e-05
MESH = pl.DeviceIdType.MESH
BF = jnp.bfloat16
F32 = jnp.float32
NY, NX, NZ, NC = 4, 4, 8, 2
BLK = 128
VMEM_LIMIT = 60 * 2**20
ANY = pl.BlockSpec(memory_space=pl.ANY)
VM = pl.BlockSpec(memory_space=pltpu.VMEM)
SM = pl.BlockSpec(memory_space=pltpu.SMEM)
DMA = pltpu.SemaphoreType.DMA


def where_am_i():
    y = lax.axis_index("section")
    t = lax.axis_index("tile")
    return y, t // (NZ * NC), (t // NC) % NZ, t % NC


def at(y, x, z, c):
    return (y, (x * NZ + z) * NC + c)


def send(src, dst, ssem, rsem, device):
    copy = pltpu.make_async_remote_copy(
        src_ref=src, dst_ref=dst, send_sem=ssem, recv_sem=rsem, device_id=device, device_id_type=MESH
    )
    copy.start()


def sent(src, ssem, device):
    pltpu.make_async_remote_copy(
        src_ref=src, dst_ref=src, send_sem=ssem, recv_sem=ssem, device_id=device, device_id_type=MESH
    ).wait_send()


def arrived(dst, rsem, device):
    pltpu.make_async_remote_copy(
        src_ref=dst, dst_ref=dst, send_sem=rsem, recv_sem=rsem, device_id=device, device_id_type=MESH
    ).wait_recv()


def greet(devices):
    barrier = pltpu.get_barrier_semaphore()
    for device in devices:
        pl.semaphore_signal(barrier, inc=1, device_id=device, device_id_type=MESH)
    pl.semaphore_wait(barrier, len(devices))


def gelu(v):
    return 0.5 * v * (1.0 + jnp.tanh(math.sqrt(2.0 / math.pi) * (v + 0.044715 * v * v * v)))


def contract_rows(left, right):
    return lax.dot_general(left, right, (((0,), (0,)), ((), ())), preferred_element_type=F32)


def against_rows(left, right):
    return lax.dot_general(left, right, (((1,), (1,)), ((), ())), preferred_element_type=F32)


def encoder_kernel(
    up, down, cams, proj, tiles, src, dst, live,
    encoded, x_all, tiles_all, index_all,
    w_up, w_down, own, y_s, y_r, x_s, x_r, u_s, u_r, z_s, z_r, b_s, b_r, t_s, t_r, i_s, i_r, p_s, p_r, v_s, v_r, w_s, w_r,
    local, index,
):
    y, x, z, c = where_am_i()
    sibling = at(y, x, z, 1 - c)
    group = x * NC + c
    moved = NY - 1
    half = NZ // 2
    steps = half + 1
    n_group = NX * NC
    plane_up, plane_down = w_up.shape[-1] - 256, w_down.shape[-1] - 128
    cols = plane_up // 2
    quarter = BLK // NY

    def layer_of(j):
        return j + jnp.where(j >= y, 1, 0)

    def up_slice(l, xx):
        return w_up.at[l, z, xx // 2, :, pl.ds(pl.multiple_of((xx % 2) * cols, 128), cols)]

    def up_block(l, zo):
        return w_up.at[l, zo, :, :, pl.ds(0, plane_up)]

    def down_block(l, xo):
        return w_down.at[l, :, xo, :, pl.ds(0, plane_down)]

    def y_part(l, core, h):
        if core == 0:
            width = (w_up.shape[-1] - plane_up) // 2
            return w_up.at[l, :, :, :, pl.ds(plane_up + h * width, width)]
        return w_down.at[l, pl.ds(h * half, half), :, :, pl.ds(plane_down, w_down.shape[-1] - plane_down)]

    def zz(offset):
        return lax.rem(z + offset + 2 * NZ, NZ)

    def xx(offset):
        return lax.rem(x + offset + NX, NX)

    def yy(offset):
        return lax.rem(y + offset + NY, NY)

    def gg(offset):
        return lax.rem(group + offset + n_group, n_group)

    def g_dev(g):
        return at(y, g // NC, z, g % NC)

    east, west = at(y, xx(1), z, c), at(y, xx(-1), z, c)
    north, south = at(yy(1), x, z, c), at(yy(-1), x, z, c)

    def tile_rows(ref, section):
        return ref.at[:, pl.ds(pl.multiple_of(section * quarter, quarter), quarter), :]

    index[...] = jnp.zeros_like(index)
    for i, ref in enumerate((src, dst, live)):
        index[i : i + 1, 0 : ref.shape[1]] = ref[...]
    loads = [
        pltpu.make_async_copy(up, w_up.at[y], local.at[0]),
        pltpu.make_async_copy(down, w_down.at[y], local.at[1]),
        pltpu.make_async_copy(cams.at[y], encoded, local.at[2]),
        pltpu.make_async_copy(tile_rows(tiles.at[x, :, c], y), tile_rows(tiles_all.at[group], y), local.at[3]),
        pltpu.make_async_copy(index, index_all.at[group], local.at[4]),
    ]
    for load in loads:
        load.start()
    greet(
        [at(yy(o), x, z, c) for o in range(1, NY)]
        + [g_dev(gg(o)) for o in range(1, n_group)]
        + [at(y, x, zz(1), c), at(y, x, zz(-1), c)]
    )
    for load in loads[:3]:
        load.wait()

    def some_block(l, xo, h):
        return w_down.at[l, pl.ds(h * half, half), xo, :, pl.ds(0, plane_down)]

    for core in range(NC):
        @pl.when(c == core)
        def _(core=core):
            if core == 0:
                for o in range(1, NY):
                    send(up_slice(y, x), up_slice(y, x), y_s.at[o - 1], y_r.at[o - 1], at(yy(o), x, z, c))
            else:
                send(down_block(y, x), down_block(y, x), y_s.at[0], y_r.at[0], north)
                send(down_block(y, x), down_block(y, x), y_s.at[1], y_r.at[1], south)
            for h, i, device in ((0, 0, north), (1, 3, south), (1, 1, north), (0, 2, south)):
                send(y_part(y, core, h), y_part(y, core, h), v_s.at[i], v_r.at[i], device)

    def sign(j, d):
        return (1 - 2 * (j % 2)) * (1 - 2 * d)

    def send_tiles():
        for o in range(1, n_group):
            g = gg(o)
            send(index, index_all.at[group], i_s.at[o - 1], i_r.at[o - 1], g_dev(g))
            send(
                tile_rows(tiles.at[g // NC, :, g % NC], y), tile_rows(tiles_all.at[group], y),
                t_s.at[o - 1], t_r.at[o - 1], g_dev(g),
            )

    @pl.when(c == 0)
    def _():
        @pl.loop(0, moved)
        def _(j):
            l = layer_of(j)
            o = yy(-l)
            arrived(up_slice(l, x), y_r.at[o - 1], sibling)
            for ox in range(1, NX):
                send(up_slice(l, x), up_slice(l, x), u_s.at[j, ox - 1], u_r.at[j, ox - 1], at(y, xx(ox), z, c))
        send_tiles()

    def z_hops(d):
        return half if d == 0 else half - 1

    @pl.when(c == 1)
    def _():
        send_tiles()
        arrived(down_block(yy(-1), x), y_r.at[0], sibling)
        send(some_block(yy(-1), x, 0), some_block(yy(-1), x, 0), y_s.at[2], y_r.at[2], north)
        arrived(down_block(yy(1), x), y_r.at[1], sibling)
        send(some_block(yy(1), x, 1), some_block(yy(1), x, 1), y_s.at[3], y_r.at[3], south)

    def layer_rows(l, r, rows):
        wide = encoded[pl.ds(r, rows), :].astype(F32)
        scaling = lax.rsqrt(jnp.mean(wide * wide, axis=-1, keepdims=True) + eps)
        normed = (wide * scaling).astype(BF)
        total = wide
        parts = 2
        for q in range(parts):
            width = w_up.shape[-1] // parts
            w1 = w_up[l, :, :, :, q * width : (q + 1) * width].reshape(wide.shape[1], width)
            hidden = gelu(jnp.dot(normed, w1, preferred_element_type=F32)).astype(BF)
            nz = NZ // parts
            w2 = w_down[l, q * nz : (q + 1) * nz].reshape(width, wide.shape[1])
            total = total + jnp.dot(hidden, w2, preferred_element_type=F32)
        encoded[pl.ds(r, rows), :] = total.astype(BF)

    tokens = encoded.shape[0]
    rows = tokens // 2

    def wait_sibling(j):
        l = layer_of(j)

        @pl.when(c == 0)
        def _():
            for i, ox in enumerate((0, 1, NX - 1, 2)):
                arrived(down_block(l, xx(-ox)), b_r.at[j, i], sibling)

        @pl.when(c == 1)
        def _():
            arrived(up_block(l, z), b_r.at[j, 0], sibling)
            for d in range(2):
                for k in range(2, z_hops(d) + 2):
                    arrived(up_block(l, zz(-sign(j, d) * (k - 1))), b_r.at[j, 1 + d * half + k - 2], sibling)

    def begin(j):
        l = layer_of(j)

        @pl.when(c == 0)
        def _():
            for ox in range(1, NX):
                arrived(up_slice(l, xx(-ox)), u_r.at[j, ox - 1], sibling)
            block = up_block(l, z)
            for d in range(2):
                if z_hops(d) >= 1:
                    send(block, block, z_s.at[j, d, 0], z_r.at[j, d, 0], at(y, x, zz(sign(j, d)), c))
            send(block, block, b_s.at[j, 0], b_r.at[j, 0], sibling)

        @pl.when(c == 1)
        def _():
            @pl.when(l == yy(2))
            def _():
                for h in range(2):
                    arrived(some_block(l, x, h), y_r.at[2 + h], sibling)

            block = down_block(l, x)
            send(block, block, x_s.at[j, 0], x_r.at[j, 0], east)
            send(block, block, x_s.at[j, 1], x_r.at[j, 1], west)
            send(block, block, b_s.at[j, 0], b_r.at[j, 0], sibling)

    def own_rows(section):
        return tiles_all.at[:, :, pl.ds(pl.multiple_of(section * quarter, quarter), quarter), :]

    def some_rows(section, h):
        return tiles_all.at[
            pl.ds(h * n_group // 2, n_group // 2), :, pl.ds(pl.multiple_of(section * quarter, quarter), quarter), :
        ]

    t0 = n_group - 1

    def y_piece(i):
        return (yy(-1), yy(-1), yy(1), yy(1), yy(2), yy(2))[i], (0, 1, 0, 1, 0, 1)[i]

    def take_y(i):
        l, h = y_piece(i)
        for core in range(NC):
            @pl.when(c == core)
            def _(core=core):
                piece = y_part(l, core, h)
                arrived(piece, v_r.at[i], sibling)
                if i == 0:
                    send(piece, piece, v_s.at[4], v_r.at[4], north)
                if i == 3:
                    send(piece, piece, v_s.at[5], v_r.at[5], south)
                send(piece, piece, w_s.at[i], w_r.at[i], sibling)

    last = max(steps, 5)

    @pl.loop(1, moved - 1 + last + 1)
    def _(slot):
        @pl.loop(0, moved)
        def _(j):
            k = slot - j
            l = layer_of(j)

            @pl.when(jnp.logical_and(c == 0, k >= 2))
            def _():
                for d in range(2):
                    s = sign(j, d)
                    block = up_block(l, zz(-s * (k - 1)))

                    @pl.when(k <= z_hops(d) + 1)
                    def _():
                        arrived(block, z_r.at[j, d, k - 2], sibling)

                        @pl.when(k <= z_hops(d))
                        def _():
                            send(block, block, z_s.at[j, d, k - 1], z_r.at[j, d, k - 1], at(y, x, zz(s), c))

                        send(block, block, b_s.at[j, 1 + d * half + k - 2], b_r.at[j, 1 + d * half + k - 2], sibling)

            @pl.when(jnp.logical_and(c == 1, k == 3))
            def _():
                block = down_block(l, xx(-1))
                arrived(block, x_r.at[j, 0], sibling)
                send(some_block(l, xx(-1), 0), some_block(l, xx(-1), 0), x_s.at[j, 2], x_r.at[j, 2], east)
                send(block, block, b_s.at[j, 1], b_r.at[j, 1], sibling)
                other = down_block(l, xx(1))
                arrived(other, x_r.at[j, 1], sibling)
                send(some_block(l, xx(1), 1), some_block(l, xx(1), 1), x_s.at[j, 3], x_r.at[j, 3], west)
                send(other, other, b_s.at[j, 2], b_r.at[j, 2], sibling)

            @pl.when(jnp.logical_and(c == 1, k == last))
            def _():
                arrived(some_block(l, xx(2), 0), x_r.at[j, 2], sibling)
                arrived(some_block(l, xx(2), 1), x_r.at[j, 3], sibling)
                block = down_block(l, xx(2))
                send(block, block, b_s.at[j, 3], b_r.at[j, 3], sibling)

            @pl.when(k == 1)
            def _():
                begin(j)

        for when, pieces in ((2, (0, 3)), (4, (1, 2)), (6, (4, 5))):
            @pl.when(slot == when)
            def _(pieces=pieces):
                for i in pieces:
                    take_y(i)

        @pl.when(slot == last)
        def _():
            for load in loads[3:]:
                load.wait()
            for o in range(1, n_group):
                arrived(tile_rows(tiles_all.at[gg(-o)], y), t_r.at[o - 1], sibling)
            send(own_rows(y), own_rows(y), t_s.at[t0], t_r.at[t0], north)
            send(own_rows(y), own_rows(y), t_s.at[t0 + 1], t_r.at[t0 + 1], south)

        @pl.when(slot == last + 1)
        def _():
            for i in range(6):
                l, h = y_piece(i)
                for core in range(NC):
                    @pl.when(c != core)
                    def _(core=core):
                        arrived(y_part(l, core, h), w_r.at[i], sibling)

        @pl.when(slot > last)
        def _():
            wait_sibling(slot - last - 1)
            layer_rows(slot - last - 1, 0, tokens)

    wait_sibling(moved - 1)

    layer_rows(NY - 2, 0, tokens)

    arrived(own_rows(yy(-1)), t_r.at[t0], sibling)
    send(some_rows(yy(-1), 0), some_rows(yy(-1), 0), t_s.at[t0 + 2], t_r.at[t0 + 2], north)
    arrived(own_rows(yy(1)), t_r.at[t0 + 1], sibling)
    send(some_rows(yy(1), 1), some_rows(yy(1), 1), t_s.at[t0 + 3], t_r.at[t0 + 3], south)
    layer_rows(NY - 1, 0, rows)

    def half_of(g, h):
        return x_all.at[g, pl.ds(h * rows, rows), :]

    def project(h):
        mine = own.at[h * rows : (h + 1) * rows]
        mine[...] = jnp.dot(encoded[h * rows : (h + 1) * rows], proj[...], preferred_element_type=F32).astype(BF)
        send(mine, half_of(group, h), p_s.at[h], p_r.at[h], east)
        send(mine, half_of(group, h), p_s.at[2 + h], p_r.at[2 + h], west)
        send(mine, half_of(group, h), p_s.at[4 + h], p_r.at[4 + h], sibling)

    project(0)
    layer_rows(NY - 1, rows, rows)
    project(1)
    keep = pltpu.make_async_copy(own, x_all.at[group], local.at[5])
    keep.start()
    near, far = (xx(-1) * NC + c, xx(1) * NC + c), xx(2) * NC + c
    arrived(half_of(near[0], 0), p_r.at[0], sibling)
    send(half_of(near[0], 0), half_of(near[0], 0), p_s.at[6], p_r.at[6], east)
    arrived(half_of(near[1], 0), p_r.at[2], sibling)
    arrived(half_of(near[1], 1), p_r.at[3], sibling)
    send(half_of(near[1], 1), half_of(near[1], 1), p_s.at[7], p_r.at[7], west)
    send(x_all.at[near[1]], x_all.at[near[1]], p_s.at[9], p_r.at[9], sibling)
    arrived(half_of(near[0], 1), p_r.at[1], sibling)
    send(x_all.at[near[0]], x_all.at[near[0]], p_s.at[8], p_r.at[8], sibling)
    arrived(half_of(far, 0), p_r.at[6], sibling)
    arrived(half_of(far, 1), p_r.at[7], sibling)
    send(x_all.at[far], x_all.at[far], p_s.at[10], p_r.at[10], sibling)
    for h in range(2):
        arrived(half_of(x * NC + 1 - c, h), p_r.at[4 + h], sibling)
    for i, ox in enumerate((-1, 1, 2)):
        arrived(x_all.at[xx(ox) * NC + 1 - c], p_r.at[8 + i], sibling)

    keep.wait()
    arrived(some_rows(yy(2), 0), t_r.at[t0 + 2], sibling)
    arrived(some_rows(yy(2), 1), t_r.at[t0 + 3], sibling)
    for o in range(1, n_group):
        arrived(index_all.at[gg(-o)], i_r.at[o - 1], sibling)
        sent(tile_rows(tiles_all.at[group], y), t_s.at[o - 1], sibling)
        sent(index_all.at[group], i_s.at[o - 1], sibling)
    for i in range(2):
        sent(own_rows(y), t_s.at[t0 + i], sibling)
        sent(some_rows(y, 0), t_s.at[t0 + 2 + i], sibling)
    for i in range(8):
        sent(own.at[0:rows], p_s.at[i], sibling)
    for i in range(8, 11):
        sent(own, p_s.at[i], sibling)
    for core in range(NC):
        @pl.when(c == core)
        def _(core=core):
            if core == 0:
                for o in range(1, NY):
                    sent(up_slice(y, x), y_s.at[o - 1], sibling)
            else:
                for i in range(2):
                    sent(down_block(y, x), y_s.at[i], sibling)
                    sent(some_block(y, x, 0), y_s.at[2 + i], sibling)
            for i in range(6):
                sent(y_part(y, core, 0), v_s.at[i], sibling)
                sent(y_part(y, core, 0), w_s.at[i], sibling)

    @pl.loop(0, moved)
    def _(j):
        @pl.when(c == 0)
        def _():
            for ox in range(1, NX):
                sent(up_slice(y, x), u_s.at[j, ox - 1], sibling)
            for d in range(2):
                for k in range(1, z_hops(d) + 1):
                    sent(up_block(y, z), z_s.at[j, d, k - 1], sibling)
            for i in range(NZ):
                sent(up_block(y, z), b_s.at[j, i], sibling)

        @pl.when(c == 1)
        def _():
            for i in range(2):
                sent(down_block(y, x), x_s.at[j, i], sibling)
                sent(some_block(y, x, 0), x_s.at[j, 2 + i], sibling)
            for i in range(NX):
                sent(down_block(y, x), b_s.at[j, i], sibling)


def encode(up, down, cams, proj, tiles, src, dst, live):
    d, f = up.shape[1:]
    tokens = cams.shape[1]
    channels = proj.shape[1]
    up = up.reshape(NZ, NX // 2, 2 * d // (NZ * NX), f)
    down = down.reshape(NZ, NX, f // (NZ * NX), d)
    tiles = tiles.reshape(NX, NZ, NC, BLK, BLK)
    n = NX * NC
    half = NZ // 2
    moved = NY - 1
    return pl.pallas_call(
        encoder_kernel,
        out_shape=(
            jax.ShapeDtypeStruct((tokens, d), BF),
            jax.ShapeDtypeStruct((n, tokens, channels), BF),
            jax.ShapeDtypeStruct((n, NZ, BLK, BLK), BF),
            jax.ShapeDtypeStruct((n, 8, 128), jnp.int32),
        ),
        in_specs=[ANY, ANY, ANY, VM, ANY, VM, VM, VM],
        out_specs=(VM, ANY, ANY, ANY),
        scratch_shapes=[
            pltpu.VMEM((NY,) + up.shape, BF),
            pltpu.VMEM((NY,) + down.shape, BF),
            pltpu.VMEM((tokens, channels), BF),
            DMA((4,)), DMA((4,)),
            DMA((moved, 4)), DMA((moved, 4)),
            DMA((moved, NX - 1)), DMA((moved, NX - 1)),
            DMA((moved, 2, half)), DMA((moved, 2, half)),
            DMA((moved, max(NZ, NX))), DMA((moved, max(NZ, NX))),
            DMA((n + 3,)), DMA((n + 3,)),
            DMA((n - 1,)), DMA((n - 1,)),
            DMA((11,)), DMA((11,)),
            DMA((6,)), DMA((6,)),
            DMA((6,)), DMA((6,)),
            DMA((6,)),
            pltpu.VMEM((8, 128), jnp.int32),
        ],
        compiler_params=pltpu.CompilerParams(
            collective_id=0, has_side_effects=True, vmem_limit_bytes=VMEM_LIMIT
        ),
    )(up, down, cams, proj, tiles, src, dst, live)


def join_kernel(index, x_all, tiles, grid_out, left, right, parts, s_buf, r_buf, s_sem, r_sem):
    y, x, z, c = where_am_i()
    half = NZ // 2
    n_group = NX * NC
    bev = grid_out.shape[0] // BLK
    chunk = grid_out.shape[0] // 2

    def zz(offset):
        return lax.rem(z + offset + 2 * NZ, NZ)

    beside = (at(y, x, zz(1), c), at(y, x, zz(-1), c))
    greet(beside)

    def hops(ch, d):
        return half if ch == d else half - 1

    def push(ch, d, k):
        send(s_buf.at[ch, d, k - 1], r_buf.at[ch, d, k - 1], s_sem.at[ch, d, k - 1], r_sem.at[ch, d, k - 1], beside[d])

    @pl.loop(0, NZ)
    def _(i):
        off = jnp.where(i == 0, half, jnp.where(i % 2 == 1, (NZ - 1 - i) // 2, -((NZ - i) // 2)))
        target = zz(off)
        p = (x * NZ + target) * NC + c
        for g in range(n_group):
            tile = tiles[g, target].astype(F32)
            dst = index[g, 1, p]
            alive = index[g, 2, p]
            for b in range(bev):
                weight = jnp.where(dst == b, alive, 0).astype(F32)
                left[b * BLK : (b + 1) * BLK, g * BLK : (g + 1) * BLK] = (tile * weight).astype(BF)
            right[g * BLK : (g + 1) * BLK, :] = x_all[g, index[g, 0, p]]
        parts[i] = jnp.dot(left[...], right[...], preferred_element_type=F32)

        @pl.when(i == 0)
        def _():
            for d in range(2):
                s_buf[d, d, 0] = parts[0, d * chunk : (d + 1) * chunk].astype(BF)
                push(d, d, 1)

        for d in range(2):
            if half == 1:
                continue

            @pl.when(i == 1 + d)
            def _(d=d):
                ch = 1 - d
                s_buf[ch, d, 0] = parts[1 + d, ch * chunk : (ch + 1) * chunk].astype(BF)
                push(ch, d, 1)

    for o in range(half - 1, 0, -1):
        for ch_is_d in (True, False):
            for d in range(2):
                ch = d if ch_is_d else 1 - d
                k = hops(ch, d) - o + 1
                if k == 1:
                    continue
                arrived(r_buf.at[ch, d, k - 2], r_sem.at[ch, d, k - 2], beside[d])
                i = NZ - 1 - 2 * o if d == 0 else NZ - 2 * o
                total = parts[i, ch * chunk : (ch + 1) * chunk] + r_buf[ch, d, k - 2].astype(F32)
                s_buf[ch, d, k - 1] = total.astype(BF)
                push(ch, d, k)
    for ch in range(2):
        total = parts[NZ - 1, ch * chunk : (ch + 1) * chunk]
        for d in range(2):
            k = hops(ch, d)
            if k == 0:
                continue
            arrived(r_buf.at[ch, d, k - 1], r_sem.at[ch, d, k - 1], beside[d])
            total = total + r_buf[ch, d, k - 1].astype(F32)
        grid_out[ch * chunk : (ch + 1) * chunk] = total
    for ch in range(2):
        for d in range(2):
            for k in range(hops(ch, d)):
                sent(s_buf.at[ch, d, k], s_sem.at[ch, d, k], beside[d])


def join(index_all, x_all, tiles_all, cells):
    channels = x_all.shape[-1]
    x_all = x_all.reshape(x_all.shape[0], -1, BLK, channels)
    n = NX * NC
    half = NZ // 2
    return pl.pallas_call(
        join_kernel,
        out_shape=jax.ShapeDtypeStruct((cells, channels), F32),
        in_specs=[SM, VM, VM],
        out_specs=VM,
        scratch_shapes=[
            pltpu.VMEM((cells, n * BLK), BF),
            pltpu.VMEM((n * BLK, channels), BF),
            pltpu.VMEM((NZ, cells, channels), F32),
            pltpu.VMEM((2, 2, half, cells // 2, channels), BF),
            pltpu.VMEM((2, 2, half, cells // 2, channels), BF),
            DMA((2, 2, half)), DMA((2, 2, half)),
        ],
        compiler_params=pltpu.CompilerParams(
            collective_id=1, has_side_effects=True, vmem_limit_bytes=VMEM_LIMIT
        ),
    )(index_all, x_all, tiles_all)


def pieces_of(shapes):
    row = 0
    for i, (rows, columns) in enumerate(shapes):
        height = rows // (NX * NY)
        for col in range(0, columns, 256):
            yield i, row, height, col
            row += height


def unpack_kernel(first, second, prediction, *outs):
    for packed, refs in ((first, outs[1:2]), (second, outs[2:])):
        width = packed.shape[3]
        for i, row, height, col in pieces_of([ref.shape for ref in refs]):
            for q in range(NX * NY):
                for core in range(NC):
                    refs[i][q * height : (q + 1) * height, col + core * width : col + (core + 1) * width] = packed[
                        core, q, row : row + height, :
                    ].astype(F32)
    outs[0][...] = prediction[...]


def unpack(first, second, prediction, shapes):
    return pl.pallas_call(
        unpack_kernel,
        out_shape=(jax.ShapeDtypeStruct(prediction.shape, BF),) + tuple(jax.ShapeDtypeStruct(a, F32) for a in shapes),
        in_specs=[VM] * 3,
        out_specs=tuple([VM] * (1 + len(shapes))),
        compiler_params=pltpu.CompilerParams(vmem_limit_bytes=VMEM_LIMIT),
    )(first, second, prediction)


class Total:
    n1, n2, width = NX * NY, NZ, 128

    def __init__(self, ins, out, scratch):
        self.ins, self.out = ins, out
        (
            self.packed, self.from0, self.half, self.from1, self.mid, self.from2, self.mine, self.gathered, self.result,
            self.s0, self.r0, self.s1, self.r1, self.s2, self.r2, self.s3, self.r3, self.s4, self.r4, self.s5, self.r5,
        ) = scratch
        y, x, z, c = where_am_i()
        self.y, self.x, self.z, self.c = y, x, z, c
        self.one, self.two = y * NX + x, z
        self.sibling = at(y, x, z, 1 - c)
        self.real = self.half.shape[1]
        self.share = self.mine.shape[0]

    @classmethod
    def scratch_for(cls, shapes):
        n1, n2, width = NX * NY, NZ, cls.width
        real = sum(a * b for a, b in shapes) // (n1 * NC * width)
        share = -(-real // (n2 * 16)) * 16
        buffers = [
            (NC, n1, real, width), (n1, real, width), (n1, real, width), (n1 - 1, real, width), (share * n2, width),
            (n2 - 1, share, width), (share, width), (share * n2, width), (NC, n1, real, width),
        ]
        counts = [1, n1 - 1, n2 - 1, n2 - 1, n1 - 1, 1]
        return [pltpu.VMEM(b, BF) for b in buffers] + [DMA((n,)) for n in counts for _ in range(2)]

    def dev1(self, q):
        return at(q // NX, q % NX, self.z, self.c)

    def dev2(self, e):
        return at(self.y, self.x, e, self.c)

    def q1(self, o):
        n1 = NX * NY
        return lax.rem(self.one + o + n1, n1)

    def q2(self, o):
        return lax.rem(self.two + o + NZ, NZ)

    def peers(self):
        n1 = NX * NY
        return [self.sibling] + [self.dev1(self.q1(o)) for o in range(1, n1)] + [self.dev2(self.q2(o)) for o in range(1, NZ)]

    def pieces(self):
        return pieces_of([ref.shape for ref in self.ins])

    def start(self):
        n1 = NX * NY

        @pl.loop(0, n1)
        def _(q):
            for i, row, height, col in self.pieces():
                for core in range(NC):
                    left = col + core * self.width
                    self.packed[core, q, row : row + height, :] = self.ins[i][
                        pl.ds(pl.multiple_of(q * height, height), height), left : left + self.width
                    ].astype(BF)
        send(self.packed.at[1 - self.c], self.from0, self.s0.at[0], self.r0.at[0], self.sibling)
        self.mid[...] = jnp.zeros_like(self.mid)

    def over_xy(self):
        n1 = NX * NY
        arrived(self.from0, self.r0.at[0], self.sibling)

        @pl.loop(0, n1)
        def _(o):
            q = lax.rem(self.one + 1 + o, n1)
            self.half[q] = (self.packed[self.c, q].astype(F32) + self.from0[q].astype(F32)).astype(BF)

            @pl.when(o < n1 - 1)
            def _():
                send(self.half.at[q], self.from1.at[o], self.s1.at[o], self.r1.at[o], self.dev1(q))

    def part(self, ref, e):
        return ref.at[pl.ds(pl.multiple_of(e * self.share, self.share), self.share), :]

    def over_z(self):
        total = self.half[self.one].astype(F32)
        for o in range(NX * NY - 1):
            arrived(self.from1.at[o], self.r1.at[o], self.sibling)
            total = total + self.from1[o].astype(F32)
        self.mid[0 : self.real, :] = total.astype(BF)
        for o in range(1, NZ):
            e = self.q2(o)
            send(self.part(self.mid, e), self.from2.at[o - 1], self.s2.at[o - 1], self.r2.at[o - 1], self.dev2(e))

    def back_over_z(self):
        total = self.mid[pl.ds(pl.multiple_of(self.two * self.share, self.share), self.share), :].astype(F32)
        for o in range(1, NZ):
            arrived(self.from2.at[o - 1], self.r2.at[o - 1], self.sibling)
            total = total + self.from2[o - 1].astype(F32)
        self.mine[...] = total.astype(BF)
        for o in range(1, NZ):
            send(self.mine, self.part(self.gathered, self.two), self.s3.at[o - 1], self.r3.at[o - 1], self.dev2(self.q2(o)))
        self.gathered[pl.ds(pl.multiple_of(self.two * self.share, self.share), self.share), :] = self.mine[...]

    def back_over_xy(self):
        for o in range(1, NZ):
            arrived(self.part(self.gathered, self.q2(-o)), self.r3.at[o - 1], self.sibling)
        for o in range(1, NX * NY):
            send(
                self.gathered.at[0 : self.real, :], self.result.at[self.c, self.one],
                self.s4.at[o - 1], self.r4.at[o - 1], self.dev1(self.q1(o)),
            )
        self.result[self.c, self.one] = self.gathered[0 : self.real, :]

    def back_over_core(self):
        for o in range(1, NX * NY):
            arrived(self.result.at[self.c, self.q1(-o)], self.r4.at[o - 1], self.sibling)
        send(self.result.at[self.c], self.result.at[self.c], self.s5.at[0], self.r5.at[0], self.sibling)

    def finish(self):
        n1 = NX * NY
        arrived(self.result.at[1 - self.c], self.r5.at[0], self.sibling)

        self.out[...] = self.result[...]
        sent(self.from0, self.s0.at[0], self.sibling)
        sent(self.result.at[self.c], self.s5.at[0], self.sibling)
        for o in range(n1 - 1):
            sent(self.half.at[0], self.s1.at[o], self.sibling)
            sent(self.half.at[0], self.s4.at[o], self.sibling)
        for o in range(NZ - 1):
            sent(self.mine, self.s2.at[o], self.sibling)
            sent(self.mine, self.s3.at[o], self.sibling)


N_GRADS = 4


def gelu_parts(v):
    inner = math.sqrt(2.0 / math.pi) * (v + 0.044715 * v * v * v)
    slope = math.sqrt(2.0 / math.pi) * (1.0 + 3.0 * 0.044715 * v * v)
    t = jnp.tanh(inner)
    return 0.5 * v * (1.0 + t), 0.5 * (1.0 + t) + 0.5 * v * (1.0 - t * t) * slope


def split_kernel(index, grid, pred_grad, tiles, encoded, ru, rd, du, dd, *refs, scale):
    prediction, proj_out, out, refs = refs[0], refs[1], refs[2], refs[3:]
    all_grad, here, left, acc, core_s, core_r, x_send, x_recv, z_s, z_r, c_s, c_r, x_s, x_r = refs[:14]
    kept = refs[14:22]
    ins = refs[22 : 22 + N_GRADS]
    rows_out, grad_proj = refs[22 + N_GRADS : 24 + N_GRADS]
    refs = refs[24 + N_GRADS :]
    total = Total(ins, out, refs[: len(refs) // 2])
    last = Total([grad_proj], proj_out, refs[len(refs) // 2 :])
    grad = pred_grad
    y, x, z, c = where_am_i()
    half = NZ // 2
    n_group = NX * NC
    chunk = grad.shape[0] // 2
    cam = rows_out.shape[0] // BLK
    sibling = at(y, x, z, 1 - c)

    def zz(offset):
        return lax.rem(z + offset + 2 * NZ, NZ)

    def xx(offset):
        return lax.rem(x + offset + NX, NX)

    beside = (at(y, x, zz(1), c), at(y, x, zz(-1), c))
    east, west = at(y, xx(1), z, c), at(y, xx(-1), z, c)
    barrier = pltpu.get_barrier_semaphore()
    for device in total.peers():
        pl.semaphore_signal(barrier, inc=1, device_id=device, device_id_type=MESH)

    def hops(ch, d):
        return half if ch == d else half - 1

    def part(origin, ch):
        return all_grad.at[origin, pl.ds(ch * chunk, chunk)]

    n1_ref, h1_ref, n2_ref, h2_ref, p1_ref, p2_ref, r1_ref, r2_ref = kept

    def heads(ch):
        r = slice(ch * chunk, (ch + 1) * chunk)

        def forward(state, w_up, w_down, n_ref, h_ref):
            scaling = lax.rsqrt(jnp.mean(state * state, axis=-1, keepdims=True) + eps)
            normed = (state * scaling).astype(BF)
            n_ref[r] = normed
            preact = jnp.dot(normed, w_up[...], preferred_element_type=F32)
            value, slope = gelu_parts(preact)
            hidden = value.astype(BF)
            h_ref[r] = hidden
            return state + jnp.dot(hidden, w_down[...], preferred_element_type=F32), scaling, slope

        def backward(g, state, scaling, slope, w_up, w_down, p_ref, r_ref):
            rounded = g.astype(BF)
            r_ref[r] = rounded
            grad_pre = (against_rows(rounded, w_down[...]) * slope).astype(BF)
            p_ref[r] = grad_pre
            grad_normed = against_rows(grad_pre, w_up[...])
            unit = state * scaling
            return g + scaling * (grad_normed - unit * jnp.mean(grad_normed * unit, axis=-1, keepdims=True))

        s0 = grid[r]
        s1, scale1, slope1 = forward(s0, ru, rd, n1_ref, h1_ref)
        s2, scale2, slope2 = forward(s1, du, dd, n2_ref, h2_ref)
        prediction[r] = s2.astype(BF)
        g1 = backward(pred_grad[r].astype(F32) * scale, s1, scale2, slope2, du, dd, p2_ref, r2_ref)
        g0 = backward(g1, s0, scale1, slope1, ru, rd, p1_ref, r1_ref)
        all_grad[z, r] = g0.astype(BF)

    for ch in range(2):
        heads(ch)
        if ch == 0:
            pl.semaphore_wait(barrier, len(total.peers()))
        for d in range(2):
            if hops(ch, d) >= 1:
                send(part(z, ch), part(z, ch), z_s.at[ch, d, 0], z_r.at[ch, d, 0], beside[d])
    ins[0][...] = contract_rows(n1_ref[...], p1_ref[...])
    ins[1][...] = contract_rows(h1_ref[...], r1_ref[...])
    ins[2][...] = contract_rows(n2_ref[...], p2_ref[...])
    ins[3][...] = contract_rows(h2_ref[...], r2_ref[...])
    total.start()

    def use(origin, first):
        p = (x * NZ + origin) * NC + c
        here[...] = all_grad[origin].reshape(here.shape)
        for g in range(n_group):
            tile = tiles[g, origin].astype(F32).T
            src = index[g, 0, p]
            alive = index[g, 2, p]
            for k in range(cam):
                weight = jnp.where(src == k, alive, 0).astype(F32)
                left[k * BLK : (k + 1) * BLK, :] = (tile * weight).astype(BF)
            product = jnp.dot(left[...], here[index[g, 1, p]], preferred_element_type=F32)
            if first:
                acc[g] = product
            else:
                acc[g] = acc[g] + product

    use(z, True)
    total.over_xy()

    @pl.loop(1, half + 1)
    def _(k):
        for d in range(2):
            s = 1 - 2 * d
            origin = zz(-s * k)
            for ch in range(2):
                @pl.when(k <= hops(ch, d))
                def _(ch=ch, d=d):
                    arrived(part(origin, ch), z_r.at[ch, d, k - 1], beside[d])

                @pl.when(k + 1 <= hops(ch, d))
                def _(ch=ch, d=d):
                    send(part(origin, ch), part(origin, ch), z_s.at[ch, d, k], z_r.at[ch, d, k], beside[d])

        @pl.when(k == max(half - 2, 1))
        def _():
            total.over_z()

        @pl.when(k == max(half - 1, 1))
        def _():
            total.back_over_z()

        @pl.when(k == half)
        def _():
            total.back_over_xy()

        use(zz(-k), False)

        @pl.when(k < half)
        def _():
            use(zz(k), False)

    rows = rows_out.shape[0] // 2
    order = (2, 1, NX - 1, 0)
    for i, o in enumerate(order):
        core_s[i] = acc[xx(o) * NC + 1 - c].astype(BF)
        send(core_s.at[i], core_r.at[i], c_s.at[i], c_r.at[i], sibling)

    def pair_sum(i, h):
        return acc[xx(order[i]) * NC + c, h * rows : (h + 1) * rows, :] + core_r[
            i, h * rows : (h + 1) * rows, :
        ].astype(F32)

    def push(n, value, device):
        x_send[n] = value.astype(BF)
        send(x_send.at[n], x_recv.at[n], x_s.at[n], x_r.at[n], device)

    for i in range(3):
        arrived(core_r.at[i], c_r.at[i], sibling)
        if i == 0:
            push(0, pair_sum(0, 0), east)
            push(1, pair_sum(0, 1), west)
        if i == 1:
            push(2, pair_sum(1, 1), east)
        if i == 2:
            push(3, pair_sum(2, 0), west)
    arrived(x_recv.at[0], x_r.at[0], sibling)
    push(4, pair_sum(1, 0) + x_recv[0].astype(F32), east)
    arrived(x_recv.at[1], x_r.at[1], sibling)
    push(5, pair_sum(2, 1) + x_recv[1].astype(F32), west)
    arrived(core_r.at[3], c_r.at[3], sibling)
    for n in range(2, 6):
        arrived(x_recv.at[n], x_r.at[n], sibling)
    rows_out[0:rows] = (pair_sum(3, 0) + x_recv[4].astype(F32) + x_recv[3].astype(F32)).astype(BF)
    rows_out[rows : 2 * rows] = (pair_sum(3, 1) + x_recv[2].astype(F32) + x_recv[5].astype(F32)).astype(BF)
    grad_proj[...] = contract_rows(encoded[...], rows_out[...])
    last.start()
    total.back_over_core()
    last.over_xy()
    total.finish()
    last.over_z()
    last.back_over_z()
    last.back_over_xy()
    last.back_over_core()
    last.finish()
    for i in range(4):
        sent(core_s.at[i], c_s.at[i], sibling)
    for n in range(6):
        sent(x_send.at[n], x_s.at[n], sibling)
    for ch in range(2):
        for d in range(2):
            for k in range(hops(ch, d)):
                sent(part(z, ch), z_s.at[ch, d, k], beside[d])


def split(index_all, grid, pred_grad, tiles_all, encoded, weights, scale):
    cells, channels = grid.shape
    tokens, features = encoded.shape
    hidden = weights[0].shape[1]
    n = NX * NC
    half = NZ // 2
    shapes = [w.shape for w in weights]

    def packed_of(some):
        rows = sum(a * b for a, b in some) // (NX * NY * NC * Total.width)
        return jax.ShapeDtypeStruct((NC, NX * NY, rows, Total.width), BF)

    return pl.pallas_call(
        functools.partial(split_kernel, scale=scale),
        out_shape=(
            jax.ShapeDtypeStruct((cells, channels), BF),
            packed_of([(features, channels)]),
            packed_of(shapes),
        ),
        in_specs=[SM, VM, VM, VM, VM] + [VM] * N_GRADS,
        out_specs=(VM, VM, VM),
        scratch_shapes=[
            pltpu.VMEM((NZ, cells, channels), BF),
            pltpu.VMEM((cells // BLK, BLK, channels), BF),
            pltpu.VMEM((tokens, BLK), BF),
            pltpu.VMEM((n, tokens, channels), F32),
            pltpu.VMEM((NX, tokens, channels), BF),
            pltpu.VMEM((NX, tokens, channels), BF),
            pltpu.VMEM((6, tokens // 2, channels), BF),
            pltpu.VMEM((6, tokens // 2, channels), BF),
            DMA((2, 2, half)), DMA((2, 2, half)),
            DMA((NX,)), DMA((NX,)),
            DMA((6,)), DMA((6,)),
        ]
        + [pltpu.VMEM((cells, w), BF) for w in (channels, hidden) * 2 + (hidden, hidden, channels, channels)]
        + [pltpu.VMEM(a, F32) for a in shapes]
        + [pltpu.VMEM((tokens, channels), BF), pltpu.VMEM((features, channels), F32)]
        + Total.scratch_for(shapes)
        + Total.scratch_for([(features, channels)]),
        compiler_params=pltpu.CompilerParams(
            collective_id=2, has_side_effects=True, vmem_limit_bytes=VMEM_LIMIT
        ),
    )(index_all, grid, pred_grad, tiles_all, encoded, *weights)


def on_device(
    cams, vit_up, vit_down, proj, frustum_tiles, src_block, dst_block, live,
    render_up, render_down, decode_up, decode_down, pred_grad,
):
    tile_count = NX * NZ * NC
    cells, channels = pred_grad.shape[1:]
    encoded, x_all, tiles_all, index_all = encode(
        vit_up, vit_down, cams, proj, frustum_tiles[0], src_block, dst_block, live
    )
    bev_grid = join(index_all, x_all, tiles_all, cells)
    scale = 1.0 / math.sqrt(cams.shape[0] * cells * tile_count)
    weights = (render_up, render_down, decode_up, decode_down)
    prediction, first, second = split(index_all, bev_grid, pred_grad[0], tiles_all, encoded, weights, scale)
    prediction, *totals = unpack(first, second, prediction, [proj.shape] + [w.shape for w in weights])
    return (prediction[None], *totals)


def solution(mesh):
    placed = (
        P(None, "tile", None),
        P("section", None, None),
        P("section", None, None),
        P(),
        P("tile", None, None, None),
        P("tile", None),
        P("tile", None),
        P("tile", None),
        P(),
        P(),
        P(),
        P(),
        P("section", "tile", None),
    )
    return jax.shard_map(
        on_device,
        mesh=mesh,
        in_specs=placed,
        out_specs=(P("section", "tile", None), P(), P(), P(), P(), P()),
        check_vma=False,
    )
```

```python
import functools
import math

import jax
import jax.numpy as jnp
from jax import lax
from jax.experimental import pallas as pl
from jax.experimental.pallas import tpu as pltpu
from jax.sharding import PartitionSpec as P

eps = 1e-05
MESH = pl.DeviceIdType.MESH
BF = jnp.bfloat16
F32 = jnp.float32
NY, NX, NZ, NC = 4, 4, 8, 2
BLK = 128
VMEM_LIMIT = 60 * 2**20
ANY = pl.BlockSpec(memory_space=pl.ANY)
VM = pl.BlockSpec(memory_space=pltpu.VMEM)
SM = pl.BlockSpec(memory_space=pltpu.SMEM)
DMA = pltpu.SemaphoreType.DMA


def where_am_i():
    y = lax.axis_index("section")
    t = lax.axis_index("tile")
    return y, t // (NZ * NC), (t // NC) % NZ, t % NC


def at(y, x, z, c):
    return (y, (x * NZ + z) * NC + c)


def send(src, dst, ssem, rsem, device):
    copy = pltpu.make_async_remote_copy(
        src_ref=src, dst_ref=dst, send_sem=ssem, recv_sem=rsem, device_id=device, device_id_type=MESH
    )
    copy.start()


def sent(src, ssem, device):
    pltpu.make_async_remote_copy(
        src_ref=src, dst_ref=src, send_sem=ssem, recv_sem=ssem, device_id=device, device_id_type=MESH
    ).wait_send()


def arrived(dst, rsem, device):
    pltpu.make_async_remote_copy(
        src_ref=dst, dst_ref=dst, send_sem=rsem, recv_sem=rsem, device_id=device, device_id_type=MESH
    ).wait_recv()


def greet(devices):
    barrier = pltpu.get_barrier_semaphore()
    for device in devices:
        pl.semaphore_signal(barrier, inc=1, device_id=device, device_id_type=MESH)
    pl.semaphore_wait(barrier, len(devices))


def gelu(v):
    return 0.5 * v * (1.0 + jnp.tanh(math.sqrt(2.0 / math.pi) * (v + 0.044715 * v * v * v)))


def contract_rows(left, right):
    return lax.dot_general(left, right, (((0,), (0,)), ((), ())), preferred_element_type=F32)


def against_rows(left, right):
    return lax.dot_general(left, right, (((1,), (1,)), ((), ())), preferred_element_type=F32)


def encoder_kernel(
    up, down, cams, proj, tiles, src, dst, live,
    encoded, x_all, tiles_all, index_all,
    w_up, w_down, own, y_s, y_r, x_s, x_r, u_s, u_r, z_s, z_r, b_s, b_r, t_s, t_r, i_s, i_r, p_s, p_r, v_s, v_r, w_s, w_r,
    local, index,
):
    y, x, z, c = where_am_i()
    sibling = at(y, x, z, 1 - c)
    group = x * NC + c
    moved = NY - 1
    half = NZ // 2
    steps = half + 1
    n_group = NX * NC
    plane_up, plane_down = 2 * w_up.shape[-1] // 3, 2 * w_down.shape[-1] // 3
    cols = plane_up // 2
    quarter = BLK // NY

    def layer_of(j):
        return j + jnp.where(j >= y, 1, 0)

    def up_slice(l, xx):
        return w_up.at[l, z, xx // 2, :, pl.ds(pl.multiple_of((xx % 2) * cols, 128), cols)]

    def up_block(l, zo):
        return w_up.at[l, zo, :, :, pl.ds(0, plane_up)]

    def down_slice(l, zo):
        return w_down.at[l, zo, x, :, pl.ds(0, plane_down)]

    def down_block(l, xo):
        return w_down.at[l, :, xo, :, pl.ds(0, plane_down)]

    def y_part(l, core, h):
        if core == 0:
            width = (w_up.shape[-1] - plane_up) // 2
            return w_up.at[l, :, :, :, pl.ds(plane_up + h * width, width)]
        return w_down.at[l, pl.ds(h * half, half), :, :, pl.ds(plane_down, w_down.shape[-1] - plane_down)]

    def zz(offset):
        return lax.rem(z + offset + 2 * NZ, NZ)

    def xx(offset):
        return lax.rem(x + offset + NX, NX)

    def yy(offset):
        return lax.rem(y + offset + NY, NY)

    def gg(offset):
        return lax.rem(group + offset + n_group, n_group)

    def g_dev(g):
        return at(y, g // NC, z, g % NC)

    east, west = at(y, xx(1), z, c), at(y, xx(-1), z, c)
    north, south = at(yy(1), x, z, c), at(yy(-1), x, z, c)

    def tile_rows(ref, section):
        return ref.at[:, pl.ds(pl.multiple_of(section * quarter, quarter), quarter), :]

    index[...] = jnp.zeros_like(index)
    for i, ref in enumerate((src, dst, live)):
        index[i : i + 1, 0 : ref.shape[1]] = ref[...]
    loads = [
        pltpu.make_async_copy(up, w_up.at[y], local.at[0]),
        pltpu.make_async_copy(down, w_down.at[y], local.at[1]),
        pltpu.make_async_copy(cams.at[y], encoded, local.at[2]),
        pltpu.make_async_copy(tile_rows(tiles.at[x, :, c], y), tile_rows(tiles_all.at[group], y), local.at[3]),
        pltpu.make_async_copy(index, index_all.at[group], local.at[4]),
    ]
    for load in loads:
        load.start()
    greet(
        [at(yy(o), x, z, c) for o in range(1, NY)]
        + [g_dev(gg(o)) for o in range(1, n_group)]
        + [at(y, x, zz(o), c) for o in ((1, -1, 2, -2) if NZ == 8 else (1, -1))]
    )
    for load in loads[:3]:
        load.wait()

    def share(l, core):
        return up_slice(l, x) if core == 0 else down_slice(l, z)

    for core in range(NC):
        @pl.when(c == core)
        def _(core=core):
            for o in range(1, NY):
                send(share(y, core), share(y, core), y_s.at[o - 1], y_r.at[o - 1], at(yy(o), x, z, c))
            for h, i, device in ((0, 0, north), (1, 3, south), (1, 1, north), (0, 2, south)):
                send(y_part(y, core, h), y_part(y, core, h), v_s.at[i], v_r.at[i], device)

    def sign(j, d):
        return (1 - 2 * (j % 2)) * (1 - 2 * d)

    def send_tiles():
        for o in range(1, n_group):
            g = gg(o)
            send(index, index_all.at[group], i_s.at[o - 1], i_r.at[o - 1], g_dev(g))
            send(
                tile_rows(tiles.at[g // NC, :, g % NC], y), tile_rows(tiles_all.at[group], y),
                t_s.at[o - 1], t_r.at[o - 1], g_dev(g),
            )

    first_hops = (1, -1, 2, -2) if NZ == 8 else tuple(range(1, NZ))
    later_hops = ((4, 1, 2), (5, 2, 2), (6, -1, -2)) if NZ == 8 else ()

    def sem_of(sems, j, i):
        return sems.at[j, i // half, i % half]

    def slice_to(j, l, i, off, origin):
        s = sign(j, 0)
        block = down_slice(l, zz(-s * origin))
        send(block, block, sem_of(z_s, j, i), sem_of(z_r, j, i), at(y, x, zz(s * off), c))

    def slices_arrived(j, l):
        s = sign(j, 0)
        for i, off in enumerate(first_hops):
            if off not in [origin for _, _, origin in later_hops]:
                arrived(down_slice(l, zz(-s * off)), sem_of(z_r, j, i), sibling)
        for i, off, origin in later_hops:
            arrived(down_slice(l, zz(-s * (off + origin))), sem_of(z_r, j, i), sibling)

    @pl.when(c == 0)
    def _():
        @pl.loop(0, moved)
        def _(j):
            l = layer_of(j)
            o = yy(-l)
            arrived(share(l, 0), y_r.at[o - 1], sibling)
            for ox in range(1, NX):
                send(up_slice(l, x), up_slice(l, x), u_s.at[j, ox - 1], u_r.at[j, ox - 1], at(y, xx(ox), z, c))
        send_tiles()

    def z_hops(d):
        return half if d == 0 else half - 1

    @pl.when(c == 1)
    def _():
        @pl.loop(0, moved)
        def _(j):
            l = layer_of(j)
            arrived(share(l, 1), y_r.at[yy(-l) - 1], sibling)
            for i, off in enumerate(first_hops):
                slice_to(j, l, i, off, 0)
        send_tiles()

        @pl.loop(0, moved)
        def _(j):
            l = layer_of(j)
            for i, off, origin in later_hops:
                if i != 5:
                    first = first_hops.index(origin)
                    arrived(down_slice(l, zz(-sign(j, 0) * origin)), sem_of(z_r, j, first), sibling)
                slice_to(j, l, i, off, origin)

    def layer_rows(l, r, rows):
        wide = encoded[pl.ds(r, rows), :].astype(F32)
        scaling = lax.rsqrt(jnp.mean(wide * wide, axis=-1, keepdims=True) + eps)
        normed = (wide * scaling).astype(BF)
        total = wide
        parts = 2
        for q in range(parts):
            width = w_up.shape[-1] // parts
            w1 = w_up[l, :, :, :, q * width : (q + 1) * width].reshape(wide.shape[1], width)
            hidden = gelu(jnp.dot(normed, w1, preferred_element_type=F32)).astype(BF)
            nz = NZ // parts
            w2 = w_down[l, q * nz : (q + 1) * nz].reshape(width, wide.shape[1])
            total = total + jnp.dot(hidden, w2, preferred_element_type=F32)
        encoded[pl.ds(r, rows), :] = total.astype(BF)

    tokens = encoded.shape[0]
    rows = tokens // 2

    def wait_sibling(j):
        l = layer_of(j)

        @pl.when(c == 0)
        def _():
            for i, ox in enumerate((0, 1, NX - 1, 2)):
                arrived(down_block(l, xx(-ox)), b_r.at[j, i], sibling)

        @pl.when(c == 1)
        def _():
            arrived(up_block(l, z), b_r.at[j, 0], sibling)
            for d in range(2):
                for k in range(2, z_hops(d) + 2):
                    arrived(up_block(l, zz(-sign(j, d) * (k - 1))), b_r.at[j, 1 + d * half + k - 2], sibling)

    def second_half(l, xo, h):
        return w_down.at[l, pl.ds(h * half, half), xo, :, pl.ds(0, plane_down)]

    def begin(j):
        l = layer_of(j)

        @pl.when(c == 0)
        def _():
            for ox in range(1, NX):
                arrived(up_slice(l, xx(-ox)), u_r.at[j, ox - 1], sibling)
            block = up_block(l, z)
            for d in range(2):
                if z_hops(d) >= 1:
                    send(block, block, z_s.at[j, d, 0], z_r.at[j, d, 0], at(y, x, zz(sign(j, d)), c))
            send(block, block, b_s.at[j, 0], b_r.at[j, 0], sibling)

        @pl.when(c == 1)
        def _():
            slices_arrived(j, l)
            block = down_block(l, x)
            send(block, block, x_s.at[j, 0], x_r.at[j, 0], east)
            send(block, block, x_s.at[j, 1], x_r.at[j, 1], west)
            send(block, block, b_s.at[j, 0], b_r.at[j, 0], sibling)

    def own_rows(section):
        return tiles_all.at[:, :, pl.ds(pl.multiple_of(section * quarter, quarter), quarter), :]

    def some_rows(section, h):
        return tiles_all.at[
            pl.ds(h * n_group // 2, n_group // 2), :, pl.ds(pl.multiple_of(section * quarter, quarter), quarter), :
        ]

    t0 = n_group - 1

    def y_piece(i):
        return (yy(-1), yy(-1), yy(1), yy(1), yy(2), yy(2))[i], (0, 1, 0, 1, 0, 1)[i]

    def take_y(i):
        l, h = y_piece(i)
        for core in range(NC):
            @pl.when(c == core)
            def _(core=core):
                piece = y_part(l, core, h)
                arrived(piece, v_r.at[i], sibling)
                if i == 0:
                    send(piece, piece, v_s.at[4], v_r.at[4], north)
                if i == 3:
                    send(piece, piece, v_s.at[5], v_r.at[5], south)
                send(piece, piece, w_s.at[i], w_r.at[i], sibling)

    last = max(steps, 5)

    @pl.loop(1, moved - 1 + last + 1)
    def _(slot):
        @pl.loop(0, moved)
        def _(j):
            k = slot - j
            l = layer_of(j)

            @pl.when(jnp.logical_and(c == 0, k >= 2))
            def _():
                for d in range(2):
                    s = sign(j, d)
                    block = up_block(l, zz(-s * (k - 1)))

                    @pl.when(k <= z_hops(d) + 1)
                    def _():
                        arrived(block, z_r.at[j, d, k - 2], sibling)

                        @pl.when(k <= z_hops(d))
                        def _():
                            send(block, block, z_s.at[j, d, k - 1], z_r.at[j, d, k - 1], at(y, x, zz(s), c))

                        send(block, block, b_s.at[j, 1 + d * half + k - 2], b_r.at[j, 1 + d * half + k - 2], sibling)

            @pl.when(jnp.logical_and(c == 1, k == 3))
            def _():
                block = down_block(l, xx(-1))
                arrived(block, x_r.at[j, 0], sibling)
                send(second_half(l, xx(-1), 0), second_half(l, xx(-1), 0), x_s.at[j, 2], x_r.at[j, 2], east)
                send(block, block, b_s.at[j, 1], b_r.at[j, 1], sibling)
                other = down_block(l, xx(1))
                arrived(other, x_r.at[j, 1], sibling)
                send(second_half(l, xx(1), 1), second_half(l, xx(1), 1), x_s.at[j, 3], x_r.at[j, 3], west)
                send(other, other, b_s.at[j, 2], b_r.at[j, 2], sibling)

            @pl.when(jnp.logical_and(c == 1, k == last))
            def _():
                arrived(second_half(l, xx(2), 0), x_r.at[j, 2], sibling)
                arrived(second_half(l, xx(2), 1), x_r.at[j, 3], sibling)
                block = down_block(l, xx(2))
                send(block, block, b_s.at[j, 3], b_r.at[j, 3], sibling)

            @pl.when(k == 1)
            def _():
                begin(j)

        for when, pieces in ((1, (0, 3)), (3, (1, 2)), (5, (4, 5))):
            @pl.when(slot == when)
            def _(pieces=pieces):
                for i in pieces:
                    take_y(i)

        @pl.when(slot == last)
        def _():
            for load in loads[3:]:
                load.wait()
            for o in range(1, n_group):
                arrived(tile_rows(tiles_all.at[gg(-o)], y), t_r.at[o - 1], sibling)
            send(own_rows(y), own_rows(y), t_s.at[t0], t_r.at[t0], north)
            send(own_rows(y), own_rows(y), t_s.at[t0 + 1], t_r.at[t0 + 1], south)

        @pl.when(slot == last + 1)
        def _():
            for i in range(6):
                l, h = y_piece(i)
                for core in range(NC):
                    @pl.when(c != core)
                    def _(core=core):
                        arrived(y_part(l, core, h), w_r.at[i], sibling)

        @pl.when(slot > last)
        def _():
            wait_sibling(slot - last - 1)
            layer_rows(slot - last - 1, 0, tokens)

    wait_sibling(moved - 1)

    layer_rows(NY - 2, 0, tokens)

    arrived(own_rows(yy(-1)), t_r.at[t0], sibling)
    send(some_rows(yy(-1), 0), some_rows(yy(-1), 0), t_s.at[t0 + 2], t_r.at[t0 + 2], north)
    arrived(own_rows(yy(1)), t_r.at[t0 + 1], sibling)
    send(some_rows(yy(1), 1), some_rows(yy(1), 1), t_s.at[t0 + 3], t_r.at[t0 + 3], south)
    layer_rows(NY - 1, 0, rows)

    def half_of(g, h):
        return x_all.at[g, pl.ds(h * rows, rows), :]

    def project(h):
        mine = own.at[h * rows : (h + 1) * rows]
        mine[...] = jnp.dot(encoded[h * rows : (h + 1) * rows], proj[...], preferred_element_type=F32).astype(BF)
        send(mine, half_of(group, h), p_s.at[h], p_r.at[h], east)
        send(mine, half_of(group, h), p_s.at[2 + h], p_r.at[2 + h], west)
        send(mine, half_of(group, h), p_s.at[4 + h], p_r.at[4 + h], sibling)

    project(0)
    layer_rows(NY - 1, rows, rows)
    project(1)
    keep = pltpu.make_async_copy(own, x_all.at[group], local.at[5])
    keep.start()
    near, far = (xx(-1) * NC + c, xx(1) * NC + c), xx(2) * NC + c
    arrived(half_of(near[0], 0), p_r.at[0], sibling)
    send(half_of(near[0], 0), half_of(near[0], 0), p_s.at[6], p_r.at[6], east)
    arrived(half_of(near[1], 0), p_r.at[2], sibling)
    arrived(half_of(near[1], 1), p_r.at[3], sibling)
    send(half_of(near[1], 1), half_of(near[1], 1), p_s.at[7], p_r.at[7], west)
    send(x_all.at[near[1]], x_all.at[near[1]], p_s.at[9], p_r.at[9], sibling)
    arrived(half_of(near[0], 1), p_r.at[1], sibling)
    send(x_all.at[near[0]], x_all.at[near[0]], p_s.at[8], p_r.at[8], sibling)
    arrived(half_of(far, 0), p_r.at[6], sibling)
    arrived(half_of(far, 1), p_r.at[7], sibling)
    send(x_all.at[far], x_all.at[far], p_s.at[10], p_r.at[10], sibling)
    for h in range(2):
        arrived(half_of(x * NC + 1 - c, h), p_r.at[4 + h], sibling)
    for i, ox in enumerate((-1, 1, 2)):
        arrived(x_all.at[xx(ox) * NC + 1 - c], p_r.at[8 + i], sibling)

    keep.wait()
    arrived(some_rows(yy(2), 0), t_r.at[t0 + 2], sibling)
    arrived(some_rows(yy(2), 1), t_r.at[t0 + 3], sibling)
    for o in range(1, n_group):
        arrived(index_all.at[gg(-o)], i_r.at[o - 1], sibling)
        sent(tile_rows(tiles_all.at[group], y), t_s.at[o - 1], sibling)
        sent(index_all.at[group], i_s.at[o - 1], sibling)
    for i in range(2):
        sent(own_rows(y), t_s.at[t0 + i], sibling)
        sent(some_rows(y, 0), t_s.at[t0 + 2 + i], sibling)
    for i in range(8):
        sent(own.at[0:rows], p_s.at[i], sibling)
    for i in range(8, 11):
        sent(own, p_s.at[i], sibling)
    for core in range(NC):
        @pl.when(c == core)
        def _(core=core):
            for o in range(1, NY):
                sent(share(y, core), y_s.at[o - 1], sibling)
            for i in range(6):
                sent(y_part(y, core, 0), v_s.at[i], sibling)
                sent(y_part(y, core, 0), w_s.at[i], sibling)

    @pl.loop(0, moved)
    def _(j):
        @pl.when(c == 0)
        def _():
            for ox in range(1, NX):
                sent(up_slice(y, x), u_s.at[j, ox - 1], sibling)
            for d in range(2):
                for k in range(1, z_hops(d) + 1):
                    sent(up_block(y, z), z_s.at[j, d, k - 1], sibling)
            for i in range(NZ):
                sent(up_block(y, z), b_s.at[j, i], sibling)

        @pl.when(c == 1)
        def _():
            for i in range(2):
                sent(down_block(y, x), x_s.at[j, i], sibling)
                sent(second_half(y, x, 0), x_s.at[j, 2 + i], sibling)
            for i in range(NZ - 1):
                sent(down_slice(y, z), sem_of(z_s, j, i), sibling)
            for i in range(NX):
                sent(down_block(y, x), b_s.at[j, i], sibling)


def encode(up, down, cams, proj, tiles, src, dst, live):
    d, f = up.shape[1:]
    tokens = cams.shape[1]
    channels = proj.shape[1]
    up = up.reshape(NZ, NX // 2, 2 * d // (NZ * NX), f)
    down = down.reshape(NZ, NX, f // (NZ * NX), d)
    tiles = tiles.reshape(NX, NZ, NC, BLK, BLK)
    n = NX * NC
    half = NZ // 2
    moved = NY - 1
    return pl.pallas_call(
        encoder_kernel,
        out_shape=(
            jax.ShapeDtypeStruct((tokens, d), BF),
            jax.ShapeDtypeStruct((n, tokens, channels), BF),
            jax.ShapeDtypeStruct((n, NZ, BLK, BLK), BF),
            jax.ShapeDtypeStruct((n, 8, 128), jnp.int32),
        ),
        in_specs=[ANY, ANY, ANY, VM, ANY, VM, VM, VM],
        out_specs=(VM, ANY, ANY, ANY),
        scratch_shapes=[
            pltpu.VMEM((NY,) + up.shape, BF),
            pltpu.VMEM((NY,) + down.shape, BF),
            pltpu.VMEM((tokens, channels), BF),
            DMA((NY - 1,)), DMA((NY - 1,)),
            DMA((moved, 4)), DMA((moved, 4)),
            DMA((moved, NX - 1)), DMA((moved, NX - 1)),
            DMA((moved, 2, half)), DMA((moved, 2, half)),
            DMA((moved, max(NZ, NX))), DMA((moved, max(NZ, NX))),
            DMA((n + 3,)), DMA((n + 3,)),
            DMA((n - 1,)), DMA((n - 1,)),
            DMA((11,)), DMA((11,)),
            DMA((6,)), DMA((6,)),
            DMA((6,)), DMA((6,)),
            DMA((6,)),
            pltpu.VMEM((8, 128), jnp.int32),
        ],
        compiler_params=pltpu.CompilerParams(
            collective_id=0, has_side_effects=True, vmem_limit_bytes=VMEM_LIMIT
        ),
    )(up, down, cams, proj, tiles, src, dst, live)


def join_kernel(index, x_all, tiles, grid_out, left, right, parts, s_buf, r_buf, s_sem, r_sem):
    y, x, z, c = where_am_i()
    half = NZ // 2
    n_group = NX * NC
    bev = grid_out.shape[0] // BLK
    chunk = grid_out.shape[0] // 2

    def zz(offset):
        return lax.rem(z + offset + 2 * NZ, NZ)

    beside = (at(y, x, zz(1), c), at(y, x, zz(-1), c))
    greet(beside)

    def hops(ch, d):
        return half if ch == d else half - 1

    def push(ch, d, k):
        send(s_buf.at[ch, d, k - 1], r_buf.at[ch, d, k - 1], s_sem.at[ch, d, k - 1], r_sem.at[ch, d, k - 1], beside[d])

    @pl.loop(0, NZ)
    def _(i):
        off = jnp.where(i == 0, half, jnp.where(i % 2 == 1, (NZ - 1 - i) // 2, -((NZ - i) // 2)))
        target = zz(off)
        p = (x * NZ + target) * NC + c
        for g in range(n_group):
            tile = tiles[g, target].astype(F32)
            dst = index[g, 1, p]
            alive = index[g, 2, p]
            for b in range(bev):
                weight = jnp.where(dst == b, alive, 0).astype(F32)
                left[b * BLK : (b + 1) * BLK, g * BLK : (g + 1) * BLK] = (tile * weight).astype(BF)
            right[g * BLK : (g + 1) * BLK, :] = x_all[g, index[g, 0, p]]
        parts[i] = jnp.dot(left[...], right[...], preferred_element_type=F32)

        @pl.when(i == 0)
        def _():
            for d in range(2):
                s_buf[d, d, 0] = parts[0, d * chunk : (d + 1) * chunk].astype(BF)
                push(d, d, 1)

        for d in range(2):
            if half == 1:
                continue

            @pl.when(i == 1 + d)
            def _(d=d):
                ch = 1 - d
                s_buf[ch, d, 0] = parts[1 + d, ch * chunk : (ch + 1) * chunk].astype(BF)
                push(ch, d, 1)

    for o in range(half - 1, 0, -1):
        for ch_is_d in (True, False):
            for d in range(2):
                ch = d if ch_is_d else 1 - d
                k = hops(ch, d) - o + 1
                if k == 1:
                    continue
                arrived(r_buf.at[ch, d, k - 2], r_sem.at[ch, d, k - 2], beside[d])
                i = NZ - 1 - 2 * o if d == 0 else NZ - 2 * o
                total = parts[i, ch * chunk : (ch + 1) * chunk] + r_buf[ch, d, k - 2].astype(F32)
                s_buf[ch, d, k - 1] = total.astype(BF)
                push(ch, d, k)
    for ch in range(2):
        total = parts[NZ - 1, ch * chunk : (ch + 1) * chunk]
        for d in range(2):
            k = hops(ch, d)
            if k == 0:
                continue
            arrived(r_buf.at[ch, d, k - 1], r_sem.at[ch, d, k - 1], beside[d])
            total = total + r_buf[ch, d, k - 1].astype(F32)
        grid_out[ch * chunk : (ch + 1) * chunk] = total
    for ch in range(2):
        for d in range(2):
            for k in range(hops(ch, d)):
                sent(s_buf.at[ch, d, k], s_sem.at[ch, d, k], beside[d])


def join(index_all, x_all, tiles_all, cells):
    channels = x_all.shape[-1]
    x_all = x_all.reshape(x_all.shape[0], -1, BLK, channels)
    n = NX * NC
    half = NZ // 2
    return pl.pallas_call(
        join_kernel,
        out_shape=jax.ShapeDtypeStruct((cells, channels), F32),
        in_specs=[SM, VM, VM],
        out_specs=VM,
        scratch_shapes=[
            pltpu.VMEM((cells, n * BLK), BF),
            pltpu.VMEM((n * BLK, channels), BF),
            pltpu.VMEM((NZ, cells, channels), F32),
            pltpu.VMEM((2, 2, half, cells // 2, channels), BF),
            pltpu.VMEM((2, 2, half, cells // 2, channels), BF),
            DMA((2, 2, half)), DMA((2, 2, half)),
        ],
        compiler_params=pltpu.CompilerParams(
            collective_id=1, has_side_effects=True, vmem_limit_bytes=VMEM_LIMIT
        ),
    )(index_all, x_all, tiles_all)


def pieces_of(shapes):
    row = 0
    for i, (rows, columns) in enumerate(shapes):
        height = rows // (NX * NY)
        for col in range(0, columns, 256):
            yield i, row, height, col
            row += height


def unpack_kernel(first, second, prediction, *outs):
    for packed, refs in ((first, outs[1:2]), (second, outs[2:])):
        width = packed.shape[3]
        for i, row, height, col in pieces_of([ref.shape for ref in refs]):
            for q in range(NX * NY):
                for core in range(NC):
                    refs[i][q * height : (q + 1) * height, col + core * width : col + (core + 1) * width] = packed[
                        core, q, row : row + height, :
                    ].astype(F32)
    outs[0][...] = prediction[...]


def unpack(first, second, prediction, shapes):
    return pl.pallas_call(
        unpack_kernel,
        out_shape=(jax.ShapeDtypeStruct(prediction.shape, BF),) + tuple(jax.ShapeDtypeStruct(a, F32) for a in shapes),
        in_specs=[VM] * 3,
        out_specs=tuple([VM] * (1 + len(shapes))),
        compiler_params=pltpu.CompilerParams(vmem_limit_bytes=VMEM_LIMIT),
    )(first, second, prediction)


class Total:
    n1, n2, width = NX * NY, NZ, 128

    def __init__(self, ins, out, scratch, paired=False):
        self.ins, self.out, self.paired = ins, out, paired
        (
            self.packed, self.from0, self.half, self.from1, self.mid, self.from2, self.mine, self.gathered, self.result,
            self.s0, self.r0, self.s1, self.r1, self.s2, self.r2, self.s3, self.r3, self.s4, self.r4, self.s5, self.r5,
        ) = scratch
        y, x, z, c = where_am_i()
        self.y, self.x, self.z, self.c = y, x, z, c
        self.one, self.two = y * NX + x, z
        self.sibling = at(y, x, z, 1 - c)
        self.real = self.half.shape[1]
        self.share = self.mine.shape[0]

    @classmethod
    def scratch_for(cls, shapes):
        n1, n2, width = NX * NY, NZ, cls.width
        real = sum(a * b for a, b in shapes) // (n1 * NC * width)
        share = -(-real // (n2 * 16)) * 16
        buffers = [
            (NC, n1, real, width), (n1, real, width), (n1, real, width), (n1 - 1, real, width), (share * n2, width),
            (n2 - 1, share, width), (share, width), (share * n2, width), (NC, n1, real, width),
        ]
        counts = [1, n1 - 1, n2 - 1, n2 - 1, n1 - 1, 1]
        return [pltpu.VMEM(b, BF) for b in buffers] + [DMA((n,)) for n in counts for _ in range(2)]

    def dev1(self, q):
        return at(q // NX, q % NX, self.z, self.c)

    def dev2(self, e):
        return at(self.y, self.x, e, self.c)

    def q1(self, o):
        n1 = NX * NY
        return lax.rem(self.one + o + n1, n1)

    def q2(self, o):
        return lax.rem(self.two + o + NZ, NZ)

    def peers(self):
        n1 = NX * NY
        return [self.sibling] + [self.dev1(self.q1(o)) for o in range(1, n1)] + [self.dev2(self.q2(o)) for o in range(1, NZ)]

    def pieces(self):
        return pieces_of([ref.shape for ref in self.ins])

    def start(self):
        n1 = NX * NY
        if self.paired:
            self.mid[...] = jnp.zeros_like(self.mid)
            return

        @pl.loop(0, n1)
        def _(q):
            for i, row, height, col in self.pieces():
                for core in range(NC):
                    left = col + core * self.width
                    self.packed[core, q, row : row + height, :] = self.ins[i][
                        pl.ds(pl.multiple_of(q * height, height), height), left : left + self.width
                    ].astype(BF)
        send(self.packed.at[1 - self.c], self.from0, self.s0.at[0], self.r0.at[0], self.sibling)
        self.mid[...] = jnp.zeros_like(self.mid)

    def over_xy(self):
        n1 = NX * NY
        if not self.paired:
            arrived(self.from0, self.r0.at[0], self.sibling)

        @pl.loop(0, n1)
        def _(o):
            q = lax.rem(self.one + 1 + o, n1)
            if self.paired:
                height = self.half.shape[1]
                self.half[q] = self.ins[0][pl.ds(pl.multiple_of(q * height, height), height), :].astype(BF)
            else:
                self.half[q] = (self.packed[self.c, q].astype(F32) + self.from0[q].astype(F32)).astype(BF)

            @pl.when(o < n1 - 1)
            def _():
                send(self.half.at[q], self.from1.at[o], self.s1.at[o], self.r1.at[o], self.dev1(q))

    def part(self, ref, e):
        return ref.at[pl.ds(pl.multiple_of(e * self.share, self.share), self.share), :]

    def over_z(self):
        total = self.half[self.one].astype(F32)
        for o in range(NX * NY - 1):
            arrived(self.from1.at[o], self.r1.at[o], self.sibling)
            total = total + self.from1[o].astype(F32)
        self.mid[0 : self.real, :] = total.astype(BF)
        for o in range(1, NZ):
            e = self.q2(o)
            send(self.part(self.mid, e), self.from2.at[o - 1], self.s2.at[o - 1], self.r2.at[o - 1], self.dev2(e))

    def back_over_z(self):
        total = self.mid[pl.ds(pl.multiple_of(self.two * self.share, self.share), self.share), :].astype(F32)
        for o in range(1, NZ):
            arrived(self.from2.at[o - 1], self.r2.at[o - 1], self.sibling)
            total = total + self.from2[o - 1].astype(F32)
        self.mine[...] = total.astype(BF)
        for o in range(1, NZ):
            send(self.mine, self.part(self.gathered, self.two), self.s3.at[o - 1], self.r3.at[o - 1], self.dev2(self.q2(o)))
        self.gathered[pl.ds(pl.multiple_of(self.two * self.share, self.share), self.share), :] = self.mine[...]

    def back_over_xy(self):
        for o in range(1, NZ):
            arrived(self.part(self.gathered, self.q2(-o)), self.r3.at[o - 1], self.sibling)
        for o in range(1, NX * NY):
            send(
                self.gathered.at[0 : self.real, :], self.result.at[self.c, self.one],
                self.s4.at[o - 1], self.r4.at[o - 1], self.dev1(self.q1(o)),
            )
        self.result[self.c, self.one] = self.gathered[0 : self.real, :]

    def back_over_core(self):
        for o in range(1, NX * NY):
            arrived(self.result.at[self.c, self.q1(-o)], self.r4.at[o - 1], self.sibling)
        send(self.result.at[self.c], self.result.at[self.c], self.s5.at[0], self.r5.at[0], self.sibling)

    def finish(self):
        n1 = NX * NY
        arrived(self.result.at[1 - self.c], self.r5.at[0], self.sibling)

        self.out[...] = self.result[...]
        if not self.paired:
            sent(self.from0, self.s0.at[0], self.sibling)
        sent(self.result.at[self.c], self.s5.at[0], self.sibling)
        for o in range(n1 - 1):
            sent(self.half.at[0], self.s1.at[o], self.sibling)
            sent(self.half.at[0], self.s4.at[o], self.sibling)
        for o in range(NZ - 1):
            sent(self.mine, self.s2.at[o], self.sibling)
            sent(self.mine, self.s3.at[o], self.sibling)


N_GRADS = 4


def gelu_parts(v):
    inner = math.sqrt(2.0 / math.pi) * (v + 0.044715 * v * v * v)
    slope = math.sqrt(2.0 / math.pi) * (1.0 + 3.0 * 0.044715 * v * v)
    t = jnp.tanh(inner)
    return 0.5 * v * (1.0 + t), 0.5 * (1.0 + t) + 0.5 * v * (1.0 - t * t) * slope


def split_kernel(index, grid, pred_grad, tiles, encoded, ru, rd, du, dd, *refs, scale):
    prediction, proj_out, out, refs = refs[0], refs[1], refs[2], refs[3:]
    all_grad, here, left, acc, core_s, core_r, x_send, x_recv, z_s, z_r, c_s, c_r, x_s, x_r = refs[:14]
    kept = refs[14:22]
    ins = refs[22 : 22 + N_GRADS]
    rows_out, grad_proj, other, e_s, e_r = refs[22 + N_GRADS : 27 + N_GRADS]
    refs = refs[27 + N_GRADS :]
    total = Total(ins, out, refs[: len(refs) // 2])
    last = Total([grad_proj], proj_out, refs[len(refs) // 2 :], paired=True)
    grad = pred_grad
    y, x, z, c = where_am_i()
    half = NZ // 2
    n_group = NX * NC
    chunk = grad.shape[0] // 2
    tokens = encoded.shape[0]
    cam = tokens // BLK
    sibling = at(y, x, z, 1 - c)

    def zz(offset):
        return lax.rem(z + offset + 2 * NZ, NZ)

    def xx(offset):
        return lax.rem(x + offset + NX, NX)

    beside = (at(y, x, zz(1), c), at(y, x, zz(-1), c))
    east, west = at(y, xx(1), z, c), at(y, xx(-1), z, c)
    barrier = pltpu.get_barrier_semaphore()
    for device in total.peers():
        pl.semaphore_signal(barrier, inc=1, device_id=device, device_id_type=MESH)

    def hops(ch, d):
        return half if ch == d else half - 1

    def part(origin, ch):
        return all_grad.at[origin, pl.ds(ch * chunk, chunk)]

    n1_ref, h1_ref, n2_ref, h2_ref, p1_ref, p2_ref, r1_ref, r2_ref = kept

    def heads(ch):
        r = slice(ch * chunk, (ch + 1) * chunk)

        def forward(state, w_up, w_down, n_ref, h_ref):
            scaling = lax.rsqrt(jnp.mean(state * state, axis=-1, keepdims=True) + eps)
            normed = (state * scaling).astype(BF)
            n_ref[r] = normed
            preact = jnp.dot(normed, w_up[...], preferred_element_type=F32)
            value, slope = gelu_parts(preact)
            hidden = value.astype(BF)
            h_ref[r] = hidden
            return state + jnp.dot(hidden, w_down[...], preferred_element_type=F32), scaling, slope

        def backward(g, state, scaling, slope, w_up, w_down, p_ref, r_ref):
            rounded = g.astype(BF)
            r_ref[r] = rounded
            grad_pre = (against_rows(rounded, w_down[...]) * slope).astype(BF)
            p_ref[r] = grad_pre
            grad_normed = against_rows(grad_pre, w_up[...])
            unit = state * scaling
            return g + scaling * (grad_normed - unit * jnp.mean(grad_normed * unit, axis=-1, keepdims=True))

        s0 = grid[r]
        s1, scale1, slope1 = forward(s0, ru, rd, n1_ref, h1_ref)
        s2, scale2, slope2 = forward(s1, du, dd, n2_ref, h2_ref)
        prediction[r] = s2.astype(BF)
        g1 = backward(pred_grad[r].astype(F32) * scale, s1, scale2, slope2, du, dd, p2_ref, r2_ref)
        g0 = backward(g1, s0, scale1, slope1, ru, rd, p1_ref, r1_ref)
        all_grad[z, r] = g0.astype(BF)

    for ch in range(2):
        heads(ch)
        if ch == 0:
            pl.semaphore_wait(barrier, len(total.peers()))
            send(encoded, other, e_s, e_r, sibling)
        for d in range(2):
            if hops(ch, d) >= 1:
                send(part(z, ch), part(z, ch), z_s.at[ch, d, 0], z_r.at[ch, d, 0], beside[d])
    ins[0][...] = contract_rows(n1_ref[...], p1_ref[...])
    ins[1][...] = contract_rows(h1_ref[...], r1_ref[...])
    ins[2][...] = contract_rows(n2_ref[...], p2_ref[...])
    ins[3][...] = contract_rows(h2_ref[...], r2_ref[...])
    total.start()

    def use(origin, first):
        p = (x * NZ + origin) * NC + c
        here[...] = all_grad[origin].reshape(here.shape)
        for g in range(n_group):
            tile = tiles[g, origin].astype(F32).T
            src = index[g, 0, p]
            alive = index[g, 2, p]
            for k in range(cam):
                weight = jnp.where(src == k, alive, 0).astype(F32)
                left[k * BLK : (k + 1) * BLK, :] = (tile * weight).astype(BF)
            product = jnp.dot(left[...], here[index[g, 1, p]], preferred_element_type=F32)
            if first:
                acc[g] = product
            else:
                acc[g] = acc[g] + product

    use(z, True)
    total.over_xy()

    @pl.loop(1, half + 1)
    def _(k):
        for d in range(2):
            s = 1 - 2 * d
            origin = zz(-s * k)
            for ch in range(2):
                @pl.when(k <= hops(ch, d))
                def _(ch=ch, d=d):
                    arrived(part(origin, ch), z_r.at[ch, d, k - 1], beside[d])

                @pl.when(k + 1 <= hops(ch, d))
                def _(ch=ch, d=d):
                    send(part(origin, ch), part(origin, ch), z_s.at[ch, d, k], z_r.at[ch, d, k], beside[d])

        @pl.when(k == max(half - 2, 1))
        def _():
            total.over_z()

        @pl.when(k == max(half - 1, 1))
        def _():
            total.back_over_z()

        @pl.when(k == half)
        def _():
            total.back_over_xy()

        use(zz(-k), False)

        @pl.when(k < half)
        def _():
            use(zz(k), False)

    wide = grid.shape[1] // NC
    order = (2, 1, NX - 1, 0)

    def channels_of(core):
        return pl.ds(pl.multiple_of(core * wide, wide), wide)

    for i, o in enumerate(order):
        for h in range(NC):
            core_s[i, h] = acc[xx(o) * NC + h, :, channels_of(1 - c)].astype(BF)
        send(core_s.at[i], core_r.at[i], c_s.at[i], c_r.at[i], sibling)

    def pair_sum(i, h):
        return acc[xx(order[i]) * NC + h, :, channels_of(c)] + core_r[i, h].astype(F32)

    def push(n, value, device):
        x_send[n] = value.astype(BF)
        send(x_send.at[n], x_recv.at[n], x_s.at[n], x_r.at[n], device)

    for i in range(3):
        arrived(core_r.at[i], c_r.at[i], sibling)
        if i == 0:
            push(0, pair_sum(0, 0), east)
            push(1, pair_sum(0, 1), west)
        if i == 1:
            push(2, pair_sum(1, 1), east)
        if i == 2:
            push(3, pair_sum(2, 0), west)
    arrived(x_recv.at[0], x_r.at[0], sibling)
    push(4, pair_sum(1, 0) + x_recv[0].astype(F32), east)
    arrived(x_recv.at[1], x_r.at[1], sibling)
    push(5, pair_sum(2, 1) + x_recv[1].astype(F32), west)
    arrived(core_r.at[3], c_r.at[3], sibling)
    for n in range(2, 6):
        arrived(x_recv.at[n], x_r.at[n], sibling)
    rows_out[0] = (pair_sum(3, 0) + x_recv[4].astype(F32) + x_recv[3].astype(F32)).astype(BF)
    rows_out[1] = (pair_sum(3, 1) + x_recv[2].astype(F32) + x_recv[5].astype(F32)).astype(BF)
    arrived(other, e_r, sibling)
    grad_proj[...] = contract_rows(encoded[...], rows_out[c]) + contract_rows(other[...], rows_out[1 - c])
    last.start()
    total.back_over_core()
    last.over_xy()
    total.finish()
    last.over_z()
    last.back_over_z()
    last.back_over_xy()
    last.back_over_core()
    last.finish()
    sent(encoded, e_s, sibling)
    for i in range(4):
        sent(core_s.at[i], c_s.at[i], sibling)
    for n in range(6):
        sent(x_send.at[n], x_s.at[n], sibling)
    for ch in range(2):
        for d in range(2):
            for k in range(hops(ch, d)):
                sent(part(z, ch), z_s.at[ch, d, k], beside[d])


def split(index_all, grid, pred_grad, tiles_all, encoded, weights, scale):
    cells, channels = grid.shape
    tokens, features = encoded.shape
    hidden = weights[0].shape[1]
    n = NX * NC
    half = NZ // 2
    shapes = [w.shape for w in weights]

    def packed_of(some):
        rows = sum(a * b for a, b in some) // (NX * NY * NC * Total.width)
        return jax.ShapeDtypeStruct((NC, NX * NY, rows, Total.width), BF)

    return pl.pallas_call(
        functools.partial(split_kernel, scale=scale),
        out_shape=(
            jax.ShapeDtypeStruct((cells, channels), BF),
            packed_of([(features, channels)]),
            packed_of(shapes),
        ),
        in_specs=[SM, VM, VM, VM, VM] + [VM] * N_GRADS,
        out_specs=(VM, VM, VM),
        scratch_shapes=[
            pltpu.VMEM((NZ, cells, channels), BF),
            pltpu.VMEM((cells // BLK, BLK, channels), BF),
            pltpu.VMEM((tokens, BLK), BF),
            pltpu.VMEM((n, tokens, channels), F32),
            pltpu.VMEM((NX, NC, tokens, channels // NC), BF),
            pltpu.VMEM((NX, NC, tokens, channels // NC), BF),
            pltpu.VMEM((6, tokens, channels // NC), BF),
            pltpu.VMEM((6, tokens, channels // NC), BF),
            DMA((2, 2, half)), DMA((2, 2, half)),
            DMA((NX,)), DMA((NX,)),
            DMA((6,)), DMA((6,)),
        ]
        + [pltpu.VMEM((cells, w), BF) for w in (channels, hidden) * 2 + (hidden, hidden, channels, channels)]
        + [pltpu.VMEM(a, F32) for a in shapes]
        + [pltpu.VMEM((NC, tokens, channels // NC), BF), pltpu.VMEM((features, channels // NC), F32)]
        + [pltpu.VMEM((tokens, features), BF), DMA(()), DMA(())]
        + Total.scratch_for(shapes)
        + Total.scratch_for([(features, channels)]),
        compiler_params=pltpu.CompilerParams(
            collective_id=2, has_side_effects=True, vmem_limit_bytes=VMEM_LIMIT
        ),
    )(index_all, grid, pred_grad, tiles_all, encoded, *weights)


def on_device(
    cams, vit_up, vit_down, proj, frustum_tiles, src_block, dst_block, live,
    render_up, render_down, decode_up, decode_down, pred_grad,
):
    tile_count = NX * NZ * NC
    cells, channels = pred_grad.shape[1:]
    encoded, x_all, tiles_all, index_all = encode(
        vit_up, vit_down, cams, proj, frustum_tiles[0], src_block, dst_block, live
    )
    bev_grid = join(index_all, x_all, tiles_all, cells)
    scale = 1.0 / math.sqrt(cams.shape[0] * cells * tile_count)
    weights = (render_up, render_down, decode_up, decode_down)
    prediction, first, second = split(index_all, bev_grid, pred_grad[0], tiles_all, encoded, weights, scale)
    prediction, *totals = unpack(first, second, prediction, [proj.shape] + [w.shape for w in weights])
    return (prediction[None], *totals)


def solution(mesh):
    placed = (
        P(None, "tile", None),
        P("section", None, None),
        P("section", None, None),
        P(),
        P("tile", None, None, None),
        P("tile", None),
        P("tile", None),
        P("tile", None),
        P(),
        P(),
        P(),
        P(),
        P("section", "tile", None),
    )
    return jax.shard_map(
        on_device,
        mesh=mesh,
        in_specs=placed,
        out_specs=(P("section", "tile", None), P(), P(), P(), P(), P()),
        check_vma=False,
    )
```

```python
import functools
import math

import jax
import jax.numpy as jnp
from jax import lax
from jax.experimental import pallas as pl
from jax.experimental.pallas import tpu as pltpu
from jax.sharding import PartitionSpec as P

eps = 1e-05
MESH = pl.DeviceIdType.MESH
BF = jnp.bfloat16
F32 = jnp.float32
NY, NX, NZ, NC = 4, 4, 8, 2
BLK = 128
VMEM_LIMIT = 60 * 2**20
ANY = pl.BlockSpec(memory_space=pl.ANY)
VM = pl.BlockSpec(memory_space=pltpu.VMEM)
SM = pl.BlockSpec(memory_space=pltpu.SMEM)
DMA = pltpu.SemaphoreType.DMA


def where_am_i():
    y = lax.axis_index("section")
    t = lax.axis_index("tile")
    return y, t // (NZ * NC), (t // NC) % NZ, t % NC


def at(y, x, z, c):
    return (y, (x * NZ + z) * NC + c)


def send(src, dst, ssem, rsem, device):
    copy = pltpu.make_async_remote_copy(
        src_ref=src, dst_ref=dst, send_sem=ssem, recv_sem=rsem, device_id=device, device_id_type=MESH
    )
    copy.start()


def sent(src, ssem, device):
    pltpu.make_async_remote_copy(
        src_ref=src, dst_ref=src, send_sem=ssem, recv_sem=ssem, device_id=device, device_id_type=MESH
    ).wait_send()


def arrived(dst, rsem, device):
    pltpu.make_async_remote_copy(
        src_ref=dst, dst_ref=dst, send_sem=rsem, recv_sem=rsem, device_id=device, device_id_type=MESH
    ).wait_recv()


def greet(devices):
    barrier = pltpu.get_barrier_semaphore()
    for device in devices:
        pl.semaphore_signal(barrier, inc=1, device_id=device, device_id_type=MESH)
    pl.semaphore_wait(barrier, len(devices))


def gelu(v):
    return 0.5 * v * (1.0 + jnp.tanh(math.sqrt(2.0 / math.pi) * (v + 0.044715 * v * v * v)))


def contract_rows(left, right):
    return lax.dot_general(left, right, (((0,), (0,)), ((), ())), preferred_element_type=F32)


def against_rows(left, right):
    return lax.dot_general(left, right, (((1,), (1,)), ((), ())), preferred_element_type=F32)


def encoder_kernel(
    up, down, cams, proj, tiles, src, dst, live,
    encoded, x_all, tiles_all, index_all,
    w_up, w_down, own, y_s, y_r, x_s, x_r, u_s, u_r, z_s, z_r, b_s, b_r, t_s, t_r, i_s, i_r, p_s, p_r, v_s, v_r, w_s, w_r,
    local, index,
):
    y, x, z, c = where_am_i()
    sibling = at(y, x, z, 1 - c)
    group = x * NC + c
    moved = NY - 1
    half = NZ // 2
    steps = half + 1
    n_group = NX * NC
    plane_up, plane_down = 2 * w_up.shape[-1] // 3, 2 * w_down.shape[-1] // 3
    cols = plane_up // 2
    quarter = BLK // NY

    def layer_of(j):
        return j + jnp.where(j >= y, 1, 0)

    def up_slice(l, xx):
        return w_up.at[l, z, xx // 2, :, pl.ds(pl.multiple_of((xx % 2) * cols, 128), cols)]

    def up_block(l, zo):
        return w_up.at[l, zo, :, :, pl.ds(0, plane_up)]

    def down_slice(l, zo):
        return w_down.at[l, zo, x, :, pl.ds(0, plane_down)]

    def down_block(l, xo):
        return w_down.at[l, :, xo, :, pl.ds(0, plane_down)]

    def y_part(l, core, h):
        if core == 0:
            width = (w_up.shape[-1] - plane_up) // 2
            return w_up.at[l, :, :, :, pl.ds(plane_up + h * width, width)]
        return w_down.at[l, pl.ds(h * half, half), :, :, pl.ds(plane_down, w_down.shape[-1] - plane_down)]

    def zz(offset):
        return lax.rem(z + offset + 2 * NZ, NZ)

    def xx(offset):
        return lax.rem(x + offset + NX, NX)

    def yy(offset):
        return lax.rem(y + offset + NY, NY)

    def gg(offset):
        return lax.rem(group + offset + n_group, n_group)

    def g_dev(g):
        return at(y, g // NC, z, g % NC)

    east, west = at(y, xx(1), z, c), at(y, xx(-1), z, c)
    north, south = at(yy(1), x, z, c), at(yy(-1), x, z, c)

    def tile_rows(ref, section):
        return ref.at[:, pl.ds(pl.multiple_of(section * quarter, quarter), quarter), :]

    index[...] = jnp.zeros_like(index)
    for i, ref in enumerate((src, dst, live)):
        index[i : i + 1, 0 : ref.shape[1]] = ref[...]
    loads = [
        pltpu.make_async_copy(up, w_up.at[y], local.at[0]),
        pltpu.make_async_copy(down, w_down.at[y], local.at[1]),
        pltpu.make_async_copy(cams.at[y], encoded, local.at[2]),
        pltpu.make_async_copy(tile_rows(tiles.at[x, :, c], y), tile_rows(tiles_all.at[group], y), local.at[3]),
        pltpu.make_async_copy(index, index_all.at[group], local.at[4]),
    ]
    for load in loads:
        load.start()
    greet(
        [at(yy(o), x, z, c) for o in range(1, NY)]
        + [g_dev(gg(o)) for o in range(1, n_group)]
        + [at(y, x, zz(o), c) for o in ((1, -1, 2, -2) if NZ == 8 else (1, -1))]
    )
    for load in loads[:3]:
        load.wait()

    def share(l, core):
        return up_slice(l, x) if core == 0 else down_slice(l, z)

    for core in range(NC):
        @pl.when(c == core)
        def _(core=core):
            for o in range(1, NY):
                send(share(y, core), share(y, core), y_s.at[o - 1], y_r.at[o - 1], at(yy(o), x, z, c))
            for h, i, device in ((0, 0, north), (1, 3, south), (1, 1, north), (0, 2, south)):
                send(y_part(y, core, h), y_part(y, core, h), v_s.at[i], v_r.at[i], device)

    def sign(j, d):
        return (1 - 2 * (j % 2)) * (1 - 2 * d)

    def send_tiles():
        for o in range(1, n_group):
            g = gg(o)
            send(index, index_all.at[group], i_s.at[o - 1], i_r.at[o - 1], g_dev(g))
            send(
                tile_rows(tiles.at[g // NC, :, g % NC], y), tile_rows(tiles_all.at[group], y),
                t_s.at[o - 1], t_r.at[o - 1], g_dev(g),
            )

    first_hops = (1, -1, 2, -2) if NZ == 8 else tuple(range(1, NZ))
    later_hops = ((4, 1, 2), (5, 2, 2), (6, -1, -2)) if NZ == 8 else ()

    def sem_of(sems, j, i):
        return sems.at[j, i // half, i % half]

    def slice_to(j, l, i, off, origin):
        s = sign(j, 0)
        block = down_slice(l, zz(-s * origin))
        send(block, block, sem_of(z_s, j, i), sem_of(z_r, j, i), at(y, x, zz(s * off), c))

    def go_on(j):
        l = layer_of(j)
        for i, off, origin in later_hops:
            if i != 5:
                first = first_hops.index(origin)
                arrived(down_slice(l, zz(-sign(j, 0) * origin)), sem_of(z_r, j, first), sibling)
            slice_to(j, l, i, off, origin)

    def slices_arrived(j, l):
        s = sign(j, 0)
        for i, off in enumerate(first_hops):
            if off not in [origin for _, _, origin in later_hops]:
                arrived(down_slice(l, zz(-s * off)), sem_of(z_r, j, i), sibling)
        for i, off, origin in later_hops:
            arrived(down_slice(l, zz(-s * (off + origin))), sem_of(z_r, j, i), sibling)

    @pl.when(c == 0)
    def _():
        @pl.loop(0, moved)
        def _(j):
            l = layer_of(j)
            o = yy(-l)
            arrived(share(l, 0), y_r.at[o - 1], sibling)
            for ox in range(1, NX):
                send(up_slice(l, x), up_slice(l, x), u_s.at[j, ox - 1], u_r.at[j, ox - 1], at(y, xx(ox), z, c))
        send_tiles()

    def z_hops(d):
        return half if d == 0 else half - 1

    @pl.when(c == 1)
    def _():
        @pl.loop(0, moved)
        def _(j):
            l = layer_of(j)
            arrived(share(l, 1), y_r.at[yy(-l) - 1], sibling)
            for i, off in enumerate(first_hops):
                slice_to(j, l, i, off, 0)
        send_tiles()
        go_on(0)

    def layer_rows(l, r, rows):
        wide = encoded[pl.ds(r, rows), :].astype(F32)
        scaling = lax.rsqrt(jnp.mean(wide * wide, axis=-1, keepdims=True) + eps)
        normed = (wide * scaling).astype(BF)
        total = wide
        parts = 2
        for q in range(parts):
            width = w_up.shape[-1] // parts
            w1 = w_up[l, :, :, :, q * width : (q + 1) * width].reshape(wide.shape[1], width)
            hidden = gelu(jnp.dot(normed, w1, preferred_element_type=F32)).astype(BF)
            nz = NZ // parts
            w2 = w_down[l, q * nz : (q + 1) * nz].reshape(width, wide.shape[1])
            total = total + jnp.dot(hidden, w2, preferred_element_type=F32)
        encoded[pl.ds(r, rows), :] = total.astype(BF)

    tokens = encoded.shape[0]
    rows = tokens // 2

    def wait_sibling(j):
        l = layer_of(j)

        @pl.when(c == 0)
        def _():
            for i, ox in enumerate((0, 1, NX - 1, 2)):
                arrived(down_block(l, xx(-ox)), b_r.at[j, i], sibling)

        @pl.when(c == 1)
        def _():
            arrived(up_block(l, z), b_r.at[j, 0], sibling)
            for d in range(2):
                for k in range(2, z_hops(d) + 2):
                    arrived(up_block(l, zz(-sign(j, d) * (k - 1))), b_r.at[j, 1 + d * half + k - 2], sibling)

    def second_half(l, xo, h):
        return w_down.at[l, pl.ds(h * half, half), xo, :, pl.ds(0, plane_down)]

    def begin(j):
        l = layer_of(j)

        @pl.when(c == 0)
        def _():
            for ox in range(1, NX):
                arrived(up_slice(l, xx(-ox)), u_r.at[j, ox - 1], sibling)
            block = up_block(l, z)
            for d in range(2):
                if z_hops(d) >= 1:
                    send(block, block, z_s.at[j, d, 0], z_r.at[j, d, 0], at(y, x, zz(sign(j, d)), c))
            send(block, block, b_s.at[j, 0], b_r.at[j, 0], sibling)

        @pl.when(c == 1)
        def _():
            slices_arrived(j, l)
            block = down_block(l, x)
            send(block, block, x_s.at[j, 0], x_r.at[j, 0], east)
            send(block, block, x_s.at[j, 1], x_r.at[j, 1], west)
            send(block, block, b_s.at[j, 0], b_r.at[j, 0], sibling)

    def own_rows(section):
        return tiles_all.at[:, :, pl.ds(pl.multiple_of(section * quarter, quarter), quarter), :]

    def some_rows(section, h):
        return tiles_all.at[
            pl.ds(h * n_group // 2, n_group // 2), :, pl.ds(pl.multiple_of(section * quarter, quarter), quarter), :
        ]

    t0 = n_group - 1

    def y_piece(i):
        return (yy(-1), yy(-1), yy(1), yy(1), yy(2), yy(2))[i], (0, 1, 0, 1, 0, 1)[i]

    def take_y(i):
        l, h = y_piece(i)
        for core in range(NC):
            @pl.when(c == core)
            def _(core=core):
                piece = y_part(l, core, h)
                arrived(piece, v_r.at[i], sibling)
                if i == 0:
                    send(piece, piece, v_s.at[4], v_r.at[4], north)
                if i == 3:
                    send(piece, piece, v_s.at[5], v_r.at[5], south)
                send(piece, piece, w_s.at[i], w_r.at[i], sibling)

    last = max(steps, 5)

    @pl.loop(1, moved - 1 + last + 1)
    def _(slot):
        @pl.loop(0, moved)
        def _(j):
            k = slot - j
            l = layer_of(j)

            @pl.when(jnp.logical_and(c == 0, k >= 2))
            def _():
                for d in range(2):
                    s = sign(j, d)
                    block = up_block(l, zz(-s * (k - 1)))

                    @pl.when(k <= z_hops(d) + 1)
                    def _():
                        arrived(block, z_r.at[j, d, k - 2], sibling)

                        @pl.when(k <= z_hops(d))
                        def _():
                            send(block, block, z_s.at[j, d, k - 1], z_r.at[j, d, k - 1], at(y, x, zz(s), c))

                        send(block, block, b_s.at[j, 1 + d * half + k - 2], b_r.at[j, 1 + d * half + k - 2], sibling)

            @pl.when(jnp.logical_and(c == 1, k == 3))
            def _():
                block = down_block(l, xx(-1))
                arrived(block, x_r.at[j, 0], sibling)
                send(second_half(l, xx(-1), 0), second_half(l, xx(-1), 0), x_s.at[j, 2], x_r.at[j, 2], east)
                send(block, block, b_s.at[j, 1], b_r.at[j, 1], sibling)
                other = down_block(l, xx(1))
                arrived(other, x_r.at[j, 1], sibling)
                send(second_half(l, xx(1), 1), second_half(l, xx(1), 1), x_s.at[j, 3], x_r.at[j, 3], west)
                send(other, other, b_s.at[j, 2], b_r.at[j, 2], sibling)

            @pl.when(jnp.logical_and(c == 1, k == last))
            def _():
                arrived(second_half(l, xx(2), 0), x_r.at[j, 2], sibling)
                arrived(second_half(l, xx(2), 1), x_r.at[j, 3], sibling)
                block = down_block(l, xx(2))
                send(block, block, b_s.at[j, 3], b_r.at[j, 3], sibling)

            @pl.when(k == 1)
            def _():
                begin(j)

            @pl.when(jnp.logical_and(c == 1, k == 0))
            def _():
                go_on(j)

        for when, pieces in ((1, (0, 3)), (3, (1, 2)), (5, (4, 5))):
            @pl.when(slot == when)
            def _(pieces=pieces):
                for i in pieces:
                    take_y(i)

        @pl.when(slot == last)
        def _():
            for load in loads[3:]:
                load.wait()
            for o in range(1, n_group):
                arrived(tile_rows(tiles_all.at[gg(-o)], y), t_r.at[o - 1], sibling)
            send(own_rows(y), own_rows(y), t_s.at[t0], t_r.at[t0], north)
            send(own_rows(y), own_rows(y), t_s.at[t0 + 1], t_r.at[t0 + 1], south)

        @pl.when(slot == last + 1)
        def _():
            for i in range(6):
                l, h = y_piece(i)
                for core in range(NC):
                    @pl.when(c != core)
                    def _(core=core):
                        arrived(y_part(l, core, h), w_r.at[i], sibling)

        @pl.when(slot > last)
        def _():
            wait_sibling(slot - last - 1)
            layer_rows(slot - last - 1, 0, tokens)

    wait_sibling(moved - 1)

    layer_rows(NY - 2, 0, tokens)

    arrived(own_rows(yy(-1)), t_r.at[t0], sibling)
    send(some_rows(yy(-1), 0), some_rows(yy(-1), 0), t_s.at[t0 + 2], t_r.at[t0 + 2], north)
    arrived(own_rows(yy(1)), t_r.at[t0 + 1], sibling)
    send(some_rows(yy(1), 1), some_rows(yy(1), 1), t_s.at[t0 + 3], t_r.at[t0 + 3], south)
    layer_rows(NY - 1, 0, rows)

    def half_of(g, h):
        return x_all.at[g, pl.ds(h * rows, rows), :]

    def project(h):
        mine = own.at[h * rows : (h + 1) * rows]
        mine[...] = jnp.dot(encoded[h * rows : (h + 1) * rows], proj[...], preferred_element_type=F32).astype(BF)
        send(mine, half_of(group, h), p_s.at[h], p_r.at[h], east)
        send(mine, half_of(group, h), p_s.at[2 + h], p_r.at[2 + h], west)
        send(mine, half_of(group, h), p_s.at[4 + h], p_r.at[4 + h], sibling)

    project(0)
    layer_rows(NY - 1, rows, rows)
    project(1)
    keep = pltpu.make_async_copy(own, x_all.at[group], local.at[5])
    keep.start()
    near, far = (xx(-1) * NC + c, xx(1) * NC + c), xx(2) * NC + c
    arrived(half_of(near[0], 0), p_r.at[0], sibling)
    send(half_of(near[0], 0), half_of(near[0], 0), p_s.at[6], p_r.at[6], east)
    arrived(half_of(near[1], 0), p_r.at[2], sibling)
    arrived(half_of(near[1], 1), p_r.at[3], sibling)
    send(half_of(near[1], 1), half_of(near[1], 1), p_s.at[7], p_r.at[7], west)
    send(x_all.at[near[1]], x_all.at[near[1]], p_s.at[9], p_r.at[9], sibling)
    arrived(half_of(near[0], 1), p_r.at[1], sibling)
    send(x_all.at[near[0]], x_all.at[near[0]], p_s.at[8], p_r.at[8], sibling)
    arrived(half_of(far, 0), p_r.at[6], sibling)
    arrived(half_of(far, 1), p_r.at[7], sibling)
    send(x_all.at[far], x_all.at[far], p_s.at[10], p_r.at[10], sibling)
    for h in range(2):
        arrived(half_of(x * NC + 1 - c, h), p_r.at[4 + h], sibling)
    for i, ox in enumerate((-1, 1, 2)):
        arrived(x_all.at[xx(ox) * NC + 1 - c], p_r.at[8 + i], sibling)

    keep.wait()
    arrived(some_rows(yy(2), 0), t_r.at[t0 + 2], sibling)
    arrived(some_rows(yy(2), 1), t_r.at[t0 + 3], sibling)
    for o in range(1, n_group):
        arrived(index_all.at[gg(-o)], i_r.at[o - 1], sibling)
        sent(tile_rows(tiles_all.at[group], y), t_s.at[o - 1], sibling)
        sent(index_all.at[group], i_s.at[o - 1], sibling)
    for i in range(2):
        sent(own_rows(y), t_s.at[t0 + i], sibling)
        sent(some_rows(y, 0), t_s.at[t0 + 2 + i], sibling)
    for i in range(8):
        sent(own.at[0:rows], p_s.at[i], sibling)
    for i in range(8, 11):
        sent(own, p_s.at[i], sibling)
    for core in range(NC):
        @pl.when(c == core)
        def _(core=core):
            for o in range(1, NY):
                sent(share(y, core), y_s.at[o - 1], sibling)
            for i in range(6):
                sent(y_part(y, core, 0), v_s.at[i], sibling)
                sent(y_part(y, core, 0), w_s.at[i], sibling)

    @pl.loop(0, moved)
    def _(j):
        @pl.when(c == 0)
        def _():
            for ox in range(1, NX):
                sent(up_slice(y, x), u_s.at[j, ox - 1], sibling)
            for d in range(2):
                for k in range(1, z_hops(d) + 1):
                    sent(up_block(y, z), z_s.at[j, d, k - 1], sibling)
            for i in range(NZ):
                sent(up_block(y, z), b_s.at[j, i], sibling)

        @pl.when(c == 1)
        def _():
            for i in range(2):
                sent(down_block(y, x), x_s.at[j, i], sibling)
                sent(second_half(y, x, 0), x_s.at[j, 2 + i], sibling)
            for i in range(NZ - 1):
                sent(down_slice(y, z), sem_of(z_s, j, i), sibling)
            for i in range(NX):
                sent(down_block(y, x), b_s.at[j, i], sibling)


def encode(up, down, cams, proj, tiles, src, dst, live):
    d, f = up.shape[1:]
    tokens = cams.shape[1]
    channels = proj.shape[1]
    up = up.reshape(NZ, NX // 2, 2 * d // (NZ * NX), f)
    down = down.reshape(NZ, NX, f // (NZ * NX), d)
    tiles = tiles.reshape(NX, NZ, NC, BLK, BLK)
    n = NX * NC
    half = NZ // 2
    moved = NY - 1
    return pl.pallas_call(
        encoder_kernel,
        out_shape=(
            jax.ShapeDtypeStruct((tokens, d), BF),
            jax.ShapeDtypeStruct((n, tokens, channels), BF),
            jax.ShapeDtypeStruct((n, NZ, BLK, BLK), BF),
            jax.ShapeDtypeStruct((n, 8, 128), jnp.int32),
        ),
        in_specs=[ANY, ANY, ANY, VM, ANY, VM, VM, VM],
        out_specs=(VM, ANY, ANY, ANY),
        scratch_shapes=[
            pltpu.VMEM((NY,) + up.shape, BF),
            pltpu.VMEM((NY,) + down.shape, BF),
            pltpu.VMEM((tokens, channels), BF),
            DMA((NY - 1,)), DMA((NY - 1,)),
            DMA((moved, 4)), DMA((moved, 4)),
            DMA((moved, NX - 1)), DMA((moved, NX - 1)),
            DMA((moved, 2, half)), DMA((moved, 2, half)),
            DMA((moved, max(NZ, NX))), DMA((moved, max(NZ, NX))),
            DMA((n + 3,)), DMA((n + 3,)),
            DMA((n - 1,)), DMA((n - 1,)),
            DMA((11,)), DMA((11,)),
            DMA((6,)), DMA((6,)),
            DMA((6,)), DMA((6,)),
            DMA((6,)),
            pltpu.VMEM((8, 128), jnp.int32),
        ],
        compiler_params=pltpu.CompilerParams(
            collective_id=0, has_side_effects=True, vmem_limit_bytes=VMEM_LIMIT
        ),
    )(up, down, cams, proj, tiles, src, dst, live)


def join_kernel(index, x_hbm, tiles_hbm, grid_out, x_all, tiles, local, left, right, parts, s_buf, r_buf, s_sem, r_sem):
    y, x, z, c = where_am_i()
    half = NZ // 2
    n_group = NX * NC
    bev = grid_out.shape[0] // BLK
    chunk = grid_out.shape[0] // 2

    def zz(offset):
        return lax.rem(z + offset + 2 * NZ, NZ)

    loads = [
        pltpu.make_async_copy(x_hbm, x_all, local.at[0]),
        pltpu.make_async_copy(tiles_hbm, tiles, local.at[1]),
    ]
    for load in loads:
        load.start()
    beside = (at(y, x, zz(1), c), at(y, x, zz(-1), c))
    greet(beside)
    for load in loads:
        load.wait()

    def hops(ch, d):
        return half if ch == d else half - 1

    def push(ch, d, k):
        send(s_buf.at[ch, d, k - 1], r_buf.at[ch, d, k - 1], s_sem.at[ch, d, k - 1], r_sem.at[ch, d, k - 1], beside[d])

    @pl.loop(0, NZ)
    def _(i):
        off = jnp.where(i == 0, half, jnp.where(i % 2 == 1, (NZ - 1 - i) // 2, -((NZ - i) // 2)))
        target = zz(off)
        p = (x * NZ + target) * NC + c
        for g in range(n_group):
            tile = tiles[g, target].astype(F32)
            dst = index[g, 1, p]
            alive = index[g, 2, p]
            for b in range(bev):
                weight = jnp.where(dst == b, alive, 0).astype(F32)
                left[b * BLK : (b + 1) * BLK, g * BLK : (g + 1) * BLK] = (tile * weight).astype(BF)
            right[g * BLK : (g + 1) * BLK, :] = x_all[g, index[g, 0, p]]
        parts[i] = jnp.dot(left[...], right[...], preferred_element_type=F32)

        @pl.when(i == 0)
        def _():
            for d in range(2):
                s_buf[d, d, 0] = parts[0, d * chunk : (d + 1) * chunk].astype(BF)
                push(d, d, 1)

        for d in range(2):
            if half == 1:
                continue

            @pl.when(i == 1 + d)
            def _(d=d):
                ch = 1 - d
                s_buf[ch, d, 0] = parts[1 + d, ch * chunk : (ch + 1) * chunk].astype(BF)
                push(ch, d, 1)

    for o in range(half - 1, 0, -1):
        for ch_is_d in (True, False):
            for d in range(2):
                ch = d if ch_is_d else 1 - d
                k = hops(ch, d) - o + 1
                if k == 1:
                    continue
                arrived(r_buf.at[ch, d, k - 2], r_sem.at[ch, d, k - 2], beside[d])
                i = NZ - 1 - 2 * o if d == 0 else NZ - 2 * o
                total = parts[i, ch * chunk : (ch + 1) * chunk] + r_buf[ch, d, k - 2].astype(F32)
                s_buf[ch, d, k - 1] = total.astype(BF)
                push(ch, d, k)
    for ch in range(2):
        total = parts[NZ - 1, ch * chunk : (ch + 1) * chunk]
        for d in range(2):
            k = hops(ch, d)
            if k == 0:
                continue
            arrived(r_buf.at[ch, d, k - 1], r_sem.at[ch, d, k - 1], beside[d])
            total = total + r_buf[ch, d, k - 1].astype(F32)
        grid_out[ch * chunk : (ch + 1) * chunk] = total
    for ch in range(2):
        for d in range(2):
            for k in range(hops(ch, d)):
                sent(s_buf.at[ch, d, k], s_sem.at[ch, d, k], beside[d])


def join(index_all, x_all, tiles_all, cells):
    channels = x_all.shape[-1]
    x_all = x_all.reshape(x_all.shape[0], -1, BLK, channels)
    n = NX * NC
    half = NZ // 2
    return pl.pallas_call(
        join_kernel,
        out_shape=jax.ShapeDtypeStruct((cells, channels), F32),
        in_specs=[SM, ANY, ANY],
        out_specs=VM,
        scratch_shapes=[
            pltpu.VMEM(x_all.shape, BF),
            pltpu.VMEM(tiles_all.shape, BF),
            DMA((2,)),
            pltpu.VMEM((cells, n * BLK), BF),
            pltpu.VMEM((n * BLK, channels), BF),
            pltpu.VMEM((NZ, cells, channels), F32),
            pltpu.VMEM((2, 2, half, cells // 2, channels), BF),
            pltpu.VMEM((2, 2, half, cells // 2, channels), BF),
            DMA((2, 2, half)), DMA((2, 2, half)),
        ],
        compiler_params=pltpu.CompilerParams(
            collective_id=1, has_side_effects=True, vmem_limit_bytes=VMEM_LIMIT
        ),
    )(index_all, x_all, tiles_all)


def pieces_of(shapes):
    row = 0
    for i, (rows, columns) in enumerate(shapes):
        height = rows // (NX * NY)
        for col in range(0, columns, 256):
            yield i, row, height, col
            row += height


def unpack_kernel(first, second, prediction, *outs):
    for packed, refs in ((first, outs[1:2]), (second, outs[2:])):
        width = packed.shape[3]
        for i, row, height, col in pieces_of([ref.shape for ref in refs]):
            for q in range(NX * NY):
                for core in range(NC):
                    refs[i][q * height : (q + 1) * height, col + core * width : col + (core + 1) * width] = packed[
                        core, q, row : row + height, :
                    ].astype(F32)
    outs[0][...] = prediction[...]


def unpack(first, second, prediction, shapes):
    return pl.pallas_call(
        unpack_kernel,
        out_shape=(jax.ShapeDtypeStruct(prediction.shape, BF),) + tuple(jax.ShapeDtypeStruct(a, F32) for a in shapes),
        in_specs=[VM] * 3,
        out_specs=tuple([VM] * (1 + len(shapes))),
        compiler_params=pltpu.CompilerParams(vmem_limit_bytes=VMEM_LIMIT),
    )(first, second, prediction)


class Total:
    n1, n2, width = NX * NY, NZ, 128

    def __init__(self, ins, out, scratch, paired=False):
        self.ins, self.out, self.paired = ins, out, paired
        (
            self.packed, self.from0, self.half, self.from1, self.mid, self.from2, self.mine, self.gathered, self.result,
            self.s0, self.r0, self.s1, self.r1, self.s2, self.r2, self.s3, self.r3, self.s4, self.r4, self.s5, self.r5,
        ) = scratch
        y, x, z, c = where_am_i()
        self.y, self.x, self.z, self.c = y, x, z, c
        self.one, self.two = y * NX + x, z
        self.sibling = at(y, x, z, 1 - c)
        self.real = self.half.shape[1]
        self.share = self.mine.shape[0]

    @classmethod
    def scratch_for(cls, shapes):
        n1, n2, width = NX * NY, NZ, cls.width
        real = sum(a * b for a, b in shapes) // (n1 * NC * width)
        share = -(-real // (n2 * 16)) * 16
        buffers = [
            (NC, n1, real, width), (n1, real, width), (n1, real, width), (n1 - 1, real, width), (share * n2, width),
            (n2 - 1, share, width), (share, width), (share * n2, width), (NC, n1, real, width),
        ]
        counts = [1, n1 - 1, n2 - 1, n2 - 1, n1 - 1, 1]
        return [pltpu.VMEM(b, BF) for b in buffers] + [DMA((n,)) for n in counts for _ in range(2)]

    def dev1(self, q):
        return at(q // NX, q % NX, self.z, self.c)

    def dev2(self, e):
        return at(self.y, self.x, e, self.c)

    def q1(self, o):
        n1 = NX * NY
        return lax.rem(self.one + o + n1, n1)

    def q2(self, o):
        return lax.rem(self.two + o + NZ, NZ)

    def peers(self):
        n1 = NX * NY
        return [self.sibling] + [self.dev1(self.q1(o)) for o in range(1, n1)] + [self.dev2(self.q2(o)) for o in range(1, NZ)]

    def pieces(self):
        return pieces_of([ref.shape for ref in self.ins])

    def start(self):
        n1 = NX * NY
        if self.paired:
            self.mid[...] = jnp.zeros_like(self.mid)
            return

        @pl.loop(0, n1)
        def _(q):
            for i, row, height, col in self.pieces():
                for core in range(NC):
                    left = col + core * self.width
                    self.packed[core, q, row : row + height, :] = self.ins[i][
                        pl.ds(pl.multiple_of(q * height, height), height), left : left + self.width
                    ].astype(BF)
        send(self.packed.at[1 - self.c], self.from0, self.s0.at[0], self.r0.at[0], self.sibling)
        self.mid[...] = jnp.zeros_like(self.mid)

    def over_xy(self):
        n1 = NX * NY
        if not self.paired:
            arrived(self.from0, self.r0.at[0], self.sibling)

        @pl.loop(0, n1)
        def _(o):
            q = lax.rem(self.one + 1 + o, n1)
            if self.paired:
                height = self.half.shape[1]
                self.half[q] = self.ins[0][pl.ds(pl.multiple_of(q * height, height), height), :].astype(BF)
            else:
                self.half[q] = (self.packed[self.c, q].astype(F32) + self.from0[q].astype(F32)).astype(BF)

            @pl.when(o < n1 - 1)
            def _():
                send(self.half.at[q], self.from1.at[o], self.s1.at[o], self.r1.at[o], self.dev1(q))

    def part(self, ref, e):
        return ref.at[pl.ds(pl.multiple_of(e * self.share, self.share), self.share), :]

    def over_z(self):
        total = self.half[self.one].astype(F32)
        for o in range(NX * NY - 1):
            arrived(self.from1.at[o], self.r1.at[o], self.sibling)
            total = total + self.from1[o].astype(F32)
        self.mid[0 : self.real, :] = total.astype(BF)
        for o in range(1, NZ):
            e = self.q2(o)
            send(self.part(self.mid, e), self.from2.at[o - 1], self.s2.at[o - 1], self.r2.at[o - 1], self.dev2(e))

    def back_over_z(self):
        total = self.mid[pl.ds(pl.multiple_of(self.two * self.share, self.share), self.share), :].astype(F32)
        for o in range(1, NZ):
            arrived(self.from2.at[o - 1], self.r2.at[o - 1], self.sibling)
            total = total + self.from2[o - 1].astype(F32)
        self.mine[...] = total.astype(BF)
        for o in range(1, NZ):
            send(self.mine, self.part(self.gathered, self.two), self.s3.at[o - 1], self.r3.at[o - 1], self.dev2(self.q2(o)))
        self.gathered[pl.ds(pl.multiple_of(self.two * self.share, self.share), self.share), :] = self.mine[...]

    def back_over_xy(self):
        for o in range(1, NZ):
            arrived(self.part(self.gathered, self.q2(-o)), self.r3.at[o - 1], self.sibling)
        for o in range(1, NX * NY):
            send(
                self.gathered.at[0 : self.real, :], self.result.at[self.c, self.one],
                self.s4.at[o - 1], self.r4.at[o - 1], self.dev1(self.q1(o)),
            )
        self.result[self.c, self.one] = self.gathered[0 : self.real, :]

    def back_over_core(self):
        for o in range(1, NX * NY):
            arrived(self.result.at[self.c, self.q1(-o)], self.r4.at[o - 1], self.sibling)
        send(self.result.at[self.c], self.result.at[self.c], self.s5.at[0], self.r5.at[0], self.sibling)

    def finish(self):
        n1 = NX * NY
        arrived(self.result.at[1 - self.c], self.r5.at[0], self.sibling)

        self.out[...] = self.result[...]
        if not self.paired:
            sent(self.from0, self.s0.at[0], self.sibling)
        sent(self.result.at[self.c], self.s5.at[0], self.sibling)
        for o in range(n1 - 1):
            sent(self.half.at[0], self.s1.at[o], self.sibling)
            sent(self.half.at[0], self.s4.at[o], self.sibling)
        for o in range(NZ - 1):
            sent(self.mine, self.s2.at[o], self.sibling)
            sent(self.mine, self.s3.at[o], self.sibling)


N_GRADS = 4


def gelu_parts(v):
    inner = math.sqrt(2.0 / math.pi) * (v + 0.044715 * v * v * v)
    slope = math.sqrt(2.0 / math.pi) * (1.0 + 3.0 * 0.044715 * v * v)
    t = jnp.tanh(inner)
    return 0.5 * v * (1.0 + t), 0.5 * (1.0 + t) + 0.5 * v * (1.0 - t * t) * slope


def split_kernel(index, grid, pred_grad, tiles_hbm, encoded, ru, rd, du, dd, *refs, scale):
    prediction, proj_out, out, refs = refs[0], refs[1], refs[2], refs[3:]
    all_grad, here, left, acc, core_s, core_r, x_send, x_recv, z_s, z_r, c_s, c_r, x_s, x_r = refs[:14]
    kept = refs[14:22]
    ins = refs[22 : 22 + N_GRADS]
    rows_out, grad_proj, other, e_s, e_r, tiles, local = refs[22 + N_GRADS : 29 + N_GRADS]
    refs = refs[29 + N_GRADS :]
    load = pltpu.make_async_copy(tiles_hbm, tiles, local)
    load.start()
    total = Total(ins, out, refs[: len(refs) // 2])
    last = Total([grad_proj], proj_out, refs[len(refs) // 2 :], paired=True)
    grad = pred_grad
    y, x, z, c = where_am_i()
    half = NZ // 2
    n_group = NX * NC
    chunk = grad.shape[0] // 2
    tokens = encoded.shape[0]
    cam = tokens // BLK
    sibling = at(y, x, z, 1 - c)

    def zz(offset):
        return lax.rem(z + offset + 2 * NZ, NZ)

    def xx(offset):
        return lax.rem(x + offset + NX, NX)

    beside = (at(y, x, zz(1), c), at(y, x, zz(-1), c))
    east, west = at(y, xx(1), z, c), at(y, xx(-1), z, c)
    barrier = pltpu.get_barrier_semaphore()
    for device in total.peers():
        pl.semaphore_signal(barrier, inc=1, device_id=device, device_id_type=MESH)

    def hops(ch, d):
        return half if ch == d else half - 1

    def part(origin, ch):
        return all_grad.at[origin, pl.ds(ch * chunk, chunk)]

    n1_ref, h1_ref, n2_ref, h2_ref, p1_ref, p2_ref, r1_ref, r2_ref = kept

    def heads(ch):
        r = slice(ch * chunk, (ch + 1) * chunk)

        def forward(state, w_up, w_down, n_ref, h_ref):
            scaling = lax.rsqrt(jnp.mean(state * state, axis=-1, keepdims=True) + eps)
            normed = (state * scaling).astype(BF)
            n_ref[r] = normed
            preact = jnp.dot(normed, w_up[...], preferred_element_type=F32)
            value, slope = gelu_parts(preact)
            hidden = value.astype(BF)
            h_ref[r] = hidden
            return state + jnp.dot(hidden, w_down[...], preferred_element_type=F32), scaling, slope

        def backward(g, state, scaling, slope, w_up, w_down, p_ref, r_ref):
            rounded = g.astype(BF)
            r_ref[r] = rounded
            grad_pre = (against_rows(rounded, w_down[...]) * slope).astype(BF)
            p_ref[r] = grad_pre
            grad_normed = against_rows(grad_pre, w_up[...])
            unit = state * scaling
            return g + scaling * (grad_normed - unit * jnp.mean(grad_normed * unit, axis=-1, keepdims=True))

        s0 = grid[r]
        s1, scale1, slope1 = forward(s0, ru, rd, n1_ref, h1_ref)
        s2, scale2, slope2 = forward(s1, du, dd, n2_ref, h2_ref)
        prediction[r] = s2.astype(BF)
        g1 = backward(pred_grad[r].astype(F32) * scale, s1, scale2, slope2, du, dd, p2_ref, r2_ref)
        g0 = backward(g1, s0, scale1, slope1, ru, rd, p1_ref, r1_ref)
        all_grad[z, r] = g0.astype(BF)

    for ch in range(2):
        heads(ch)
        if ch == 0:
            pl.semaphore_wait(barrier, len(total.peers()))
            send(encoded, other, e_s, e_r, sibling)
        for d in range(2):
            if hops(ch, d) >= 1:
                send(part(z, ch), part(z, ch), z_s.at[ch, d, 0], z_r.at[ch, d, 0], beside[d])
    ins[0][...] = contract_rows(n1_ref[...], p1_ref[...])
    ins[1][...] = contract_rows(h1_ref[...], r1_ref[...])
    ins[2][...] = contract_rows(n2_ref[...], p2_ref[...])
    ins[3][...] = contract_rows(h2_ref[...], r2_ref[...])
    total.start()

    def use(origin, first):
        p = (x * NZ + origin) * NC + c
        here[...] = all_grad[origin].reshape(here.shape)
        for g in range(n_group):
            tile = tiles[g, origin].astype(F32).T
            src = index[g, 0, p]
            alive = index[g, 2, p]
            for k in range(cam):
                weight = jnp.where(src == k, alive, 0).astype(F32)
                left[k * BLK : (k + 1) * BLK, :] = (tile * weight).astype(BF)
            product = jnp.dot(left[...], here[index[g, 1, p]], preferred_element_type=F32)
            if first:
                acc[g] = product
            else:
                acc[g] = acc[g] + product

    load.wait()
    use(z, True)
    total.over_xy()

    @pl.loop(1, half + 1)
    def _(k):
        for d in range(2):
            s = 1 - 2 * d
            origin = zz(-s * k)
            for ch in range(2):
                @pl.when(k <= hops(ch, d))
                def _(ch=ch, d=d):
                    arrived(part(origin, ch), z_r.at[ch, d, k - 1], beside[d])

                @pl.when(k + 1 <= hops(ch, d))
                def _(ch=ch, d=d):
                    send(part(origin, ch), part(origin, ch), z_s.at[ch, d, k], z_r.at[ch, d, k], beside[d])

        @pl.when(k == max(half - 2, 1))
        def _():
            total.over_z()

        @pl.when(k == max(half - 1, 1))
        def _():
            total.back_over_z()

        @pl.when(k == half)
        def _():
            total.back_over_xy()

        use(zz(-k), False)

        @pl.when(k < half)
        def _():
            use(zz(k), False)

    wide = grid.shape[1] // NC
    order = (2, 1, NX - 1, 0)

    def channels_of(core):
        return pl.ds(pl.multiple_of(core * wide, wide), wide)

    for i, o in enumerate(order):
        for h in range(NC):
            core_s[i, h] = acc[xx(o) * NC + h, :, channels_of(1 - c)].astype(BF)
        send(core_s.at[i], core_r.at[i], c_s.at[i], c_r.at[i], sibling)

    def pair_sum(i, h):
        return acc[xx(order[i]) * NC + h, :, channels_of(c)] + core_r[i, h].astype(F32)

    def push(n, value, device):
        x_send[n] = value.astype(BF)
        send(x_send.at[n], x_recv.at[n], x_s.at[n], x_r.at[n], device)

    for i in range(3):
        arrived(core_r.at[i], c_r.at[i], sibling)
        if i == 0:
            push(0, pair_sum(0, 0), east)
            push(1, pair_sum(0, 1), west)
        if i == 1:
            push(2, pair_sum(1, 1), east)
        if i == 2:
            push(3, pair_sum(2, 0), west)
    arrived(x_recv.at[0], x_r.at[0], sibling)
    push(4, pair_sum(1, 0) + x_recv[0].astype(F32), east)
    arrived(x_recv.at[1], x_r.at[1], sibling)
    push(5, pair_sum(2, 1) + x_recv[1].astype(F32), west)
    arrived(core_r.at[3], c_r.at[3], sibling)
    for n in range(2, 6):
        arrived(x_recv.at[n], x_r.at[n], sibling)
    rows_out[0] = (pair_sum(3, 0) + x_recv[4].astype(F32) + x_recv[3].astype(F32)).astype(BF)
    rows_out[1] = (pair_sum(3, 1) + x_recv[2].astype(F32) + x_recv[5].astype(F32)).astype(BF)
    arrived(other, e_r, sibling)
    grad_proj[...] = contract_rows(encoded[...], rows_out[c]) + contract_rows(other[...], rows_out[1 - c])
    last.start()
    total.back_over_core()
    last.over_xy()
    total.finish()
    last.over_z()
    last.back_over_z()
    last.back_over_xy()
    last.back_over_core()
    last.finish()
    sent(encoded, e_s, sibling)
    for i in range(4):
        sent(core_s.at[i], c_s.at[i], sibling)
    for n in range(6):
        sent(x_send.at[n], x_s.at[n], sibling)
    for ch in range(2):
        for d in range(2):
            for k in range(hops(ch, d)):
                sent(part(z, ch), z_s.at[ch, d, k], beside[d])


def split(index_all, grid, pred_grad, tiles_all, encoded, weights, scale):
    cells, channels = grid.shape
    tokens, features = encoded.shape
    hidden = weights[0].shape[1]
    n = NX * NC
    half = NZ // 2
    shapes = [w.shape for w in weights]

    def packed_of(some):
        rows = sum(a * b for a, b in some) // (NX * NY * NC * Total.width)
        return jax.ShapeDtypeStruct((NC, NX * NY, rows, Total.width), BF)

    return pl.pallas_call(
        functools.partial(split_kernel, scale=scale),
        out_shape=(
            jax.ShapeDtypeStruct((cells, channels), BF),
            packed_of([(features, channels)]),
            packed_of(shapes),
        ),
        in_specs=[SM, VM, VM, ANY, VM] + [VM] * N_GRADS,
        out_specs=(VM, VM, VM),
        scratch_shapes=[
            pltpu.VMEM((NZ, cells, channels), BF),
            pltpu.VMEM((cells // BLK, BLK, channels), BF),
            pltpu.VMEM((tokens, BLK), BF),
            pltpu.VMEM((n, tokens, channels), F32),
            pltpu.VMEM((NX, NC, tokens, channels // NC), BF),
            pltpu.VMEM((NX, NC, tokens, channels // NC), BF),
            pltpu.VMEM((6, tokens, channels // NC), BF),
            pltpu.VMEM((6, tokens, channels // NC), BF),
            DMA((2, 2, half)), DMA((2, 2, half)),
            DMA((NX,)), DMA((NX,)),
            DMA((6,)), DMA((6,)),
        ]
        + [pltpu.VMEM((cells, w), BF) for w in (channels, hidden) * 2 + (hidden, hidden, channels, channels)]
        + [pltpu.VMEM(a, F32) for a in shapes]
        + [pltpu.VMEM((NC, tokens, channels // NC), BF), pltpu.VMEM((features, channels // NC), F32)]
        + [pltpu.VMEM((tokens, features), BF), DMA(()), DMA(()), pltpu.VMEM(tiles_all.shape, BF), DMA(())]
        + Total.scratch_for(shapes)
        + Total.scratch_for([(features, channels)]),
        compiler_params=pltpu.CompilerParams(
            collective_id=2, has_side_effects=True, vmem_limit_bytes=VMEM_LIMIT
        ),
    )(index_all, grid, pred_grad, tiles_all, encoded, *weights)


def on_device(
    cams, vit_up, vit_down, proj, frustum_tiles, src_block, dst_block, live,
    render_up, render_down, decode_up, decode_down, pred_grad,
):
    tile_count = NX * NZ * NC
    cells, channels = pred_grad.shape[1:]
    encoded, x_all, tiles_all, index_all = encode(
        vit_up, vit_down, cams, proj, frustum_tiles[0], src_block, dst_block, live
    )
    bev_grid = join(index_all, x_all, tiles_all, cells)
    scale = 1.0 / math.sqrt(cams.shape[0] * cells * tile_count)
    weights = (render_up, render_down, decode_up, decode_down)
    prediction, first, second = split(index_all, bev_grid, pred_grad[0], tiles_all, encoded, weights, scale)
    prediction, *totals = unpack(first, second, prediction, [proj.shape] + [w.shape for w in weights])
    return (prediction[None], *totals)


def solution(mesh):
    placed = (
        P(None, "tile", None),
        P("section", None, None),
        P("section", None, None),
        P(),
        P("tile", None, None, None),
        P("tile", None),
        P("tile", None),
        P("tile", None),
        P(),
        P(),
        P(),
        P(),
        P("section", "tile", None),
    )
    return jax.shard_map(
        on_device,
        mesh=mesh,
        in_specs=placed,
        out_specs=(P("section", "tile", None), P(), P(), P(), P(), P()),
        check_vma=False,
    )
```

```python
import functools
import math

import jax
import jax.numpy as jnp
from jax import lax
from jax.experimental import pallas as pl
from jax.experimental.pallas import tpu as pltpu
from jax.sharding import PartitionSpec as P

eps = 1e-05
MESH = pl.DeviceIdType.MESH
BF = jnp.bfloat16
F32 = jnp.float32
NY, NX, NZ, NC = 4, 4, 8, 2
BLK = 128
VMEM_LIMIT = 60 * 2**20
ANY = pl.BlockSpec(memory_space=pl.ANY)
VM = pl.BlockSpec(memory_space=pltpu.VMEM)
SM = pl.BlockSpec(memory_space=pltpu.SMEM)
DMA = pltpu.SemaphoreType.DMA


def where_am_i():
    y = lax.axis_index("section")
    t = lax.axis_index("tile")
    return y, t // (NZ * NC), (t // NC) % NZ, t % NC


def at(y, x, z, c):
    return (y, (x * NZ + z) * NC + c)


def send(src, dst, ssem, rsem, device):
    copy = pltpu.make_async_remote_copy(
        src_ref=src, dst_ref=dst, send_sem=ssem, recv_sem=rsem, device_id=device, device_id_type=MESH
    )
    copy.start()


def sent(src, ssem, device):
    pltpu.make_async_remote_copy(
        src_ref=src, dst_ref=src, send_sem=ssem, recv_sem=ssem, device_id=device, device_id_type=MESH
    ).wait_send()


def arrived(dst, rsem, device):
    pltpu.make_async_remote_copy(
        src_ref=dst, dst_ref=dst, send_sem=rsem, recv_sem=rsem, device_id=device, device_id_type=MESH
    ).wait_recv()


def greet(devices):
    barrier = pltpu.get_barrier_semaphore()
    for device in devices:
        pl.semaphore_signal(barrier, inc=1, device_id=device, device_id_type=MESH)
    pl.semaphore_wait(barrier, len(devices))


def gelu(v):
    return 0.5 * v * (1.0 + jnp.tanh(math.sqrt(2.0 / math.pi) * (v + 0.044715 * v * v * v)))


def contract_rows(left, right):
    return lax.dot_general(left, right, (((0,), (0,)), ((), ())), preferred_element_type=F32)


def against_rows(left, right):
    return lax.dot_general(left, right, (((1,), (1,)), ((), ())), preferred_element_type=F32)


def encoder_kernel(
    up, down, cams, proj, tiles, src, dst, live,
    encoded, x_all, tiles_all, index_all,
    w_up, w_down, own, y_s, y_r, x_s, x_r, u_s, u_r, z_s, z_r, b_s, b_r, t_s, t_r, i_s, i_r, p_s, p_r, v_s, v_r, w_s, w_r,
    local, index,
):
    y, x, z, c = where_am_i()
    sibling = at(y, x, z, 1 - c)
    group = x * NC + c
    moved = NY - 1
    half = NZ // 2
    steps = half + 1
    n_group = NX * NC
    plane_up, plane_down = 2 * w_up.shape[-1] // 3, 2 * w_down.shape[-1] // 3
    cols = plane_up // 2
    quarter = BLK // NY

    def layer_of(j):
        return j + jnp.where(j >= y, 1, 0)

    def up_slice(l, xx):
        return w_up.at[l, z, xx // 2, :, pl.ds(pl.multiple_of((xx % 2) * cols, 128), cols)]

    def up_block(l, zo):
        return w_up.at[l, zo, :, :, pl.ds(0, plane_up)]

    def down_slice(l, zo):
        return w_down.at[l, zo, x, :, pl.ds(0, plane_down)]

    def down_block(l, xo):
        return w_down.at[l, :, xo, :, pl.ds(0, plane_down)]

    def y_part(l, core, h):
        if core == 0:
            width = (w_up.shape[-1] - plane_up) // 2
            return w_up.at[l, :, :, :, pl.ds(plane_up + h * width, width)]
        return w_down.at[l, pl.ds(h * half, half), :, :, pl.ds(plane_down, w_down.shape[-1] - plane_down)]

    def zz(offset):
        return lax.rem(z + offset + 2 * NZ, NZ)

    def xx(offset):
        return lax.rem(x + offset + NX, NX)

    def yy(offset):
        return lax.rem(y + offset + NY, NY)

    def gg(offset):
        return lax.rem(group + offset + n_group, n_group)

    def g_dev(g):
        return at(y, g // NC, z, g % NC)

    east, west = at(y, xx(1), z, c), at(y, xx(-1), z, c)
    north, south = at(yy(1), x, z, c), at(yy(-1), x, z, c)

    def tile_rows(ref, section):
        return ref.at[:, pl.ds(pl.multiple_of(section * quarter, quarter), quarter), :]

    index[...] = jnp.zeros_like(index)
    for i, ref in enumerate((src, dst, live)):
        index[i : i + 1, 0 : ref.shape[1]] = ref[...]
    loads = [
        pltpu.make_async_copy(up, w_up.at[y], local.at[0]),
        pltpu.make_async_copy(down, w_down.at[y], local.at[1]),
        pltpu.make_async_copy(cams.at[y], encoded, local.at[2]),
        pltpu.make_async_copy(tile_rows(tiles.at[x, :, c], y), tile_rows(tiles_all.at[group], y), local.at[3]),
        pltpu.make_async_copy(index, index_all.at[group], local.at[4]),
    ]
    for load in loads:
        load.start()
    greet(
        [at(yy(o), x, z, c) for o in range(1, NY)]
        + [g_dev(gg(o)) for o in range(1, n_group)]
        + [at(y, x, zz(o), c) for o in ((1, -1, 2, -2) if NZ == 8 else (1, -1))]
    )
    for load in loads[:3]:
        load.wait()

    def share(l, core):
        return up_slice(l, x) if core == 0 else down_slice(l, z)

    for core in range(NC):
        @pl.when(c == core)
        def _(core=core):
            for o in range(1, NY):
                send(share(y, core), share(y, core), y_s.at[o - 1], y_r.at[o - 1], at(yy(o), x, z, c))
            for h, i, device in ((0, 0, north), (1, 3, south), (1, 1, north), (0, 2, south)):
                send(y_part(y, core, h), y_part(y, core, h), v_s.at[i], v_r.at[i], device)

    def sign(j, d):
        return (1 - 2 * (j % 2)) * (1 - 2 * d)

    def send_tiles():
        for o in range(1, n_group):
            g = gg(o)
            send(index, index_all.at[group], i_s.at[o - 1], i_r.at[o - 1], g_dev(g))
            send(
                tile_rows(tiles.at[g // NC, :, g % NC], y), tile_rows(tiles_all.at[group], y),
                t_s.at[o - 1], t_r.at[o - 1], g_dev(g),
            )

    first_hops = (1, -1, 2, -2) if NZ == 8 else tuple(range(1, NZ))
    later_hops = ((4, 1, 2), (5, 2, 2), (6, -1, -2)) if NZ == 8 else ()

    def sem_of(sems, j, i):
        return sems.at[j, i // half, i % half]

    def slice_to(j, l, i, off, origin):
        s = sign(j, 0)
        block = down_slice(l, zz(-s * origin))
        send(block, block, sem_of(z_s, j, i), sem_of(z_r, j, i), at(y, x, zz(s * off), c))

    def go_on(j):
        l = layer_of(j)
        for i, off, origin in later_hops:
            if i != 5:
                first = first_hops.index(origin)
                arrived(down_slice(l, zz(-sign(j, 0) * origin)), sem_of(z_r, j, first), sibling)
            slice_to(j, l, i, off, origin)

    def slices_arrived(j, l):
        s = sign(j, 0)
        for i, off in enumerate(first_hops):
            if off not in [origin for _, _, origin in later_hops]:
                arrived(down_slice(l, zz(-s * off)), sem_of(z_r, j, i), sibling)
        for i, off, origin in later_hops:
            arrived(down_slice(l, zz(-s * (off + origin))), sem_of(z_r, j, i), sibling)

    @pl.when(c == 0)
    def _():
        @pl.loop(0, moved)
        def _(j):
            l = layer_of(j)
            o = yy(-l)
            arrived(share(l, 0), y_r.at[o - 1], sibling)
            for ox in range(1, NX):
                send(up_slice(l, x), up_slice(l, x), u_s.at[j, ox - 1], u_r.at[j, ox - 1], at(y, xx(ox), z, c))
        send_tiles()

    def z_hops(d):
        return half if d == 0 else half - 1

    @pl.when(c == 1)
    def _():
        @pl.loop(0, moved)
        def _(j):
            l = layer_of(j)
            arrived(share(l, 1), y_r.at[yy(-l) - 1], sibling)
            for i, off in enumerate(first_hops):
                slice_to(j, l, i, off, 0)
        send_tiles()
        go_on(0)

    def layer_rows(l, r, rows):
        wide = encoded[pl.ds(r, rows), :].astype(F32)
        scaling = lax.rsqrt(jnp.mean(wide * wide, axis=-1, keepdims=True) + eps)
        normed = (wide * scaling).astype(BF)
        total = wide
        parts = 2
        for q in range(parts):
            width = w_up.shape[-1] // parts
            w1 = w_up[l, :, :, :, q * width : (q + 1) * width].reshape(wide.shape[1], width)
            hidden = gelu(jnp.dot(normed, w1, preferred_element_type=F32)).astype(BF)
            nz = NZ // parts
            w2 = w_down[l, q * nz : (q + 1) * nz].reshape(width, wide.shape[1])
            total = total + jnp.dot(hidden, w2, preferred_element_type=F32)
        encoded[pl.ds(r, rows), :] = total.astype(BF)

    tokens = encoded.shape[0]
    rows = tokens // 2

    def wait_sibling(j):
        l = layer_of(j)

        @pl.when(c == 0)
        def _():
            for i, ox in enumerate((0, 1, NX - 1, 2)):
                arrived(down_block(l, xx(-ox)), b_r.at[j, i], sibling)

        @pl.when(c == 1)
        def _():
            arrived(up_block(l, z), b_r.at[j, 0], sibling)
            for d in range(2):
                for k in range(2, z_hops(d) + 2):
                    arrived(up_block(l, zz(-sign(j, d) * (k - 1))), b_r.at[j, 1 + d * half + k - 2], sibling)

    def second_half(l, xo, h):
        return w_down.at[l, pl.ds(h * half, half), xo, :, pl.ds(0, plane_down)]

    def begin(j):
        l = layer_of(j)

        @pl.when(c == 0)
        def _():
            for ox in range(1, NX):
                arrived(up_slice(l, xx(-ox)), u_r.at[j, ox - 1], sibling)
            block = up_block(l, z)
            for d in range(2):
                if z_hops(d) >= 1:
                    send(block, block, z_s.at[j, d, 0], z_r.at[j, d, 0], at(y, x, zz(sign(j, d)), c))
            send(block, block, b_s.at[j, 0], b_r.at[j, 0], sibling)

        @pl.when(c == 1)
        def _():
            slices_arrived(j, l)
            block = down_block(l, x)
            send(block, block, x_s.at[j, 0], x_r.at[j, 0], east)
            send(block, block, x_s.at[j, 1], x_r.at[j, 1], west)
            send(block, block, b_s.at[j, 0], b_r.at[j, 0], sibling)

    def own_rows(section):
        return tiles_all.at[:, :, pl.ds(pl.multiple_of(section * quarter, quarter), quarter), :]

    def some_rows(section, h):
        return tiles_all.at[
            pl.ds(h * n_group // 2, n_group // 2), :, pl.ds(pl.multiple_of(section * quarter, quarter), quarter), :
        ]

    t0 = n_group - 1

    def y_piece(i):
        return (yy(-1), yy(-1), yy(1), yy(1), yy(2), yy(2))[i], (0, 1, 0, 1, 0, 1)[i]

    def take_y(i):
        l, h = y_piece(i)
        for core in range(NC):
            @pl.when(c == core)
            def _(core=core):
                piece = y_part(l, core, h)
                arrived(piece, v_r.at[i], sibling)
                if i == 0:
                    send(piece, piece, v_s.at[4], v_r.at[4], north)
                if i == 3:
                    send(piece, piece, v_s.at[5], v_r.at[5], south)
                send(piece, piece, w_s.at[i], w_r.at[i], sibling)

    last = max(steps, 5)

    @pl.loop(1, moved - 1 + last + 1)
    def _(slot):
        @pl.loop(0, moved)
        def _(j):
            k = slot - j
            l = layer_of(j)

            @pl.when(jnp.logical_and(c == 0, k >= 2))
            def _():
                for d in range(2):
                    s = sign(j, d)
                    block = up_block(l, zz(-s * (k - 1)))

                    @pl.when(k <= z_hops(d) + 1)
                    def _():
                        arrived(block, z_r.at[j, d, k - 2], sibling)

                        @pl.when(k <= z_hops(d))
                        def _():
                            send(block, block, z_s.at[j, d, k - 1], z_r.at[j, d, k - 1], at(y, x, zz(s), c))

                        send(block, block, b_s.at[j, 1 + d * half + k - 2], b_r.at[j, 1 + d * half + k - 2], sibling)

            @pl.when(jnp.logical_and(c == 1, k == 3))
            def _():
                block = down_block(l, xx(-1))
                arrived(block, x_r.at[j, 0], sibling)
                send(second_half(l, xx(-1), 0), second_half(l, xx(-1), 0), x_s.at[j, 2], x_r.at[j, 2], east)
                send(block, block, b_s.at[j, 1], b_r.at[j, 1], sibling)
                other = down_block(l, xx(1))
                arrived(other, x_r.at[j, 1], sibling)
                send(second_half(l, xx(1), 1), second_half(l, xx(1), 1), x_s.at[j, 3], x_r.at[j, 3], west)
                send(other, other, b_s.at[j, 2], b_r.at[j, 2], sibling)

            @pl.when(jnp.logical_and(c == 1, k == last))
            def _():
                arrived(second_half(l, xx(2), 0), x_r.at[j, 2], sibling)
                arrived(second_half(l, xx(2), 1), x_r.at[j, 3], sibling)
                block = down_block(l, xx(2))
                send(block, block, b_s.at[j, 3], b_r.at[j, 3], sibling)

            @pl.when(k == 1)
            def _():
                begin(j)

            @pl.when(jnp.logical_and(c == 1, k == 0))
            def _():
                go_on(j)

        for when, pieces in ((1, (0, 3)), (3, (1, 2)), (5, (4, 5))):
            @pl.when(slot == when)
            def _(pieces=pieces):
                for i in pieces:
                    take_y(i)

        @pl.when(slot == last)
        def _():
            for load in loads[3:]:
                load.wait()
            for o in range(1, n_group):
                arrived(tile_rows(tiles_all.at[gg(-o)], y), t_r.at[o - 1], sibling)
            send(own_rows(y), own_rows(y), t_s.at[t0], t_r.at[t0], north)
            send(own_rows(y), own_rows(y), t_s.at[t0 + 1], t_r.at[t0 + 1], south)

        @pl.when(slot == last + 1)
        def _():
            for i in range(6):
                l, h = y_piece(i)
                for core in range(NC):
                    @pl.when(c != core)
                    def _(core=core):
                        arrived(y_part(l, core, h), w_r.at[i], sibling)

        @pl.when(slot > last)
        def _():
            wait_sibling(slot - last - 1)
            layer_rows(slot - last - 1, 0, tokens)

    wait_sibling(moved - 1)

    layer_rows(NY - 2, 0, tokens)

    arrived(own_rows(yy(-1)), t_r.at[t0], sibling)
    send(some_rows(yy(-1), 0), some_rows(yy(-1), 0), t_s.at[t0 + 2], t_r.at[t0 + 2], north)
    arrived(own_rows(yy(1)), t_r.at[t0 + 1], sibling)
    send(some_rows(yy(1), 1), some_rows(yy(1), 1), t_s.at[t0 + 3], t_r.at[t0 + 3], south)
    layer_rows(NY - 1, 0, rows)

    def half_of(g, h):
        return x_all.at[g, pl.ds(h * rows, rows), :]

    def project(h):
        mine = own.at[h * rows : (h + 1) * rows]
        mine[...] = jnp.dot(encoded[h * rows : (h + 1) * rows], proj[...], preferred_element_type=F32).astype(BF)
        send(mine, half_of(group, h), p_s.at[h], p_r.at[h], east)
        send(mine, half_of(group, h), p_s.at[2 + h], p_r.at[2 + h], west)
        send(mine, half_of(group, h), p_s.at[4 + h], p_r.at[4 + h], sibling)

    project(0)
    layer_rows(NY - 1, rows, rows)
    project(1)
    keep = pltpu.make_async_copy(own, x_all.at[group], local.at[5])
    keep.start()
    near, far = (xx(-1) * NC + c, xx(1) * NC + c), xx(2) * NC + c
    arrived(half_of(near[0], 0), p_r.at[0], sibling)
    send(half_of(near[0], 0), half_of(near[0], 0), p_s.at[6], p_r.at[6], east)
    arrived(half_of(near[1], 0), p_r.at[2], sibling)
    arrived(half_of(near[1], 1), p_r.at[3], sibling)
    send(half_of(near[1], 1), half_of(near[1], 1), p_s.at[7], p_r.at[7], west)
    send(x_all.at[near[1]], x_all.at[near[1]], p_s.at[9], p_r.at[9], sibling)
    arrived(half_of(near[0], 1), p_r.at[1], sibling)
    send(x_all.at[near[0]], x_all.at[near[0]], p_s.at[8], p_r.at[8], sibling)
    arrived(half_of(far, 0), p_r.at[6], sibling)
    arrived(half_of(far, 1), p_r.at[7], sibling)
    send(x_all.at[far], x_all.at[far], p_s.at[10], p_r.at[10], sibling)
    for h in range(2):
        arrived(half_of(x * NC + 1 - c, h), p_r.at[4 + h], sibling)
    for i, ox in enumerate((-1, 1, 2)):
        arrived(x_all.at[xx(ox) * NC + 1 - c], p_r.at[8 + i], sibling)

    keep.wait()
    arrived(some_rows(yy(2), 0), t_r.at[t0 + 2], sibling)
    arrived(some_rows(yy(2), 1), t_r.at[t0 + 3], sibling)
    for o in range(1, n_group):
        arrived(index_all.at[gg(-o)], i_r.at[o - 1], sibling)
        sent(tile_rows(tiles_all.at[group], y), t_s.at[o - 1], sibling)
        sent(index_all.at[group], i_s.at[o - 1], sibling)
    for i in range(2):
        sent(own_rows(y), t_s.at[t0 + i], sibling)
        sent(some_rows(y, 0), t_s.at[t0 + 2 + i], sibling)
    for i in range(8):
        sent(own.at[0:rows], p_s.at[i], sibling)
    for i in range(8, 11):
        sent(own, p_s.at[i], sibling)
    for core in range(NC):
        @pl.when(c == core)
        def _(core=core):
            for o in range(1, NY):
                sent(share(y, core), y_s.at[o - 1], sibling)
            for i in range(6):
                sent(y_part(y, core, 0), v_s.at[i], sibling)
                sent(y_part(y, core, 0), w_s.at[i], sibling)

    @pl.loop(0, moved)
    def _(j):
        @pl.when(c == 0)
        def _():
            for ox in range(1, NX):
                sent(up_slice(y, x), u_s.at[j, ox - 1], sibling)
            for d in range(2):
                for k in range(1, z_hops(d) + 1):
                    sent(up_block(y, z), z_s.at[j, d, k - 1], sibling)
            for i in range(NZ):
                sent(up_block(y, z), b_s.at[j, i], sibling)

        @pl.when(c == 1)
        def _():
            for i in range(2):
                sent(down_block(y, x), x_s.at[j, i], sibling)
                sent(second_half(y, x, 0), x_s.at[j, 2 + i], sibling)
            for i in range(NZ - 1):
                sent(down_slice(y, z), sem_of(z_s, j, i), sibling)
            for i in range(NX):
                sent(down_block(y, x), b_s.at[j, i], sibling)


def encode(up, down, cams, proj, tiles, src, dst, live):
    d, f = up.shape[1:]
    tokens = cams.shape[1]
    channels = proj.shape[1]
    up = up.reshape(NZ, NX // 2, 2 * d // (NZ * NX), f)
    down = down.reshape(NZ, NX, f // (NZ * NX), d)
    tiles = tiles.reshape(NX, NZ, NC, BLK, BLK)
    n = NX * NC
    half = NZ // 2
    moved = NY - 1
    return pl.pallas_call(
        encoder_kernel,
        out_shape=(
            jax.ShapeDtypeStruct((tokens, d), BF),
            jax.ShapeDtypeStruct((n, tokens, channels), BF),
            jax.ShapeDtypeStruct((n, NZ, BLK, BLK), BF),
            jax.ShapeDtypeStruct((n, 8, 128), jnp.int32),
        ),
        in_specs=[ANY, ANY, ANY, VM, ANY, VM, VM, VM],
        out_specs=(VM, ANY, ANY, ANY),
        scratch_shapes=[
            pltpu.VMEM((NY,) + up.shape, BF),
            pltpu.VMEM((NY,) + down.shape, BF),
            pltpu.VMEM((tokens, channels), BF),
            DMA((NY - 1,)), DMA((NY - 1,)),
            DMA((moved, 4)), DMA((moved, 4)),
            DMA((moved, NX - 1)), DMA((moved, NX - 1)),
            DMA((moved, 2, half)), DMA((moved, 2, half)),
            DMA((moved, max(NZ, NX))), DMA((moved, max(NZ, NX))),
            DMA((n + 3,)), DMA((n + 3,)),
            DMA((n - 1,)), DMA((n - 1,)),
            DMA((11,)), DMA((11,)),
            DMA((6,)), DMA((6,)),
            DMA((6,)), DMA((6,)),
            DMA((6,)),
            pltpu.VMEM((8, 128), jnp.int32),
        ],
        compiler_params=pltpu.CompilerParams(
            collective_id=0, has_side_effects=True, vmem_limit_bytes=VMEM_LIMIT
        ),
    )(up, down, cams, proj, tiles, src, dst, live)


def join_kernel(index, x_hbm, tiles_hbm, grid_out, x_all, tiles, local, left, right, parts, s_buf, r_buf, s_sem, r_sem):
    y, x, z, c = where_am_i()
    half = NZ // 2
    n_group = NX * NC
    bev = grid_out.shape[0] // BLK
    chunk = grid_out.shape[0] // 2

    def zz(offset):
        return lax.rem(z + offset + 2 * NZ, NZ)

    loads = [
        pltpu.make_async_copy(x_hbm, x_all, local.at[0]),
        pltpu.make_async_copy(tiles_hbm, tiles, local.at[1]),
    ]
    for load in loads:
        load.start()
    beside = (at(y, x, zz(1), c), at(y, x, zz(-1), c))
    greet(beside)
    for load in loads:
        load.wait()

    def hops(ch, d):
        return half if ch == d else half - 1

    def push(ch, d, k):
        send(s_buf.at[ch, d, k - 1], r_buf.at[ch, d, k - 1], s_sem.at[ch, d, k - 1], r_sem.at[ch, d, k - 1], beside[d])

    @pl.loop(0, NZ)
    def _(i):
        off = jnp.where(i == 0, half, jnp.where(i % 2 == 1, (NZ - 1 - i) // 2, -((NZ - i) // 2)))
        target = zz(off)
        p = (x * NZ + target) * NC + c
        for g in range(n_group):
            tile = tiles[g, target].astype(F32)
            dst = index[g, 1, p]
            alive = index[g, 2, p]
            for b in range(bev):
                weight = jnp.where(dst == b, alive, 0).astype(F32)
                left[b * BLK : (b + 1) * BLK, g * BLK : (g + 1) * BLK] = (tile * weight).astype(BF)
            right[g * BLK : (g + 1) * BLK, :] = x_all[g, index[g, 0, p]]
        parts[i] = jnp.dot(left[...], right[...], preferred_element_type=F32)

        @pl.when(i == 0)
        def _():
            for d in range(2):
                s_buf[d, d, 0] = parts[0, d * chunk : (d + 1) * chunk].astype(BF)
                push(d, d, 1)

        for d in range(2):
            if half == 1:
                continue

            @pl.when(i == 1 + d)
            def _(d=d):
                ch = 1 - d
                s_buf[ch, d, 0] = parts[1 + d, ch * chunk : (ch + 1) * chunk].astype(BF)
                push(ch, d, 1)

    for o in range(half - 1, 0, -1):
        for ch_is_d in (True, False):
            for d in range(2):
                ch = d if ch_is_d else 1 - d
                k = hops(ch, d) - o + 1
                if k == 1:
                    continue
                arrived(r_buf.at[ch, d, k - 2], r_sem.at[ch, d, k - 2], beside[d])
                i = NZ - 1 - 2 * o if d == 0 else NZ - 2 * o
                total = parts[i, ch * chunk : (ch + 1) * chunk] + r_buf[ch, d, k - 2].astype(F32)
                s_buf[ch, d, k - 1] = total.astype(BF)
                push(ch, d, k)
    for ch in range(2):
        total = parts[NZ - 1, ch * chunk : (ch + 1) * chunk]
        for d in range(2):
            k = hops(ch, d)
            if k == 0:
                continue
            arrived(r_buf.at[ch, d, k - 1], r_sem.at[ch, d, k - 1], beside[d])
            total = total + r_buf[ch, d, k - 1].astype(F32)
        grid_out[ch * chunk : (ch + 1) * chunk] = total
    for ch in range(2):
        for d in range(2):
            for k in range(hops(ch, d)):
                sent(s_buf.at[ch, d, k], s_sem.at[ch, d, k], beside[d])


def join(index_all, x_all, tiles_all, cells):
    channels = x_all.shape[-1]
    x_all = x_all.reshape(x_all.shape[0], -1, BLK, channels)
    n = NX * NC
    half = NZ // 2
    return pl.pallas_call(
        join_kernel,
        out_shape=jax.ShapeDtypeStruct((cells, channels), F32),
        in_specs=[SM, ANY, ANY],
        out_specs=VM,
        scratch_shapes=[
            pltpu.VMEM(x_all.shape, BF),
            pltpu.VMEM(tiles_all.shape, BF),
            DMA((2,)),
            pltpu.VMEM((cells, n * BLK), BF),
            pltpu.VMEM((n * BLK, channels), BF),
            pltpu.VMEM((NZ, cells, channels), F32),
            pltpu.VMEM((2, 2, half, cells // 2, channels), BF),
            pltpu.VMEM((2, 2, half, cells // 2, channels), BF),
            DMA((2, 2, half)), DMA((2, 2, half)),
        ],
        compiler_params=pltpu.CompilerParams(
            collective_id=1, has_side_effects=True, vmem_limit_bytes=VMEM_LIMIT
        ),
    )(index_all, x_all, tiles_all)


def pieces_of(shapes):
    row = 0
    for i, (rows, columns) in enumerate(shapes):
        height = rows // (NX * NY)
        for col in range(0, columns, 256):
            yield i, row, height, col
            row += height


def unpack_kernel(first, second, prediction, *outs):
    for packed, refs in ((first, outs[1:2]), (second, outs[2:])):
        width = packed.shape[3]
        for i, row, height, col in pieces_of([ref.shape for ref in refs]):
            for q in range(NX * NY):
                for core in range(NC):
                    refs[i][q * height : (q + 1) * height, col + core * width : col + (core + 1) * width] = packed[
                        core, q, row : row + height, :
                    ].astype(F32)
    outs[0][...] = prediction[...]


def unpack(first, second, prediction, shapes):
    return pl.pallas_call(
        unpack_kernel,
        out_shape=(jax.ShapeDtypeStruct(prediction.shape, BF),) + tuple(jax.ShapeDtypeStruct(a, F32) for a in shapes),
        in_specs=[VM] * 3,
        out_specs=tuple([VM] * (1 + len(shapes))),
        compiler_params=pltpu.CompilerParams(vmem_limit_bytes=VMEM_LIMIT),
    )(first, second, prediction)


class Total:
    n1, n2, width = NX * NY, NZ, 128

    def __init__(self, ins, out, scratch, paired=False):
        self.ins, self.out, self.paired = ins, out, paired
        (
            self.packed, self.from0, self.half, self.from1, self.mid, self.from2, self.mine, self.gathered, self.result,
            self.s0, self.r0, self.s1, self.r1, self.s2, self.r2, self.s3, self.r3, self.s4, self.r4, self.s5, self.r5,
        ) = scratch
        y, x, z, c = where_am_i()
        self.y, self.x, self.z, self.c = y, x, z, c
        self.one, self.two = y * NX + x, z
        self.sibling = at(y, x, z, 1 - c)
        self.real = self.half.shape[1]
        self.share = self.mine.shape[0]

    @classmethod
    def scratch_for(cls, shapes, paired=False):
        n1, n2, width = NX * NY, NZ, cls.width
        real = sum(a * b for a, b in shapes) // (n1 * NC * width)
        share = -(-real // (n2 * 16)) * 16
        buffers = [
            (NC, n1, real, width), (n1, real, width), (n1, real, width), (n1 - 1, real, width), (share * n2, width),
            (n2, real, width) if paired else (n2 - 1, share, width),
            (share, width), (share * n2, width), (NC, n1, real, width),
        ]
        counts = [1, n1 - 1, n2 - 1, n2 - 1, n1 - 1, 1]
        return [pltpu.VMEM(b, BF) for b in buffers] + [DMA((n,)) for n in counts for _ in range(2)]

    def dev1(self, q):
        return at(q // NX, q % NX, self.z, self.c)

    def dev2(self, e):
        return at(self.y, self.x, e, self.c)

    def q1(self, o):
        n1 = NX * NY
        return lax.rem(self.one + o + n1, n1)

    def q2(self, o):
        return lax.rem(self.two + o + NZ, NZ)

    def peers(self):
        n1 = NX * NY
        return [self.sibling] + [self.dev1(self.q1(o)) for o in range(1, n1)] + [self.dev2(self.q2(o)) for o in range(1, NZ)]

    def pieces(self):
        return pieces_of([ref.shape for ref in self.ins])

    def start(self):
        n1 = NX * NY
        if self.paired:
            self.mid[...] = jnp.zeros_like(self.mid)
            return

        @pl.loop(0, n1)
        def _(q):
            for i, row, height, col in self.pieces():
                for core in range(NC):
                    left = col + core * self.width
                    self.packed[core, q, row : row + height, :] = self.ins[i][
                        pl.ds(pl.multiple_of(q * height, height), height), left : left + self.width
                    ].astype(BF)
        send(self.packed.at[1 - self.c], self.from0, self.s0.at[0], self.r0.at[0], self.sibling)
        self.mid[...] = jnp.zeros_like(self.mid)

    def over_xy(self):
        n1 = NX * NY
        if not self.paired:
            arrived(self.from0, self.r0.at[0], self.sibling)

        @pl.loop(0, n1)
        def _(o):
            q = lax.rem(self.one + 1 + o, n1)
            if self.paired:
                height = self.half.shape[1]
                self.half[q] = self.ins[0][pl.ds(pl.multiple_of(q * height, height), height), :].astype(BF)
            else:
                self.half[q] = (self.packed[self.c, q].astype(F32) + self.from0[q].astype(F32)).astype(BF)

            @pl.when(o < n1 - 1)
            def _():
                send(self.half.at[q], self.from1.at[o], self.s1.at[o], self.r1.at[o], self.dev1(q))

    def part(self, ref, e):
        return ref.at[pl.ds(pl.multiple_of(e * self.share, self.share), self.share), :]

    def over_z(self):
        total = self.half[self.one].astype(F32)
        for o in range(NX * NY - 1):
            arrived(self.from1.at[o], self.r1.at[o], self.sibling)
            total = total + self.from1[o].astype(F32)
        self.mid[0 : self.real, :] = total.astype(BF)
        if self.paired:
            self.from2[self.two] = self.mid[0 : self.real, :]
            for o in range(1, NZ):
                send(
                    self.mid.at[0 : self.real, :], self.from2.at[self.two],
                    self.s2.at[o - 1], self.r2.at[o - 1], self.dev2(self.q2(o)),
                )
            return
        for o in range(1, NZ):
            e = self.q2(o)
            send(self.part(self.mid, e), self.from2.at[o - 1], self.s2.at[o - 1], self.r2.at[o - 1], self.dev2(e))

    def back_over_z(self):
        if self.paired:
            for o in range(1, NZ):
                arrived(self.from2.at[self.q2(-o)], self.r2.at[o - 1], self.sibling)
            total = self.from2[0].astype(F32)
            for e in range(1, NZ):
                total = total + self.from2[e].astype(F32)
            self.gathered[0 : self.real, :] = total.astype(BF)
            return
        total = self.mid[pl.ds(pl.multiple_of(self.two * self.share, self.share), self.share), :].astype(F32)
        for o in range(1, NZ):
            arrived(self.from2.at[o - 1], self.r2.at[o - 1], self.sibling)
            total = total + self.from2[o - 1].astype(F32)
        self.mine[...] = total.astype(BF)
        for o in range(1, NZ):
            send(self.mine, self.part(self.gathered, self.two), self.s3.at[o - 1], self.r3.at[o - 1], self.dev2(self.q2(o)))
        self.gathered[pl.ds(pl.multiple_of(self.two * self.share, self.share), self.share), :] = self.mine[...]

    def back_over_xy(self):
        for o in range(1, 1 if self.paired else NZ):
            arrived(self.part(self.gathered, self.q2(-o)), self.r3.at[o - 1], self.sibling)
        for o in range(1, NX * NY):
            send(
                self.gathered.at[0 : self.real, :], self.result.at[self.c, self.one],
                self.s4.at[o - 1], self.r4.at[o - 1], self.dev1(self.q1(o)),
            )
        self.result[self.c, self.one] = self.gathered[0 : self.real, :]

    def back_over_core(self):
        for o in range(1, NX * NY):
            arrived(self.result.at[self.c, self.q1(-o)], self.r4.at[o - 1], self.sibling)
        send(self.result.at[self.c], self.result.at[self.c], self.s5.at[0], self.r5.at[0], self.sibling)

    def finish(self):
        n1 = NX * NY
        arrived(self.result.at[1 - self.c], self.r5.at[0], self.sibling)

        self.out[...] = self.result[...]
        if not self.paired:
            sent(self.from0, self.s0.at[0], self.sibling)
        sent(self.result.at[self.c], self.s5.at[0], self.sibling)
        for o in range(n1 - 1):
            sent(self.half.at[0], self.s1.at[o], self.sibling)
            sent(self.half.at[0], self.s4.at[o], self.sibling)
        for o in range(NZ - 1):
            sent(self.mid.at[0 : self.real, :] if self.paired else self.mine, self.s2.at[o], self.sibling)
            if not self.paired:
                sent(self.mine, self.s3.at[o], self.sibling)


N_GRADS = 4


def gelu_parts(v):
    inner = math.sqrt(2.0 / math.pi) * (v + 0.044715 * v * v * v)
    slope = math.sqrt(2.0 / math.pi) * (1.0 + 3.0 * 0.044715 * v * v)
    t = jnp.tanh(inner)
    return 0.5 * v * (1.0 + t), 0.5 * (1.0 + t) + 0.5 * v * (1.0 - t * t) * slope


def split_kernel(index, grid, pred_grad, tiles_hbm, encoded, ru, rd, du, dd, *refs, scale):
    prediction, proj_out, out, refs = refs[0], refs[1], refs[2], refs[3:]
    all_grad, here, left, acc, core_s, core_r, x_send, x_recv, z_s, z_r, c_s, c_r, x_s, x_r = refs[:14]
    kept = refs[14:22]
    ins = refs[22 : 22 + N_GRADS]
    rows_out, grad_proj, other, e_s, e_r, tiles, local = refs[22 + N_GRADS : 29 + N_GRADS]
    refs = refs[29 + N_GRADS :]
    load = pltpu.make_async_copy(tiles_hbm, tiles, local)
    load.start()
    total = Total(ins, out, refs[: len(refs) // 2])
    last = Total([grad_proj], proj_out, refs[len(refs) // 2 :], paired=True)
    grad = pred_grad
    y, x, z, c = where_am_i()
    half = NZ // 2
    n_group = NX * NC
    chunk = grad.shape[0] // 2
    tokens = encoded.shape[0]
    cam = tokens // BLK
    sibling = at(y, x, z, 1 - c)

    def zz(offset):
        return lax.rem(z + offset + 2 * NZ, NZ)

    def xx(offset):
        return lax.rem(x + offset + NX, NX)

    beside = (at(y, x, zz(1), c), at(y, x, zz(-1), c))
    east, west = at(y, xx(1), z, c), at(y, xx(-1), z, c)
    barrier = pltpu.get_barrier_semaphore()
    for device in total.peers():
        pl.semaphore_signal(barrier, inc=1, device_id=device, device_id_type=MESH)

    def hops(ch, d):
        return half if ch == d else half - 1

    def part(origin, ch):
        return all_grad.at[origin, pl.ds(ch * chunk, chunk)]

    n1_ref, h1_ref, n2_ref, h2_ref, p1_ref, p2_ref, r1_ref, r2_ref = kept

    def heads(ch):
        r = slice(ch * chunk, (ch + 1) * chunk)

        def forward(state, w_up, w_down, n_ref, h_ref):
            scaling = lax.rsqrt(jnp.mean(state * state, axis=-1, keepdims=True) + eps)
            normed = (state * scaling).astype(BF)
            n_ref[r] = normed
            preact = jnp.dot(normed, w_up[...], preferred_element_type=F32)
            value, slope = gelu_parts(preact)
            hidden = value.astype(BF)
            h_ref[r] = hidden
            return state + jnp.dot(hidden, w_down[...], preferred_element_type=F32), scaling, slope

        def backward(g, state, scaling, slope, w_up, w_down, p_ref, r_ref):
            rounded = g.astype(BF)
            r_ref[r] = rounded
            grad_pre = (against_rows(rounded, w_down[...]) * slope).astype(BF)
            p_ref[r] = grad_pre
            grad_normed = against_rows(grad_pre, w_up[...])
            unit = state * scaling
            return g + scaling * (grad_normed - unit * jnp.mean(grad_normed * unit, axis=-1, keepdims=True))

        s0 = grid[r]
        s1, scale1, slope1 = forward(s0, ru, rd, n1_ref, h1_ref)
        s2, scale2, slope2 = forward(s1, du, dd, n2_ref, h2_ref)
        prediction[r] = s2.astype(BF)
        g1 = backward(pred_grad[r].astype(F32) * scale, s1, scale2, slope2, du, dd, p2_ref, r2_ref)
        g0 = backward(g1, s0, scale1, slope1, ru, rd, p1_ref, r1_ref)
        all_grad[z, r] = g0.astype(BF)

    for ch in range(2):
        heads(ch)
        if ch == 0:
            pl.semaphore_wait(barrier, len(total.peers()))
            send(encoded, other, e_s, e_r, sibling)
        for d in range(2):
            if hops(ch, d) >= 1:
                send(part(z, ch), part(z, ch), z_s.at[ch, d, 0], z_r.at[ch, d, 0], beside[d])
    ins[0][...] = contract_rows(n1_ref[...], p1_ref[...])
    ins[1][...] = contract_rows(h1_ref[...], r1_ref[...])
    ins[2][...] = contract_rows(n2_ref[...], p2_ref[...])
    ins[3][...] = contract_rows(h2_ref[...], r2_ref[...])
    total.start()

    def use(origin, first):
        p = (x * NZ + origin) * NC + c
        here[...] = all_grad[origin].reshape(here.shape)
        for g in range(n_group):
            tile = tiles[g, origin].astype(F32).T
            src = index[g, 0, p]
            alive = index[g, 2, p]
            for k in range(cam):
                weight = jnp.where(src == k, alive, 0).astype(F32)
                left[k * BLK : (k + 1) * BLK, :] = (tile * weight).astype(BF)
            product = jnp.dot(left[...], here[index[g, 1, p]], preferred_element_type=F32)
            if first:
                acc[g] = product
            else:
                acc[g] = acc[g] + product

    load.wait()
    use(z, True)
    total.over_xy()

    @pl.loop(1, half + 1)
    def _(k):
        for d in range(2):
            s = 1 - 2 * d
            origin = zz(-s * k)
            for ch in range(2):
                @pl.when(k <= hops(ch, d))
                def _(ch=ch, d=d):
                    arrived(part(origin, ch), z_r.at[ch, d, k - 1], beside[d])

                @pl.when(k + 1 <= hops(ch, d))
                def _(ch=ch, d=d):
                    send(part(origin, ch), part(origin, ch), z_s.at[ch, d, k], z_r.at[ch, d, k], beside[d])

        @pl.when(k == max(half - 2, 1))
        def _():
            total.over_z()

        @pl.when(k == max(half - 1, 1))
        def _():
            total.back_over_z()

        @pl.when(k == half)
        def _():
            total.back_over_xy()

        use(zz(-k), False)

        @pl.when(k < half)
        def _():
            use(zz(k), False)

    wide = grid.shape[1] // NC
    order = (2, 1, NX - 1, 0)

    def channels_of(core):
        return pl.ds(pl.multiple_of(core * wide, wide), wide)

    for i, o in enumerate(order):
        for h in range(NC):
            core_s[i, h] = acc[xx(o) * NC + h, :, channels_of(1 - c)].astype(BF)
        send(core_s.at[i], core_r.at[i], c_s.at[i], c_r.at[i], sibling)

    def pair_sum(i, h):
        return acc[xx(order[i]) * NC + h, :, channels_of(c)] + core_r[i, h].astype(F32)

    def push(n, value, device):
        x_send[n] = value.astype(BF)
        send(x_send.at[n], x_recv.at[n], x_s.at[n], x_r.at[n], device)

    for i in range(3):
        arrived(core_r.at[i], c_r.at[i], sibling)
        if i == 0:
            push(0, pair_sum(0, 0), east)
            push(1, pair_sum(0, 1), west)
        if i == 1:
            push(2, pair_sum(1, 1), east)
        if i == 2:
            push(3, pair_sum(2, 0), west)
    arrived(x_recv.at[0], x_r.at[0], sibling)
    push(4, pair_sum(1, 0) + x_recv[0].astype(F32), east)
    arrived(x_recv.at[1], x_r.at[1], sibling)
    push(5, pair_sum(2, 1) + x_recv[1].astype(F32), west)
    arrived(core_r.at[3], c_r.at[3], sibling)
    for n in range(2, 6):
        arrived(x_recv.at[n], x_r.at[n], sibling)
    rows_out[0] = (pair_sum(3, 0) + x_recv[4].astype(F32) + x_recv[3].astype(F32)).astype(BF)
    rows_out[1] = (pair_sum(3, 1) + x_recv[2].astype(F32) + x_recv[5].astype(F32)).astype(BF)
    arrived(other, e_r, sibling)
    grad_proj[...] = contract_rows(encoded[...], rows_out[c]) + contract_rows(other[...], rows_out[1 - c])
    last.start()
    total.back_over_core()
    last.over_xy()
    total.finish()
    last.over_z()
    last.back_over_z()
    last.back_over_xy()
    last.back_over_core()
    last.finish()
    sent(encoded, e_s, sibling)
    for i in range(4):
        sent(core_s.at[i], c_s.at[i], sibling)
    for n in range(6):
        sent(x_send.at[n], x_s.at[n], sibling)
    for ch in range(2):
        for d in range(2):
            for k in range(hops(ch, d)):
                sent(part(z, ch), z_s.at[ch, d, k], beside[d])


def split(index_all, grid, pred_grad, tiles_all, encoded, weights, scale):
    cells, channels = grid.shape
    tokens, features = encoded.shape
    hidden = weights[0].shape[1]
    n = NX * NC
    half = NZ // 2
    shapes = [w.shape for w in weights]

    def packed_of(some):
        rows = sum(a * b for a, b in some) // (NX * NY * NC * Total.width)
        return jax.ShapeDtypeStruct((NC, NX * NY, rows, Total.width), BF)

    return pl.pallas_call(
        functools.partial(split_kernel, scale=scale),
        out_shape=(
            jax.ShapeDtypeStruct((cells, channels), BF),
            packed_of([(features, channels)]),
            packed_of(shapes),
        ),
        in_specs=[SM, VM, VM, ANY, VM] + [VM] * N_GRADS,
        out_specs=(VM, VM, VM),
        scratch_shapes=[
            pltpu.VMEM((NZ, cells, channels), BF),
            pltpu.VMEM((cells // BLK, BLK, channels), BF),
            pltpu.VMEM((tokens, BLK), BF),
            pltpu.VMEM((n, tokens, channels), F32),
            pltpu.VMEM((NX, NC, tokens, channels // NC), BF),
            pltpu.VMEM((NX, NC, tokens, channels // NC), BF),
            pltpu.VMEM((6, tokens, channels // NC), BF),
            pltpu.VMEM((6, tokens, channels // NC), BF),
            DMA((2, 2, half)), DMA((2, 2, half)),
            DMA((NX,)), DMA((NX,)),
            DMA((6,)), DMA((6,)),
        ]
        + [pltpu.VMEM((cells, w), BF) for w in (channels, hidden) * 2 + (hidden, hidden, channels, channels)]
        + [pltpu.VMEM(a, F32) for a in shapes]
        + [pltpu.VMEM((NC, tokens, channels // NC), BF), pltpu.VMEM((features, channels // NC), F32)]
        + [pltpu.VMEM((tokens, features), BF), DMA(()), DMA(()), pltpu.VMEM(tiles_all.shape, BF), DMA(())]
        + Total.scratch_for(shapes)
        + Total.scratch_for([(features, channels)], paired=True),
        compiler_params=pltpu.CompilerParams(
            collective_id=2, has_side_effects=True, vmem_limit_bytes=VMEM_LIMIT
        ),
    )(index_all, grid, pred_grad, tiles_all, encoded, *weights)


def on_device(
    cams, vit_up, vit_down, proj, frustum_tiles, src_block, dst_block, live,
    render_up, render_down, decode_up, decode_down, pred_grad,
):
    tile_count = NX * NZ * NC
    cells, channels = pred_grad.shape[1:]
    encoded, x_all, tiles_all, index_all = encode(
        vit_up, vit_down, cams, proj, frustum_tiles[0], src_block, dst_block, live
    )
    bev_grid = join(index_all, x_all, tiles_all, cells)
    scale = 1.0 / math.sqrt(cams.shape[0] * cells * tile_count)
    weights = (render_up, render_down, decode_up, decode_down)
    prediction, first, second = split(index_all, bev_grid, pred_grad[0], tiles_all, encoded, weights, scale)
    prediction, *totals = unpack(first, second, prediction, [proj.shape] + [w.shape for w in weights])
    return (prediction[None], *totals)


def solution(mesh):
    placed = (
        P(None, "tile", None),
        P("section", None, None),
        P("section", None, None),
        P(),
        P("tile", None, None, None),
        P("tile", None),
        P("tile", None),
        P("tile", None),
        P(),
        P(),
        P(),
        P(),
        P("section", "tile", None),
    )
    return jax.shard_map(
        on_device,
        mesh=mesh,
        in_specs=placed,
        out_specs=(P("section", "tile", None), P(), P(), P(), P(), P()),
        check_vma=False,
    )
```
